32 devices in a mesh: dp: 8 (over y, x, core), fsdp: 4 (over z).
Axes of the slice: x: 2, y: 2, z: 4, core: 2. Of those that a mesh axis runs over, the one named last changes fastest.
Arguments:
- latents: bfloat16 [16, 512, 1024], P('dp', 'fsdp'), may hold values from -6 to 6
- pixels: bfloat16 [16384, 261], P('dp'), may hold values from -6 to 6
- lengths: int32 [8, 2], P('dp'), may hold values from 1 to 1280, 1792 in all within a row
- pix_gain: bfloat16 [261], replicated, may hold values from 0.099609375 to 1.8984375
- pix_bias: bfloat16 [261], replicated, may hold values from -1.5 to 1.5
- pix_kv: bfloat16 [2, 261, 1024], P(None, None, ('dp', 'fsdp')), may hold values from -0.375 to 0.375
- enc_query: bfloat16 [1024, 1024], P(('dp', 'fsdp')), may hold values from -0.1875 to 0.1875
- enc_out: bfloat16 [1024, 1024], P(('dp', 'fsdp')), may hold values from -3 to 3
- enc_mlp: bfloat16 [2, 1024, 1024], P(None, ('dp', 'fsdp')), may hold values from -0.1875 to 0.1875
- enc_gains: bfloat16 [2, 1024], P(None, ('dp', 'fsdp')), may hold values from 0.099609375 to 1.8984375
- enc_biases: bfloat16 [4, 1024], P(None, ('dp', 'fsdp')), may hold values from -1.5 to 1.5
- lat_qkv: bfloat16 [3, 1024, 1024], P(None, ('dp', 'fsdp')), may hold values from -0.1875 to 0.1875
- lat_out: bfloat16 [1024, 1024], P(('dp', 'fsdp')), may hold values from -2 to 2
- lat_mlp: bfloat16 [2, 1024, 1024], P(None, ('dp', 'fsdp')), may hold values from -0.1875 to 0.1875
- lat_gains: bfloat16 [2, 1024], P(None, ('dp', 'fsdp')), may hold values from 0.099609375 to 1.8984375
- lat_biases: bfloat16 [4, 1024], P(None, ('dp', 'fsdp')), may hold values from -1.5 to 1.5
- cotangent: bfloat16 [16, 512, 1024], P('dp', 'fsdp'), may hold values from -6 to 6
Outputs:
- result: bfloat16 [16, 512, 1024], P('dp', 'fsdp')
- d_latents: float32 [16, 512, 1024], P('dp', 'fsdp')
- d_pixels: float32 [16384, 261], P(('dp', 'fsdp'))
- d_pix_gain: float32 [261], replicated
- d_pix_bias: float32 [261], replicated
- d_pix_kv: float32 [2, 261, 1024], P(None, None, ('dp', 'fsdp'))
- d_enc_query: float32 [1024, 1024], P(('dp', 'fsdp'))
- d_enc_out: float32 [1024, 1024], P(('dp', 'fsdp'))
- d_enc_mlp: float32 [2, 1024, 1024], P(None, ('dp', 'fsdp'))
- d_enc_gains: float32 [2, 1024], P(None, ('dp', 'fsdp'))
- d_enc_biases: float32 [4, 1024], P(None, ('dp', 'fsdp'))
- d_lat_qkv: float32 [3, 1024, 1024], P(None, ('dp', 'fsdp'))
- d_lat_out: float32 [1024, 1024], P(('dp', 'fsdp'))
- d_lat_mlp: float32 [2, 1024, 1024], P(None, ('dp', 'fsdp'))
- d_lat_gains: float32 [2, 1024], P(None, ('dp', 'fsdp'))
- d_lat_biases: float32 [4, 1024], P(None, ('dp', 'fsdp'))
The draws below stay inside these ranges and needn't reach their ends.
Inputs may be any that keep to these rules, and one draw needn't show every extreme that they name: `lengths`: the pixel counts of one index of dp sum to 1792; on every index of dp each is at most 1280.
All inputs are finite; a program needn't handle non-finite values.
Results may differ from the reference program's by a relative error of at most 0.015.
Values may be sent and summed in bfloat16 or wider, within the bound.
No kernel may reach another device: no remote copies, remote signals or barrier semaphores. Data moves between devices by JAX's collectives and lax.ppermute only.
A program may use at most 192 MiB of HBM per device.

```python
import math
import jax
import jax.numpy as jnp
import numpy as np
from jax import lax

D = 1024
C = 261
LATENTS = 512
HEADS = 8
HEAD = 128
IMG_DEV = 2
MOST = 1280
PIX_DEV = 2048
PIX_USED = 1792
IMAGES = 16
PIXELS = 16384
N_DP = 8


def shard_levels(rng, extent, split, smallest, top_value):
    loudness, own = 1.0, jax.random.fold_in(rng, 6)
    for dim, blocks in split:
        heights = jnp.exp(jax.random.uniform(jax.random.fold_in(own, dim), (blocks,), jnp.float32, smallest / len(split), top_value / len(split)))
        loudness = loudness * jnp.repeat(heights, extent[dim] // blocks).reshape([-1 if axis == dim else 1 for axis in range(len(extent))])
    return loudness


def profile(number_of, total, bound, lean):
    loads = [(1 << 20) // math.isqrt(standing ** lean) + 1 for standing in range(2, number_of + 1)]
    surplus, holding = total - bound - (number_of - 1), [1] * (number_of - 1)
    while surplus > 0:
        movable = [i for i in range(number_of - 1) if holding[i] < bound]
        pool, remaining = sum([loads[i] for i in movable]), surplus
        for i in movable:
            extra = min(bound - holding[i], max(1, remaining * loads[i] // pool), surplus)
            holding[i] = holding[i] + extra
            surplus = surplus - extra
    return np.array([bound] + holding)


def ragged(rng, amount, total, limit, lean):
    if amount == 2:
        one = jax.random.randint(rng, (), max(1, total - limit), min(limit, total - 1) + 1)
        return jnp.stack([one, total - one])
    sizes = jnp.asarray(profile(amount, total, limit, lean), jnp.int32)
    pairs = (amount - 1) // 2
    giver, sink = sizes[1:1 + 2 * pairs:2], sizes[2:2 + 2 * pairs:2]
    slack = jnp.minimum(giver - 1, limit - sink)
    shifted = jax.random.randint(jax.random.fold_in(rng, 1), (pairs,), 0, 1 << 20) % (slack + 1)
    sizes = sizes.at[1:1 + 2 * pairs:2].set(giver - shifted).at[2:2 + 2 * pairs:2].set(sink + shifted)
    return sizes[jax.random.permutation(jax.random.fold_in(rng, 2), amount)]


def noise(own_key, extent, width, most, pieces=(), kind=jnp.bfloat16):
    values = jax.random.normal(own_key, extent, jnp.float32) * width
    if len(pieces) > 0:
        values = shard_levels(own_key, extent, pieces, -0.22, 0.18) * values
    return jnp.clip(values, min=-most, max=most).astype(kind)


def setup_inputs(seed: int = 0) -> dict:
    arg_keys = jax.random.split(jax.random.key(seed), 18)
    return {
        "latents": noise(arg_keys[0], (IMAGES, LATENTS, D), 1.0, 6.0, ((0, 8), (1, 4))),
        "pixels": noise(arg_keys[1], (PIXELS, C), 1.0, 6.0, ((0, 8),)),
        "lengths": jax.vmap(lambda own: ragged(own, IMG_DEV, PIX_USED, MOST, 1))(jax.random.split(arg_keys[2], (IMAGES // IMG_DEV))).reshape((IMAGES // IMG_DEV, IMG_DEV)).astype(jnp.int32),
        "pix_gain": jnp.clip(1.0 + 0.18 * jax.random.normal(arg_keys[3], (C,), jnp.float32), 0.099609375, 1.8984375).astype(jnp.bfloat16),
        "pix_bias": noise(arg_keys[4], (C,), 0.3, 1.5),
        "pix_kv": noise(arg_keys[5], (2, C, D), C ** -0.5, 0.375, ((2, 32),)),
        "enc_query": noise(arg_keys[6], (D, D), D ** -0.5, 0.1875, ((0, 32),)),
        "enc_out": noise(arg_keys[7], (D, D), 4 ** -0.5, 3.0, ((0, 32),)),
        "enc_mlp": noise(arg_keys[8], (2, D, D), D ** -0.5, 0.1875, ((1, 32),)),
        "enc_gains": jnp.clip(1.0 + 0.18 * jax.random.normal(arg_keys[9], (2, D), jnp.float32), 0.099609375, 1.8984375).astype(jnp.bfloat16),
        "enc_biases": noise(arg_keys[10], (4, D), 0.3, 1.5, ((1, 32),)),
        "lat_qkv": noise(arg_keys[11], (3, D, D), D ** -0.5, 0.1875, ((1, 32),)),
        "lat_out": noise(arg_keys[12], (D, D), 8 ** -0.5, 2.0, ((0, 32),)),
        "lat_mlp": noise(arg_keys[13], (2, D, D), D ** -0.5, 0.1875, ((1, 32),)),
        "lat_gains": jnp.clip(1.0 + 0.18 * jax.random.normal(arg_keys[14], (2, D), jnp.float32), 0.099609375, 1.8984375).astype(jnp.bfloat16),
        "lat_biases": noise(arg_keys[15], (4, D), 0.3, 1.5, ((1, 32),)),
        "cotangent": noise(arg_keys[16], (IMAGES, LATENTS, D), 1.0, 6.0, ((0, 8), (1, 4))),
    }


@jax.custom_vjp
def low(v):
    return lax.optimization_barrier(v.astype(jnp.bfloat16)).astype(jnp.float32)

@jax.custom_vjp
def low_back(v):
    return v

def low_keep(v):
    return (low(v), None)

def low_pass(kept, grad):
    return (grad,)

def back_keep(v):
    return (v, None)

def back_low(kept, grad):
    return (low(grad),)
low.defvjp(low_keep, low_pass)
low_back.defvjp(back_keep, back_low)
EPSILON = 1e-05

def layer_norm(values, gains, biases):
    average = lax.optimization_barrier(jnp.mean(values, axis=-1, keepdims=True))
    centered = values - average
    variance = lax.optimization_barrier(jnp.mean(centered * centered, axis=-1, keepdims=True))
    return centered * lax.rsqrt(variance + EPSILON) * gains + biases

def linear(inputs, matrix):
    return low_back(jnp.einsum('...i,ij->...j', low(inputs), matrix, precision=lax.Precision.HIGHEST))

def softmax_rows(scores):
    largest = lax.optimization_barrier(jnp.max(scores, axis=-1, keepdims=True))
    powers = jnp.exp(scores - largest)
    return powers / lax.optimization_barrier(jnp.sum(powers, axis=-1, keepdims=True))

def feed_forward(resid, gains, biases, mlp_w):
    normed = layer_norm(resid, gains[1], biases[1])
    hidden = jax.nn.gelu(linear(normed, mlp_w[0]) + biases[2], approximate=False)
    return resid + linear(hidden, mlp_w[1]) + biases[3]

def encoder(latent, pixel, sizes, params):
    pix_gain, pix_bias, pix_kv, enc_query, enc_out, enc_mlp, enc_gains, enc_biases = params
    pixel_normed = layer_norm(pixel, pix_gain, pix_bias)
    key_rows = low(linear(pixel_normed, pix_kv[0]))
    value_rows = low(linear(pixel_normed, pix_kv[1]))
    filler = jnp.zeros((MOST, D), jnp.float32)
    key_rows = jnp.concatenate([key_rows, filler], axis=0)
    value_rows = jnp.concatenate([value_rows, filler], axis=0)
    starts = (jnp.cumsum(sizes) - sizes).astype(jnp.int32)

    def window(source, first):
        return lax.dynamic_slice_in_dim(source, first.astype(jnp.int32), MOST, 0)
    key_win = jax.vmap(window, (None, 0))(key_rows, starts)
    value_win = jax.vmap(window, (None, 0))(value_rows, starts)
    valid = jnp.arange(MOST, dtype=jnp.int32)[None, :] < sizes[:, None]
    normed = layer_norm(latent, enc_gains[0], enc_biases[0])
    queries = low(linear(normed, enc_query))
    scores = low_back(jnp.einsum('iqd,ikd->iqk', queries, key_win, precision=lax.Precision.HIGHEST)) * D ** (-0.5)
    scores = jnp.where(valid[:, None, :], scores, -1e+30)
    probs = low(softmax_rows(scores))
    mixed = low_back(jnp.einsum('iqk,ikd->iqd', probs, value_win, precision=lax.Precision.HIGHEST))
    resid = latent + linear(mixed, enc_out)
    return feed_forward(resid, enc_gains, enc_biases, enc_mlp)

def self_attention(latent, params):
    lat_qkv, lat_out, lat_mlp, lat_gains, lat_biases = params
    normed = layer_norm(latent, lat_gains[0], lat_biases[0])
    split_shape = (latent.shape[0], LATENTS, HEADS, HEAD)
    queries = low(linear(normed, lat_qkv[0])).reshape(split_shape)
    key_rows = low(linear(normed, lat_qkv[1])).reshape(split_shape)
    value_rows = low(linear(normed, lat_qkv[2])).reshape(split_shape)
    scores = low_back(jnp.einsum('iqhd,ikhd->ihqk', queries, key_rows, precision=lax.Precision.HIGHEST)) * HEAD ** (-0.5)
    probs = low(softmax_rows(scores))
    mixed = low_back(jnp.einsum('ihqk,ikhd->iqhd', probs, value_rows, precision=lax.Precision.HIGHEST))
    resid = latent + linear(mixed.reshape(latent.shape), lat_out)
    return feed_forward(resid, lat_gains, lat_biases, lat_mlp)

def reference(latents, pixels, lengths, pix_gain, pix_bias, pix_kv, enc_query, enc_out, enc_mlp, enc_gains, enc_biases, lat_qkv, lat_out, lat_mlp, lat_gains, lat_biases, cotangent):
    weights = jax.tree.map(lambda array_in: array_in.astype(jnp.float32), (pix_gain, pix_bias, pix_kv, enc_query, enc_out, enc_mlp, enc_gains, enc_biases, lat_qkv, lat_out, lat_mlp, lat_gains, lat_biases))
    groups = N_DP
    latent_groups = latents.astype(jnp.float32).reshape(groups, IMG_DEV, LATENTS, D)
    pixel_groups = pixels.astype(jnp.float32).reshape(groups, PIX_DEV, C)
    cot_groups = cotangent.astype(jnp.float32).reshape(groups, IMG_DEV, LATENTS, D)

    def group_step(totals, inputs):
        latent, pixel, sizes, grad_out = inputs

        def forward(latent_in, pixel_in, params):
            return self_attention(encoder(latent_in, pixel_in, sizes, params[:8]), params[8:])
        output, pullback = jax.vjp(forward, latent, pixel, weights)
        d_latent, d_pixel, d_weights = pullback(grad_out)
        totals = jax.tree.map(jnp.add, totals, d_weights)
        return (totals, (output, d_latent, d_pixel))
    zeros = jax.tree.map(jnp.zeros_like, weights)
    totals, (outputs, d_lat, d_pix) = lax.scan(group_step, zeros, (latent_groups, pixel_groups, lengths, cot_groups))
    return (outputs.reshape(IMAGES, LATENTS, D).astype(jnp.bfloat16), d_lat.reshape(IMAGES, LATENTS, D), d_pix.reshape(PIXELS, C), totals[0], totals[1], totals[2], totals[3], totals[4], totals[5], totals[6], totals[7], totals[8], totals[9], totals[10], totals[11], totals[12])
```

```python
from functools import partial

import jax
import jax.numpy as jnp
from jax import lax
from jax.experimental import pallas as pl
from jax.experimental.pallas import tpu as pltpu
from jax.sharding import PartitionSpec as P

HEADS = 8
HEAD = 128
USED = 1792
EPSILON = 1e-05
MASKED = -1e30
AXES = ("dp", "fsdp")
LANES = 128
BF = jnp.bfloat16
F32 = jnp.float32


def dot(left, right, dims):
    return lax.dot_general(left, right, ((dims[0], dims[1]), ((), ())), preferred_element_type=F32)


def mm(left, right):
    return dot(left, right, ((left.ndim - 1,), (0,)))


def mm_t(left, right):
    return dot(left, right, ((left.ndim - 1,), (1,)))


def tm(left, right):
    return dot(left, right, ((0,), (0,)))


def norm_parts(values):
    average = jnp.mean(values, axis=-1, keepdims=True)
    centered = values - average
    variance = jnp.mean(centered * centered, axis=-1, keepdims=True)
    inverse = lax.rsqrt(variance + EPSILON)
    return centered * inverse, inverse


def norm_back(hat, inverse, gains, grad_out):
    grad_hat = grad_out * gains
    first = jnp.mean(grad_hat, axis=-1, keepdims=True)
    second = jnp.mean(grad_hat * hat, axis=-1, keepdims=True)
    return inverse * (grad_hat - first - hat * second)


def gelu(values):
    return 0.5 * values * (1.0 + lax.erf(values * (0.5**0.5)))


def gelu_slope(values):
    density = jnp.exp(-0.5 * values * values) * ((0.5 / jnp.pi) ** 0.5)
    return 0.5 * (1.0 + lax.erf(values * (0.5**0.5))) + values * density


def xor_permute(values, sizes, step):
    dp_size, fsdp_size = sizes
    total = dp_size * fsdp_size
    return lax.ppermute(values, AXES, [(i, i ^ step) for i in range(total)])


def halve(values, bit, left, me, sizes):
    above = sum(1 for other in left if other > bit)
    below = len(left) - 1 - above
    rows, width = values.shape[-2:]
    view = values.reshape(2**above, 2, 2**below, rows, width)
    mine = (me >> bit) & 1
    send = lax.dynamic_index_in_dim(view, 1 - mine, 1, keepdims=False)
    keep = lax.dynamic_index_in_dim(view, mine, 1, keepdims=False)
    got = xor_permute(send, sizes, 1 << bit)
    summed = keep.astype(F32) + got.astype(F32)
    return summed.reshape(-1, rows, width)


def reduce_scatter(values, sizes, me):
    dp_size, fsdp_size = sizes
    low_bits = fsdp_size.bit_length() - 1
    all_bits = list(range((dp_size * fsdp_size).bit_length() - 1))
    core, far = all_bits[low_bits], all_bits[low_bits + 1 :]
    left = list(all_bits)
    values = halve(values, core, left, me, sizes).astype(BF)
    left.remove(core)
    half = values.shape[1] // 32 * 16 or values.shape[1] // 2
    pieces = []
    for piece, order in ((values[:, :half], far), (values[:, half:], far[::-1])):
        rest = list(left)
        for bit in order:
            piece = halve(piece, bit, rest, me, sizes).astype(BF)
            rest.remove(bit)
        pieces.append(piece)
    values = jnp.concatenate(pieces, axis=1)
    rest = all_bits[:low_bits]
    for bit in rest[::-1]:
        summed = halve(values, bit, list(rest), me, sizes)
        rest = rest[:-1]
        values = summed.astype(BF)
    return summed[0]


def butterfly(values, sizes):
    for bit in range((sizes[0] * sizes[1]).bit_length() - 1):
        values = values + xor_permute(values, sizes, 1 << bit)
    return values


def attend(q, k):
    scores = mm_t(q, k) * (HEAD**-0.5)
    powers = jnp.exp(scores - jnp.max(scores, axis=-1, keepdims=True))
    return powers / jnp.sum(powers, axis=-1, keepdims=True)


def attention_kernel(q_ref, k_ref, v_ref, o_ref):
    keys = k_ref.shape[0] * k_ref.shape[2]
    for head in range(q_ref.shape[2] // HEAD):
        cols = pl.ds(head * HEAD, HEAD)
        probs = attend(q_ref[0, :, cols], k_ref[:, 0, :, cols].reshape(keys, HEAD))
        o_ref[0, :, cols] = mm(probs.astype(BF), v_ref[:, 0, :, cols].reshape(keys, HEAD)).astype(BF)


def attention_back_kernel(q_ref, k_ref, v_ref, g_ref, dq_ref, dk_ref, dv_ref):
    shards, _, rows, _ = k_ref.shape
    keys = shards * rows
    scale = HEAD**-0.5
    for head in range(q_ref.shape[2] // HEAD):
        cols = pl.ds(head * HEAD, HEAD)
        q, grad = q_ref[0, :, cols], g_ref[0, :, cols]
        k = k_ref[:, 0, :, cols].reshape(keys, HEAD)
        v = v_ref[:, 0, :, cols].reshape(keys, HEAD)
        probs = attend(q, k)
        grad_probs = mm_t(grad, v)
        inner = jnp.sum(probs * grad_probs, axis=-1, keepdims=True)
        grad_scores = (probs * (grad_probs - inner) * scale).astype(BF)
        dq_ref[0, :, cols] = mm(grad_scores, k).astype(BF)
        dk_ref[:, 0, :, cols] = tm(grad_scores, q).astype(BF).reshape(shards, rows, HEAD)
        dv_ref[:, 0, :, cols] = tm(probs.astype(BF), grad).astype(BF).reshape(shards, rows, HEAD)


def attention_specs(images, rows, width, shards, group):
    own = pl.BlockSpec((1, rows, group), lambda i, h: (i, 0, h))
    whole = pl.BlockSpec((shards, 1, rows, group), lambda i, h: (0, i, 0, h))
    return own, whole, (images, width // group)


def attention(q, k, v):
    images, rows, width = q.shape
    own, whole, grid = attention_specs(images, rows, width, k.shape[0], 4 * HEAD)
    flops = 4 * images * rows * rows * k.shape[0] * width
    return pl.pallas_call(
        attention_kernel,
        grid=grid,
        in_specs=[own, whole, whole],
        out_specs=own,
        out_shape=jax.ShapeDtypeStruct(q.shape, BF),
        cost_estimate=pl.CostEstimate(flops=flops, bytes_accessed=5 * 2**20, transcendentals=2**20),
        name="attention",
    )(q, k, v)


def attention_back(q, k, v, grad):
    images, rows, width = q.shape
    own, whole, grid = attention_specs(images, rows, width, k.shape[0], 4 * HEAD)
    flops = 10 * images * rows * rows * k.shape[0] * width
    return pl.pallas_call(
        attention_back_kernel,
        grid=grid,
        in_specs=[own, whole, whole, own],
        out_specs=[own, whole, whole],
        out_shape=[jax.ShapeDtypeStruct(a.shape, BF) for a in (q, k, v)],
        cost_estimate=pl.CostEstimate(flops=flops, bytes_accessed=10 * 2**20, transcendentals=2**20),
        name="attention_back",
    )(q, k, v, grad)


def feed_forward(resid, gain, shift, bias_one, bias_two, first, second):
    hat, inverse = norm_parts(resid)
    normed = (hat * gain + shift).astype(BF)
    pre = mm(normed, first) + bias_one
    act = gelu(pre).astype(BF)
    return resid + mm(act, second) + bias_two, (hat, inverse, normed, pre, act)


def feed_back(kept, gain, first, second, grad_out):
    hat, inverse, normed, pre, act = kept
    grad_low = grad_out.astype(BF)
    d_second = tm(act, grad_low).astype(BF)
    d_pre = mm_t(grad_low, second) * gelu_slope(pre)
    d_pre_low = d_pre.astype(BF)
    d_first = tm(normed, d_pre_low).astype(BF)
    d_normed = mm_t(d_pre_low, first)
    d_resid = norm_back(hat, inverse, gain, d_normed)
    sums = (
        jnp.sum(d_normed * hat, axis=0),
        jnp.sum(d_normed, axis=0),
        jnp.sum(d_pre, axis=0),
        jnp.sum(grad_out, axis=0),
    )
    return grad_out + d_resid, d_first, d_second, sums


def pad_lanes(values, width):
    return jnp.pad(values, [(0, 0)] * (values.ndim - 1) + [(0, width - values.shape[-1])])


def body(
    sizes,
    latents,
    pixels,
    lengths,
    pix_gain,
    pix_bias,
    pix_kv,
    enc_query,
    enc_out,
    enc_mlp,
    enc_gains,
    enc_biases,
    lat_qkv,
    lat_out,
    lat_mlp,
    lat_gains,
    lat_biases,
    cotangent,
):
    dp_size, fsdp_size = sizes
    devices = dp_size * fsdp_size
    my_fsdp = lax.axis_index("fsdp")
    me = lax.axis_index("dp") * fsdp_size + my_fsdp
    images, lat_rows, width = latents.shape
    rows = images * lat_rows
    pix_rows, features = pixels.shape
    padded = -(-features // LANES) * LANES
    own = width // devices

    kv_t = pad_lanes(jnp.transpose(pix_kv, (2, 0, 1)), width // 2)
    small = jnp.concatenate([enc_gains, enc_biases, lat_gains, lat_biases], axis=0)
    kv_t = kv_t.at[:, 0, padded : padded + small.shape[0]].set(small.T)
    enc_pack = jnp.concatenate([kv_t.reshape(own, width), enc_query, enc_out, enc_mlp[0], enc_mlp[1]], axis=0)
    lat_pack = jnp.concatenate([lat_qkv[0], lat_qkv[1], lat_qkv[2], lat_out, lat_mlp[0], lat_mlp[1]], axis=0)
    enc_all = lax.all_gather(enc_pack, AXES, axis=0, tiled=False)
    lat_all = lax.all_gather(lat_pack, AXES, axis=0, tiled=False)

    def part(whole, index):
        return whole[:, index * own : (index + 1) * own].reshape(width, width)

    kv_full, w_query, w_out, w_first, w_second = [part(enc_all, i) for i in range(5)]
    l_query, l_key, l_value, l_out, l_first, l_second = [part(lat_all, i) for i in range(6)]
    key_t = kv_full[:, :padded]
    value_t = kv_full[:, width // 2 : width // 2 + padded]
    small_all = kv_full[:, padded : padded + small.shape[0]].T.astype(F32)
    n_gain, n_bias = enc_gains.shape[0], enc_biases.shape[0]
    gains_enc, biases_enc = small_all[:n_gain], small_all[n_gain : n_gain + n_bias]
    gains_lat, biases_lat = small_all[n_gain + n_bias : 2 * n_gain + n_bias], small_all[2 * n_gain + n_bias :]

    gain_f = pix_gain.astype(F32)
    pix_hat, pix_inverse = norm_parts(pixels.astype(F32))
    pix_low = pad_lanes((pix_hat * gain_f + pix_bias.astype(F32)).astype(BF), padded)[:USED]

    latent_in = latents.astype(F32).reshape(rows, width)
    in_hat, in_inverse = norm_parts(latent_in)
    in_low = (in_hat * gains_enc[0] + biases_enc[0]).astype(BF)
    enc_q = mm(in_low, w_query).astype(BF)
    query_pix = mm(enc_q, key_t).astype(BF)
    counts = lengths[0]
    ends = jnp.cumsum(counts)
    firsts = ends - counts
    column = lax.broadcasted_iota(jnp.int32, (images, lat_rows, USED), 2)
    valid = ((column >= firsts[:, None, None]) & (column < ends[:, None, None])).reshape(rows, USED)
    enc_scale = width**-0.5
    scores = jnp.where(valid, mm_t(query_pix, pix_low) * enc_scale, MASKED)
    powers = jnp.exp(scores - jnp.max(scores, axis=-1, keepdims=True))
    probs = powers / jnp.sum(powers, axis=-1, keepdims=True)
    probs_low = probs.astype(BF)
    mixed_pix = mm(probs_low, pix_low).astype(BF)
    enc_mixed = mm_t(mixed_pix, value_t).astype(BF)
    enc_resid = latent_in + mm(enc_mixed, w_out)
    first_out, enc_kept = feed_forward(
        enc_resid, gains_enc[1], biases_enc[1], biases_enc[2], biases_enc[3], w_first, w_second
    )

    lat_hat, lat_inverse = norm_parts(first_out)
    lat_low = (lat_hat * gains_lat[0] + biases_lat[0]).astype(BF)
    shards = [lat_low] + [xor_permute(lat_low, sizes, k) for k in range(1, fsdp_size)]
    lat_every = jnp.concatenate(shards, axis=0)
    shape = (images, lat_rows, width)
    lat_q = mm(lat_low, l_query).astype(BF).reshape(shape)
    lat_k = mm(lat_every, l_key).astype(BF).reshape((fsdp_size,) + shape)
    lat_v = mm(lat_every, l_value).astype(BF).reshape((fsdp_size,) + shape)
    lat_mixed = attention(lat_q, lat_k, lat_v).reshape(rows, width)
    lat_resid = first_out + mm(lat_mixed, l_out)
    second_out, lat_kept = feed_forward(
        lat_resid, gains_lat[1], biases_lat[1], biases_lat[2], biases_lat[3], l_first, l_second
    )
    result = second_out.astype(BF).reshape(shape)

    grad_out = cotangent.astype(F32).reshape(rows, width)
    grad_mid, d_l_first, d_l_second, lat_sums = feed_back(lat_kept, gains_lat[1], l_first, l_second, grad_out)
    grad_mid_low = grad_mid.astype(BF)
    d_l_out = tm(lat_mixed, grad_mid_low).astype(BF)
    d_mixed = mm_t(grad_mid_low, l_out).astype(BF).reshape(shape)
    d_q, d_k, d_v = attention_back(lat_q, lat_k, lat_v, d_mixed)
    d_q, d_k, d_v = d_q.reshape(rows, width), d_k.reshape(-1, width), d_v.reshape(-1, width)
    d_l_query = tm(lat_low, d_q).astype(BF)
    d_l_key = tm(lat_every, d_k).astype(BF)
    d_l_value = tm(lat_every, d_v).astype(BF)
    d_every = mm_t(d_k, l_key) + mm_t(d_v, l_value)
    d_lat_normed = mm_t(d_q, l_query) + d_every[:rows]
    for k in range(1, fsdp_size):
        piece = d_every[k * rows : (k + 1) * rows].astype(BF)
        d_lat_normed = d_lat_normed + xor_permute(piece, sizes, k).astype(F32)
    d_first_out = grad_mid + norm_back(lat_hat, lat_inverse, gains_lat[0], d_lat_normed)
    lat_front = (jnp.sum(d_lat_normed * lat_hat, axis=0), jnp.sum(d_lat_normed, axis=0))

    def stack(pieces):
        return jnp.concatenate([p.reshape(devices, own, width) for p in pieces], axis=1)

    lat_grads = reduce_scatter(
        stack([d_l_query, d_l_key, d_l_value, d_l_out, d_l_first, d_l_second]), sizes, me
    )

    grad_enc, d_first, d_second, enc_sums = feed_back(enc_kept, gains_enc[1], w_first, w_second, d_first_out)
    grad_enc_low = grad_enc.astype(BF)
    d_w_out = tm(enc_mixed, grad_enc_low).astype(BF)
    d_enc_mixed = mm_t(grad_enc_low, w_out).astype(BF)
    d_value_t = tm(d_enc_mixed, mixed_pix)
    mixed_back = mm(d_enc_mixed, value_t).astype(BF)
    d_probs = mm_t(mixed_back, pix_low)
    inner = jnp.sum(probs * d_probs, axis=-1, keepdims=True)
    d_scores = (probs * (d_probs - inner) * enc_scale).astype(BF)
    d_query_pix = mm(d_scores, pix_low).astype(BF)
    d_enc_q = mm_t(d_query_pix, key_t).astype(BF)
    d_key_t = tm(enc_q, d_query_pix)
    d_pix_low = tm(d_scores, query_pix) + tm(probs_low, mixed_back)
    d_w_query = tm(in_low, d_enc_q).astype(BF)
    d_in_normed = mm_t(d_enc_q, w_query)
    d_latents = grad_enc + norm_back(in_hat, in_inverse, gains_enc[0], d_in_normed)
    enc_front = (jnp.sum(d_in_normed * in_hat, axis=0), jnp.sum(d_in_normed, axis=0))

    d_pix_all = d_pix_low[:, :features]
    d_pix_sums = jnp.stack([jnp.sum(d_pix_all * pix_hat[:USED], axis=0), jnp.sum(d_pix_all, axis=0)])
    d_pix_sums = butterfly(pad_lanes(d_pix_sums, padded), sizes)[:, :features]
    share = pix_rows // fsdp_size
    d_pix_pad = jnp.pad(d_pix_low, ((0, pix_rows - USED), (0, 0)))
    d_pix_own = lax.dynamic_slice_in_dim(d_pix_pad, my_fsdp * share, share, 0)
    for k in range(1, fsdp_size):
        piece = lax.dynamic_slice_in_dim(d_pix_pad, (my_fsdp ^ k) * share, share, 0).astype(BF)
        d_pix_own = d_pix_own + xor_permute(piece, sizes, k).astype(F32)
    hat_own = lax.dynamic_slice_in_dim(pix_hat, my_fsdp * share, share, 0)
    inverse_own = lax.dynamic_slice_in_dim(pix_inverse, my_fsdp * share, share, 0)
    d_pixels = norm_back(hat_own, inverse_own, gain_f, d_pix_own[:, :features])

    small_grads = jnp.stack(
        [enc_front[0], enc_sums[0], enc_front[1], enc_sums[1], enc_sums[2], enc_sums[3]]
        + [lat_front[0], lat_sums[0], lat_front[1], lat_sums[1], lat_sums[2], lat_sums[3]]
    )
    high = small_grads.astype(BF)
    low = (small_grads - high.astype(F32)).astype(BF)
    n_small = small_grads.shape[0]
    half_pad = width // 2 - padded
    kv_grads = jnp.concatenate(
        [
            d_key_t.astype(BF),
            pad_lanes(high.T, half_pad),
            d_value_t.astype(BF),
            pad_lanes(low.T, half_pad),
        ],
        axis=1,
    )
    enc_grads = reduce_scatter(stack([kv_grads, d_w_query, d_w_out, d_first, d_second]), sizes, me)

    def mine(whole, index):
        return whole[index * own : (index + 1) * own]

    kv_own = mine(enc_grads, 0)
    d_pix_kv = jnp.stack([kv_own[:, :features].T, kv_own[:, width // 2 : width // 2 + features].T])
    start = width // 2 + padded
    small_own = (kv_own[:, padded : padded + n_small] + kv_own[:, start : start + n_small]).T
    return (
        result,
        d_latents.reshape(shape),
        d_pixels,
        d_pix_sums[0],
        d_pix_sums[1],
        d_pix_kv,
        mine(enc_grads, 1),
        mine(enc_grads, 2),
        jnp.stack([mine(enc_grads, 3), mine(enc_grads, 4)]),
        small_own[:n_gain],
        small_own[n_gain : n_gain + n_bias],
        jnp.stack([mine(lat_grads, 0), mine(lat_grads, 1), mine(lat_grads, 2)]),
        mine(lat_grads, 3),
        jnp.stack([mine(lat_grads, 4), mine(lat_grads, 5)]),
        small_own[n_gain + n_bias : 2 * n_gain + n_bias],
        small_own[2 * n_gain + n_bias :],
    )


def solution(mesh):
    split, rows, columns = P("dp", "fsdp", None), P(AXES, None), P(None, AXES)
    middle = P(None, AXES, None)
    weights = (P(None, None, AXES), rows, rows, middle, columns, columns, middle, rows, middle, columns, columns)
    return jax.shard_map(
        partial(body, (mesh.shape["dp"], mesh.shape["fsdp"])),
        mesh=mesh,
        in_specs=(split, P("dp", None), P("dp", None), P(), P()) + weights + (split,),
        out_specs=(split, split, rows, P(), P()) + weights,
        check_vma=False,
    )
```

```python
from functools import partial

import jax
import jax.numpy as jnp
from jax import lax
from jax.experimental.layout import Layout, with_layout_constraint
from jax.experimental import pallas as pl
from jax.experimental.pallas import tpu as pltpu
from jax.sharding import PartitionSpec as P

HEADS = 8
HEAD = 128
USED = 1792
EPSILON = 1e-05
MASKED = -1e30
AXES = ("dp", "fsdp")
LANES = 128
BF = jnp.bfloat16
F32 = jnp.float32


def dot(left, right, dims):
    return lax.dot_general(left, right, ((dims[0], dims[1]), ((), ())), preferred_element_type=F32)


def mm(left, right):
    return dot(left, right, ((left.ndim - 1,), (0,)))


def mm_t(left, right):
    return dot(left, right, ((left.ndim - 1,), (1,)))


def tm(left, right):
    return dot(left, right, ((0,), (0,)))


def norm_parts(values):
    average = jnp.mean(values, axis=-1, keepdims=True)
    centered = values - average
    variance = jnp.mean(centered * centered, axis=-1, keepdims=True)
    inverse = lax.rsqrt(variance + EPSILON)
    return centered * inverse, inverse


def norm_back(hat, inverse, gains, grad_out):
    grad_hat = grad_out * gains
    first = jnp.mean(grad_hat, axis=-1, keepdims=True)
    second = jnp.mean(grad_hat * hat, axis=-1, keepdims=True)
    return inverse * (grad_hat - first - hat * second)


def gelu(values):
    return 0.5 * values * (1.0 + lax.erf(values * (0.5**0.5)))


def gelu_slope(values):
    density = jnp.exp(-0.5 * values * values) * ((0.5 / jnp.pi) ** 0.5)
    return 0.5 * (1.0 + lax.erf(values * (0.5**0.5))) + values * density


def xor_permute(values, sizes, step):
    dp_size, fsdp_size = sizes
    total = dp_size * fsdp_size
    return lax.ppermute(values, AXES, [(i, i ^ step) for i in range(total)])


def tie(*values):
    return lax.optimization_barrier(values)


def bits_of(sizes):
    low = sizes[1].bit_length() - 1
    every = list(range((sizes[0] * sizes[1]).bit_length() - 1))
    return every[:low], every[low], every[low + 1 :]


def gather_fsdp(values, sizes):
    return [values] + [xor_permute(values, sizes, k) for k in range(1, sizes[1])]


def order_fsdp(parts, sizes, me):
    low, _, _ = bits_of(sizes)
    for bit in low:
        mine = ((me >> bit) & 1) == 1
        parts = [jnp.where(mine, parts[k ^ (1 << bit)], parts[k]) for k in range(len(parts))]
    return jnp.stack(parts)


def merge(own, got, bit, above, me):
    mine = ((me >> bit) & 1) == 1
    view = (2**above, -1) + own.shape[1:]
    own, got = own.reshape(view), got.reshape(view)
    both = jnp.stack([jnp.where(mine, got, own), jnp.where(mine, own, got)], axis=1)
    return both.reshape((-1,) + own.shape[2:])


def far_step(groups, place, sizes, me):
    _, _, far = bits_of(sizes)
    result = []
    for values, order in zip(groups, (far, far[::-1])):
        bit, held = order[place], order[:place]
        got = xor_permute(values, sizes, 1 << bit)
        result.append(merge(values, got, bit, sum(1 for other in held if other > bit), me))
    return result


def merge_kernel(plan, *refs):
    (own_a, got_a, own_b, got_b), outs = refs[:4], refs[4:]
    fsdp_size, core = own_a.shape[1], lax.axis_index("dp") & 1
    for flip in (0, 1):

        @pl.when(core == flip)
        def _(flip=flip):
            sources = ((own_a, own_b), (got_a, got_b))
            for out, (start, own, segments) in zip(outs, plan):
                for side in (0, 1):
                    for shard in range(fsdp_size):
                        row, column = (side * fsdp_size + shard) * own, 0
                        for group, first, count in segments:
                            source = sources[side ^ flip][group]
                            out[row : row + own, column : column + count] = source[
                                0, shard, start : start + own, first : first + count
                            ]
                            column += count


def core_merge(groups, plan, sizes, me):
    _, core, _ = bits_of(sizes)
    got = [xor_permute(values, sizes, 1 << core) for values in groups]
    far_size, fsdp_size, _, columns = groups[0].shape
    if plan[0][1] % 16:
        mine = ((me >> core) & 1) == 1
        both = [
            jnp.stack([jnp.where(mine, g, v), jnp.where(mine, v, g)], axis=1) for v, g in zip(groups, got)
        ]
        wholes = []
        for start, own, segments in plan:
            parts = [both[p][:, :, :, start : start + own, a : a + n] for p, a, n in segments]
            whole = jnp.concatenate(parts, axis=-1)
            wholes.append(whole.reshape(-1, whole.shape[-1]))
        return wholes
    spec = pl.BlockSpec((1,) + groups[0].shape[1:], lambda i: (i, 0, 0, 0))
    shapes = [(2 * fsdp_size * own, sum(n for _, _, n in segments)) for _, own, segments in plan]
    return pl.pallas_call(
        partial(merge_kernel, plan),
        grid=(far_size,),
        in_specs=[spec] * 4,
        out_specs=[pl.BlockSpec(shape, lambda i: (i, 0)) for shape in shapes],
        out_shape=[jax.ShapeDtypeStruct((far_size * r, w), BF) for r, w in shapes],
        cost_estimate=pl.CostEstimate(flops=0, bytes_accessed=24 * 2**20, transcendentals=0),
        name="merge",
    )(groups[0], got[0], groups[1], got[1])


def halves_of(values):
    half = values.shape[-1] // 2
    return [values[..., :half], values[..., half:]]


def core_sum(grads, sizes, me):
    _, core, _ = bits_of(sizes)
    mine = (me >> core) & 1
    sends, keeps = [], []
    for grad in grads:
        view = grad.reshape(sizes[0] // 2, 2, -1, grad.shape[-1])
        sends.append(lax.dynamic_index_in_dim(view, 1 - mine, 1, keepdims=False))
        keeps.append(lax.dynamic_index_in_dim(view, mine, 1, keepdims=False))
    got = xor_permute(jnp.stack(sends), sizes, 1 << core)
    sums = [(keep.astype(F32) + got[i].astype(F32)).astype(BF) for i, keep in enumerate(keeps)]
    return jnp.stack(sums, axis=1)


def far_sum(values, bit, held, sizes, me):
    above = sum(1 for other in held if other > bit)
    view = values.reshape((2**above, 2, -1) + values.shape[1:])
    mine = (me >> bit) & 1
    send = lax.dynamic_index_in_dim(view, 1 - mine, 1, keepdims=False)
    keep = lax.dynamic_index_in_dim(view, mine, 1, keepdims=False)
    got = xor_permute(send, sizes, 1 << bit)
    summed = (keep.astype(F32) + got.astype(F32)).astype(BF)
    return summed.reshape((-1,) + values.shape[1:])


def fsdp_sum(values, sizes, my_fsdp):
    view = values.reshape(values.shape[0], sizes[1], -1, values.shape[-1])
    total = lax.dynamic_index_in_dim(view, my_fsdp, 1, keepdims=False).astype(F32)
    for k in range(1, sizes[1]):
        send = lax.dynamic_index_in_dim(view, my_fsdp ^ k, 1, keepdims=False)
        total = total + xor_permute(send, sizes, k).astype(F32)
    return total


def far_pair(groups, place, sizes, me):
    _, _, far = bits_of(sizes)
    result = []
    for group, order in zip(groups, (far, far[::-1])):
        held = [bit for bit in far if bit not in order[:place]]
        result.append(far_sum(group, order[place], held, sizes, me))
    return result


def finish_sum(groups, sizes, my_fsdp):
    return fsdp_sum(jnp.concatenate([group[0] for group in groups], axis=-1), sizes, my_fsdp)


def butterfly(values, sizes):
    for bit in range((sizes[0] * sizes[1]).bit_length() - 1):
        values = values + xor_permute(values, sizes, 1 << bit)
    return values


def attend(q, k):
    scores = mm_t(q, k) * (HEAD**-0.5)
    powers = jnp.exp(scores - jnp.max(scores, axis=-1, keepdims=True))
    return powers / jnp.sum(powers, axis=-1, keepdims=True)


def attention_kernel(q_ref, k_ref, v_ref, o_ref):
    keys = k_ref.shape[0] * k_ref.shape[2]
    for head in range(q_ref.shape[2] // HEAD):
        cols = pl.ds(head * HEAD, HEAD)
        probs = attend(q_ref[0, :, cols], k_ref[:, 0, :, cols].reshape(keys, HEAD))
        o_ref[0, :, cols] = mm(probs.astype(BF), v_ref[:, 0, :, cols].reshape(keys, HEAD)).astype(BF)


def attention_back_kernel(q_ref, k_ref, v_ref, g_ref, dq_ref, dk_ref, dv_ref):
    shards, _, rows, _ = k_ref.shape
    keys = shards * rows
    scale = HEAD**-0.5
    for head in range(q_ref.shape[2] // HEAD):
        cols = pl.ds(head * HEAD, HEAD)
        q, grad = q_ref[0, :, cols], g_ref[0, :, cols]
        k = k_ref[:, 0, :, cols].reshape(keys, HEAD)
        v = v_ref[:, 0, :, cols].reshape(keys, HEAD)
        probs = attend(q, k)
        grad_probs = mm_t(grad, v)
        inner = jnp.sum(probs * grad_probs, axis=-1, keepdims=True)
        grad_scores = (probs * (grad_probs - inner) * scale).astype(BF)
        dq_ref[0, :, cols] = mm(grad_scores, k).astype(BF)
        dk_ref[:, 0, :, cols] = tm(grad_scores, q).astype(BF).reshape(shards, rows, HEAD)
        dv_ref[:, 0, :, cols] = tm(probs.astype(BF), grad).astype(BF).reshape(shards, rows, HEAD)


def attention_specs(images, rows, width, shards, group):
    own = pl.BlockSpec((1, rows, group), lambda i, h: (i, 0, h))
    whole = pl.BlockSpec((shards, 1, rows, group), lambda i, h: (0, i, 0, h))
    return own, whole, (images, width // group)


def attention(q, k, v):
    images, rows, width = q.shape
    own, whole, grid = attention_specs(images, rows, width, k.shape[0], 4 * HEAD)
    flops = 4 * images * rows * rows * k.shape[0] * width
    return pl.pallas_call(
        attention_kernel,
        grid=grid,
        in_specs=[own, whole, whole],
        out_specs=own,
        out_shape=jax.ShapeDtypeStruct(q.shape, BF),
        cost_estimate=pl.CostEstimate(flops=flops, bytes_accessed=5 * 2**20, transcendentals=2**20),
        name="attention",
    )(q, k, v)


def attention_back(q, k, v, grad):
    images, rows, width = q.shape
    own, whole, grid = attention_specs(images, rows, width, k.shape[0], 4 * HEAD)
    flops = 10 * images * rows * rows * k.shape[0] * width
    return pl.pallas_call(
        attention_back_kernel,
        grid=grid,
        in_specs=[own, whole, whole, own],
        out_specs=[own, whole, whole],
        out_shape=[jax.ShapeDtypeStruct(a.shape, BF) for a in (q, k, v)],
        cost_estimate=pl.CostEstimate(flops=flops, bytes_accessed=10 * 2**20, transcendentals=2**20),
        name="attention_back",
    )(q, k, v, grad)


def feed_forward(resid, gain, shift, bias_one, bias_two, first, second):
    hat, inverse = norm_parts(resid)
    normed = (hat * gain + shift).astype(BF)
    pre = mm(normed, first) + bias_one
    act = gelu(pre).astype(BF)
    return resid + mm(act, second) + bias_two, (hat, inverse, normed, pre, act)


def feed_back(kept, gain, first, second, grad_out):
    hat, inverse, normed, pre, act = kept
    grad_low = grad_out.astype(BF)
    d_second = tm(act, grad_low).astype(BF)
    d_pre = mm_t(grad_low, second) * gelu_slope(pre)
    d_pre_low = d_pre.astype(BF)
    d_first = tm(normed, d_pre_low).astype(BF)
    d_normed = mm_t(d_pre_low, first)
    d_resid = norm_back(hat, inverse, gain, d_normed)
    sums = (
        jnp.sum(d_normed * hat, axis=0),
        jnp.sum(d_normed, axis=0),
        jnp.sum(d_pre, axis=0),
        jnp.sum(grad_out, axis=0),
    )
    return grad_out + d_resid, d_first, d_second, sums


def pad_lanes(values, width):
    return jnp.pad(values, [(0, 0)] * (values.ndim - 1) + [(0, width - values.shape[-1])])


def body(
    sizes,
    latents,
    pixels,
    lengths,
    pix_gain,
    pix_bias,
    pix_kv,
    enc_query,
    enc_out,
    enc_mlp,
    enc_gains,
    enc_biases,
    lat_qkv,
    lat_out,
    lat_mlp,
    lat_gains,
    lat_biases,
    cotangent,
):
    dp_size, fsdp_size = sizes
    devices = dp_size * fsdp_size
    my_fsdp = lax.axis_index("fsdp")
    me = lax.axis_index("dp") * fsdp_size + my_fsdp
    images, lat_rows, width = latents.shape
    rows = images * lat_rows
    pix_rows, features = pixels.shape
    padded = -(-features // LANES) * LANES
    own = width // devices

    _, _, far = bits_of(sizes)
    half = width // 2
    whole_plan = [(0, 0, half), (1, 0, half)]
    enc_parts = gather_fsdp(jnp.concatenate([enc_mlp[0], enc_mlp[1], enc_query, enc_out], axis=0), sizes)
    kv_t = pad_lanes(jnp.transpose(pix_kv, (2, 0, 1)), half)
    small = jnp.concatenate([enc_gains, enc_biases, lat_gains, lat_biases], axis=0)
    n_small = small.shape[0]
    kv_t = jnp.concatenate([kv_t[:, 0, :padded], pad_lanes(small.T, half - padded), kv_t[:, 1]], axis=1)
    kv_parts = gather_fsdp(kv_t, sizes)
    parts = tie(*enc_parts, *kv_parts)
    parts = [jnp.concatenate([e, k], axis=0) for e, k in zip(parts[:fsdp_size], parts[fsdp_size:])]
    enc_groups = [v[None] for v in halves_of(order_fsdp(parts, sizes, me))]
    other_parts = gather_fsdp(jnp.concatenate([lat_out, lat_mlp[0], lat_mlp[1]], axis=0), sizes)
    for place in range(len(far)):
        enc_groups = far_step(enc_groups, place, sizes, me)
        if place == 0:
            qkv, *enc_groups = tie(lat_qkv, *enc_groups)
            qkv_parts = gather_fsdp(qkv.reshape(3 * own, width), sizes)
    groups = tie(*enc_groups, *qkv_parts)
    enc_groups, qkv_parts = groups[:2], list(groups[2:])
    qkv_groups = [v[None] for v in halves_of(order_fsdp(qkv_parts, sizes, me))]
    plan = [(i * own, own, whole_plan) for i in range(4)]
    plan += [(4 * own, own, [(0, 0, padded)]), (4 * own, own, [(1, 0, padded)]), (4 * own, own, [(0, padded, half - padded)])]
    w_first, w_second, w_query, w_out, key_t, value_t, small_t = core_merge(enc_groups, plan, sizes, me)
    qkv_groups = far_step(qkv_groups, 0, sizes, me)
    small_all = mm_t(jnp.eye(n_small, half - padded, dtype=BF), small_t)
    n_gain, n_bias = enc_gains.shape[0], enc_biases.shape[0]
    gains_enc, biases_enc = small_all[:n_gain], small_all[n_gain : n_gain + n_bias]
    gains_lat, biases_lat = small_all[n_gain + n_bias : 2 * n_gain + n_bias], small_all[2 * n_gain + n_bias :]

    gain_f = pix_gain.astype(F32)
    pix_hat, pix_inverse = norm_parts(pixels.astype(F32))
    pix_low = pad_lanes((pix_hat * gain_f + pix_bias.astype(F32)).astype(BF), padded)[:USED]

    latent_in = latents.astype(F32).reshape(rows, width)
    in_hat, in_inverse = norm_parts(latent_in)
    in_low = (in_hat * gains_enc[0] + biases_enc[0]).astype(BF)
    enc_q = mm(in_low, w_query).astype(BF)
    enc_q, *qkv_groups = tie(enc_q, *qkv_groups)
    for place in range(1, len(far)):
        qkv_groups = far_step(qkv_groups, place, sizes, me)
    query_pix = mm(enc_q, key_t).astype(BF)
    counts = lengths[0]
    ends = jnp.cumsum(counts)
    firsts = ends - counts
    column = lax.broadcasted_iota(jnp.int32, (images, lat_rows, USED), 2)
    valid = ((column >= firsts[:, None, None]) & (column < ends[:, None, None])).reshape(rows, USED)
    enc_scale = width**-0.5
    scores = jnp.where(valid, mm_t(query_pix, pix_low) * enc_scale, MASKED)
    powers = jnp.exp(scores - jnp.max(scores, axis=-1, keepdims=True))
    probs = powers / jnp.sum(powers, axis=-1, keepdims=True)
    probs_low = probs.astype(BF)
    mixed_pix = mm(probs_low, pix_low).astype(BF)
    enc_mixed = mm_t(mixed_pix, value_t).astype(BF)
    enc_resid = latent_in + mm(enc_mixed, w_out)
    first_out, enc_kept = feed_forward(
        enc_resid, gains_enc[1], biases_enc[1], biases_enc[2], biases_enc[3], w_first, w_second
    )

    lat_hat, lat_inverse = norm_parts(first_out)
    lat_low = (lat_hat * gains_lat[0] + biases_lat[0]).astype(BF)
    lat_low, *groups = tie(lat_low, *qkv_groups, *other_parts)
    shards = gather_fsdp(lat_low, sizes)
    plan = [(i * own, own, whole_plan) for i in range(3)]
    l_query, l_key, l_value = core_merge(groups[:2], plan, sizes, me)
    other_groups = [v[None] for v in halves_of(order_fsdp(list(groups[2:]), sizes, me))]
    for place in range(len(far)):
        other_groups = far_step(other_groups, place, sizes, me)
    lat_every = jnp.concatenate(shards, axis=0)
    shape = (images, lat_rows, width)
    lat_q = mm(lat_low, l_query).astype(BF).reshape(shape)
    lat_k = mm(lat_every, l_key).astype(BF).reshape((fsdp_size,) + shape)
    lat_v = mm(lat_every, l_value).astype(BF).reshape((fsdp_size,) + shape)
    l_out, l_first, l_second = core_merge(other_groups, plan, sizes, me)
    lat_mixed = attention(lat_q, lat_k, lat_v).reshape(rows, width)
    lat_resid = first_out + mm(lat_mixed, l_out)
    second_out, lat_kept = feed_forward(
        lat_resid, gains_lat[1], biases_lat[1], biases_lat[2], biases_lat[3], l_first, l_second
    )
    result = second_out.astype(BF).reshape(shape)

    grad_out = cotangent.astype(F32).reshape(rows, width)
    grad_mid, d_l_first, d_l_second, lat_sums = feed_back(lat_kept, gains_lat[1], l_first, l_second, grad_out)
    grad_mid_low = grad_mid.astype(BF)
    d_l_out = tm(lat_mixed, grad_mid_low).astype(BF)
    d_mixed = mm_t(grad_mid_low, l_out).astype(BF).reshape(shape)
    after_groups = halves_of(core_sum([d_l_first, d_l_second, d_l_out], sizes, me))
    d_q, d_k, d_v = attention_back(lat_q, lat_k, lat_v, d_mixed)
    d_q, d_k, d_v, *after_groups = tie(d_q, d_k, d_v, *after_groups)
    d_q, d_k, d_v = d_q.reshape(rows, width), d_k.reshape(-1, width), d_v.reshape(-1, width)
    d_every = mm_t(d_k, l_key) + mm_t(d_v, l_value)
    d_lat_normed = mm_t(d_q, l_query) + d_every[:rows]
    for k in range(1, fsdp_size):
        piece = d_every[k * rows : (k + 1) * rows].astype(BF)
        d_lat_normed = d_lat_normed + xor_permute(piece, sizes, k).astype(F32)
    d_l_query = tm(lat_low, d_q).astype(BF)
    d_l_key = tm(lat_every, d_k).astype(BF)
    d_l_value = tm(lat_every, d_v).astype(BF)
    for place in range(len(far)):
        after_groups = far_pair(after_groups, place, sizes, me)
    qkv_groups = halves_of(core_sum([d_l_query, d_l_key, d_l_value], sizes, me))
    qkv_groups = far_pair(qkv_groups, 0, sizes, me)
    d_lat_normed, *groups = tie(d_lat_normed, *after_groups, *qkv_groups)
    after_groups, qkv_groups = groups[:2], groups[2:]
    for place in range(1, len(far)):
        qkv_groups = far_pair(qkv_groups, place, sizes, me)
    after_grads = finish_sum(after_groups, sizes, my_fsdp)
    d_first_out = grad_mid + norm_back(lat_hat, lat_inverse, gains_lat[0], d_lat_normed)
    lat_front = (jnp.sum(d_lat_normed * lat_hat, axis=0), jnp.sum(d_lat_normed, axis=0))

    grad_enc, d_first, d_second, enc_sums = feed_back(enc_kept, gains_enc[1], w_first, w_second, d_first_out)
    grad_enc_low = grad_enc.astype(BF)
    d_w_out = tm(enc_mixed, grad_enc_low).astype(BF)
    d_enc_mixed = mm_t(grad_enc_low, w_out).astype(BF)
    d_value_t = tm(d_enc_mixed, mixed_pix)
    mixed_back = mm(d_enc_mixed, value_t).astype(BF)
    mixed_back, after_grads, *qkv_groups = tie(mixed_back, after_grads, *qkv_groups)
    qkv_grads = finish_sum(qkv_groups, sizes, my_fsdp)
    mlp_groups = halves_of(core_sum([d_first, d_second, d_w_out], sizes, me))
    mlp_groups = far_pair(mlp_groups, 0, sizes, me)
    d_probs = mm_t(mixed_back, pix_low)
    inner = jnp.sum(probs * d_probs, axis=-1, keepdims=True)
    d_scores = (probs * (d_probs - inner) * enc_scale).astype(BF)
    d_query_pix = mm(d_scores, pix_low).astype(BF)
    d_query_pix, qkv_grads, *mlp_groups = tie(d_query_pix, qkv_grads, *mlp_groups)
    for place in range(1, len(far)):
        mlp_groups = far_pair(mlp_groups, place, sizes, me)
    d_enc_q = mm_t(d_query_pix, key_t).astype(BF)
    d_key_t = tm(enc_q, d_query_pix)
    d_pix_t = tm(query_pix, d_scores) + tm(mixed_back, probs_low)
    d_w_query = tm(in_low, d_enc_q).astype(BF)
    d_in_normed = mm_t(d_enc_q, w_query)
    d_latents = grad_enc + norm_back(in_hat, in_inverse, gains_enc[0], d_in_normed)
    enc_front = (jnp.sum(d_in_normed * in_hat, axis=0), jnp.sum(d_in_normed, axis=0))

    d_pix_t = d_pix_t[:features]
    d_pix_sums = jnp.stack([jnp.sum(d_pix_t * pix_hat[:USED].T, axis=1), jnp.sum(d_pix_t, axis=1)])
    d_pix_sums = butterfly(pad_lanes(d_pix_sums, padded), sizes)[:, :features]
    share = pix_rows // fsdp_size
    d_pix_pad = pad_lanes(d_pix_t, pix_rows)
    d_pix_own = lax.dynamic_slice_in_dim(d_pix_pad, my_fsdp * share, share, 1)
    for k in range(1, fsdp_size):
        piece = lax.dynamic_slice_in_dim(d_pix_pad, (my_fsdp ^ k) * share, share, 1).astype(BF)
        d_pix_own = d_pix_own + xor_permute(piece, sizes, k).astype(F32)
    hat_own = lax.dynamic_slice_in_dim(pix_hat, my_fsdp * share, share, 0)
    inverse_own = lax.dynamic_slice_in_dim(pix_inverse, my_fsdp * share, share, 0)
    d_pixels = norm_back(hat_own, inverse_own, gain_f, d_pix_own.T)

    small_grads = jnp.stack(
        [enc_front[0], enc_sums[0], enc_front[1], enc_sums[1], enc_sums[2], enc_sums[3]]
        + [lat_front[0], lat_sums[0], lat_front[1], lat_sums[1], lat_sums[2], lat_sums[3]]
    )
    high = small_grads.astype(BF)
    low = (small_grads - high.astype(F32)).astype(BF)
    half_pad = half - padded
    spread = jnp.eye(n_small, half_pad, dtype=BF)
    kv_grads = jnp.concatenate(
        [d_key_t.astype(BF), tm(high, spread).astype(BF), d_value_t.astype(BF), tm(low, spread).astype(BF)], axis=1
    )
    kv_grads = with_layout_constraint(kv_grads, Layout((0, 1)))
    end_groups = halves_of(core_sum([kv_grads, d_w_query], sizes, me))
    for place in range(len(far)):
        end_groups = far_pair(end_groups, place, sizes, me)
    mlp_grads = finish_sum(mlp_groups, sizes, my_fsdp)
    end_grads = finish_sum(end_groups, sizes, my_fsdp)
    kv_own = end_grads[0]
    d_pix_kv = jnp.stack([kv_own[:, :features].T, kv_own[:, width // 2 : width // 2 + features].T])
    start = width // 2 + padded
    small_own = (kv_own[:, padded : padded + n_small] + kv_own[:, start : start + n_small]).T
    return (
        result,
        d_latents.reshape(shape),
        d_pixels,
        d_pix_sums[0],
        d_pix_sums[1],
        d_pix_kv,
        end_grads[1],
        mlp_grads[2],
        mlp_grads[:2],
        small_own[:n_gain],
        small_own[n_gain : n_gain + n_bias],
        qkv_grads,
        after_grads[2],
        after_grads[:2],
        small_own[n_gain + n_bias : 2 * n_gain + n_bias],
        small_own[2 * n_gain + n_bias :],
    )


def solution(mesh):
    split, rows, columns = P("dp", "fsdp", None), P(AXES, None), P(None, AXES)
    middle = P(None, AXES, None)
    weights = (P(None, None, AXES), rows, rows, middle, columns, columns, middle, rows, middle, columns, columns)
    return jax.shard_map(
        partial(body, (mesh.shape["dp"], mesh.shape["fsdp"])),
        mesh=mesh,
        in_specs=(split, P("dp", None), P("dp", None), P(), P()) + weights + (split,),
        out_specs=(split, split, rows, P(), P()) + weights,
        check_vma=False,
    )
```

```python
from functools import partial

import jax
import jax.numpy as jnp
from jax import lax
from jax.experimental.layout import Layout, with_layout_constraint
from jax.experimental import pallas as pl
from jax.experimental.pallas import tpu as pltpu
from jax.sharding import PartitionSpec as P

HEADS = 8
HEAD = 128
USED = 1792
EPSILON = 1e-05
MASKED = -1e30
AXES = ("dp", "fsdp")
LANES = 128
HEADS_AT_ONCE = 2
BF = jnp.bfloat16
F32 = jnp.float32


def dot(left, right, dims):
    return lax.dot_general(left, right, ((dims[0], dims[1]), ((), ())), preferred_element_type=F32)


def mm(left, right):
    return dot(left, right, ((left.ndim - 1,), (0,)))


def mm_t(left, right):
    return dot(left, right, ((left.ndim - 1,), (1,)))


def tm(left, right):
    return dot(left, right, ((0,), (0,)))


def norm_parts(values):
    average = jnp.mean(values, axis=-1, keepdims=True)
    centered = values - average
    variance = jnp.mean(centered * centered, axis=-1, keepdims=True)
    inverse = lax.rsqrt(variance + EPSILON)
    return centered * inverse, inverse


def norm_back(hat, inverse, gains, grad_out):
    grad_hat = grad_out * gains
    first = jnp.mean(grad_hat, axis=-1, keepdims=True)
    second = jnp.mean(grad_hat * hat, axis=-1, keepdims=True)
    return inverse * (grad_hat - first - hat * second)


def gelu(values):
    return 0.5 * values * (1.0 + lax.erf(values * (0.5**0.5)))


def gelu_slope(values):
    density = jnp.exp(-0.5 * values * values) * ((0.5 / jnp.pi) ** 0.5)
    return 0.5 * (1.0 + lax.erf(values * (0.5**0.5))) + values * density


def xor_permute(values, sizes, step):
    dp_size, fsdp_size = sizes
    total = dp_size * fsdp_size
    return lax.ppermute(values, AXES, [(i, i ^ step) for i in range(total)])


def seal(*values):
    return lax.optimization_barrier(values)


def bits_of(sizes):
    low = sizes[1].bit_length() - 1
    every = list(range((sizes[0] * sizes[1]).bit_length() - 1))
    return every[:low], every[low], every[low + 1 :]


def gather_fsdp(values, sizes):
    return [values] + [xor_permute(values, sizes, k) for k in range(1, sizes[1])]


def slot_shift(values, size, j):
    return lax.ppermute(values, "fsdp", [(i, (i + j) % size) for i in range(size)])


def order_fsdp(parts, sizes, me):
    low, _, _ = bits_of(sizes)
    for bit in low:
        mine = ((me >> bit) & 1) == 1
        parts = [jnp.where(mine, parts[k ^ (1 << bit)], parts[k]) for k in range(len(parts))]
    return jnp.stack(parts)


def merge(own, got, bit, above, me):
    mine = ((me >> bit) & 1) == 1
    view = (2**above, -1) + own.shape[1:]
    own, got = own.reshape(view), got.reshape(view)
    both = jnp.stack([jnp.where(mine, got, own), jnp.where(mine, own, got)], axis=1)
    return both.reshape((-1,) + own.shape[2:])


def far_step(groups, place, sizes, me):
    _, _, far = bits_of(sizes)
    result = []
    for values, order in zip(groups, (far, far[::-1])):
        bit, held = order[place], order[:place]
        got = xor_permute(values, sizes, 1 << bit)
        result.append(merge(values, got, bit, sum(1 for other in held if other > bit), me))
    return result


def core_swap(groups, sizes):
    _, core, _ = bits_of(sizes)
    return [xor_permute(values, sizes, 1 << core) for values in groups]


def sources_of(groups, got, count, sizes, me):
    own = groups[0].shape[2] // count
    if own % 16 == 0:
        return [groups[0], got[0], groups[1], got[1]]
    _, core, _ = bits_of(sizes)
    mine = ((me >> core) & 1) == 1
    both = [jnp.stack([jnp.where(mine, g, v), jnp.where(mine, v, g)], axis=1) for v, g in zip(groups, got)]
    whole = jnp.concatenate(both, axis=-1)
    parts = [whole[:, :, :, i * own : (i + 1) * own] for i in range(count)]
    return [part.reshape(-1, part.shape[-1]) for part in parts]


def halves_of(values):
    half = values.shape[-1] // 2
    return [values[..., :half], values[..., half:]]


def core_terms(grads, sizes, me):
    _, core, _ = bits_of(sizes)
    if len(grads) == 1:
        mine = (me >> core) & 1
        count, width = grads[0].shape[0], grads[0].shape[-1]
        view = jnp.swapaxes(grads[0].reshape(count, sizes[0] // 2, 2, -1, width), 0, 1)
        send = lax.dynamic_index_in_dim(view, 1 - mine, 2, keepdims=False)
        keep = lax.dynamic_index_in_dim(view, mine, 2, keepdims=False)
    else:
        send, keep = grads
    got = xor_permute(send, sizes, 1 << core)
    return [list(terms) for terms in zip(halves_of(keep), halves_of(got))]


def sum_of(terms):
    total = terms[0].astype(F32)
    for term in terms[1:]:
        total = total + term.astype(F32)
    return total


def far_terms(terms, bit, held, sizes, me):
    above = sum(1 for other in held if other > bit)
    mine = (me >> bit) & 1

    def half(term, side):
        view = term.reshape((2**above, 2, -1) + term.shape[1:])
        part = lax.dynamic_index_in_dim(view, side, 1, keepdims=False)
        return part.reshape((-1,) + term.shape[1:])

    send = sum_of([half(term, 1 - mine) for term in terms]).astype(BF)
    return [half(term, mine) for term in terms] + [xor_permute(send, sizes, 1 << bit)]


def far_pair(groups, place, sizes, me):
    _, _, far = bits_of(sizes)
    result = []
    for terms, order in zip(groups, (far, far[::-1])):
        held = [bit for bit in far if bit not in order[:place]]
        result.append(far_terms(terms, order[place], held, sizes, me))
    return result


def finish_sum(groups, sizes, my_fsdp):
    def part(term, shard):
        view = term[0].reshape(term.shape[1], sizes[1], -1, term.shape[-1])
        return lax.dynamic_index_in_dim(view, shard, 1, keepdims=False)

    def both(shard):
        return jnp.concatenate([sum_of([part(term, shard) for term in terms]) for terms in groups], axis=-1)

    got = [xor_permute(both(my_fsdp ^ k).astype(BF), sizes, k) for k in range(1, sizes[1])]
    return sum_of([both(my_fsdp)] + got)


def total_over(values, bits, sizes):
    for bit in bits:
        values = values + xor_permute(values, sizes, 1 << bit)
    return values


class Pack:
    def __init__(self, sizes, own, width):
        self.far, self.fsdp, self.own, self.width = sizes[0] // 2, sizes[1], own, width
        self.block = width // sizes[0]
        self.packed = own % 16 == 0
        self.split = self.block % LANES == 0

    def sources(self, count):
        return 4 if self.packed else count

    def scratch(self):
        shape = (self.far, 2, self.fsdp, self.own, self.width) if self.packed else (self.width, self.width)
        return pltpu.VMEM(shape, BF)

    def fetch(self, sources, index, scratch, sem):
        if not self.packed:
            pltpu.make_async_copy(sources[index], scratch, sem).start()
            return
        core = lax.axis_index("dp") & 1
        rows, half = pl.ds(index * self.own, self.own), self.width // 2
        for start, mine, other in ((0, sources[0], sources[1]), (half, sources[2], sources[3])):
            for source, side in ((mine, core), (other, 1 - core)):
                target = scratch.at[:, side, :, :, pl.ds(start, half)]
                pltpu.make_async_copy(source.at[:, :, rows, :], target, sem).start()

    def ready(self, scratch, sem):
        pltpu.make_async_copy(scratch, scratch, sem).wait()
        return scratch[...].reshape(self.width, self.width)

    def grads(self, count):
        if not self.split:
            return [jax.ShapeDtypeStruct((count, self.width, self.width), BF)]
        return [jax.ShapeDtypeStruct((self.far, count, self.block, self.width), BF)] * 2

    def columns(self, ref):
        if not self.split:
            return [ref[...]]
        core = lax.axis_index("dp") & 1
        result = []
        for side in (1 - core, core):
            starts = [pl.multiple_of((2 * i + side) * self.block, self.block) for i in range(self.far)]
            result.append(jnp.concatenate([ref[:, pl.ds(start, self.block)] for start in starts], axis=1))
        return result

    def put(self, refs, index, values):
        for ref, value in zip(refs, values):
            value = value.astype(BF)
            if self.split:
                ref[:, index] = value.reshape(self.far, self.block, self.width)
            else:
                ref[index] = value

    def put_product(self, refs, index, left_ref, right):
        self.put(refs, index, [tm(left, right) for left in self.columns(left_ref)])


def kernel_call(kernel, name, operands, sources, outs, scratch, vmem_mb, work_mb, scalars=()):
    specs = [pl.BlockSpec(memory_space=pltpu.SMEM)] * len(scalars)
    specs += [pl.BlockSpec(memory_space=pltpu.VMEM)] * len(operands)
    specs += [pl.BlockSpec(memory_space=pl.ANY)] * len(sources)
    return pl.pallas_call(
        kernel,
        in_specs=specs,
        out_specs=[pl.BlockSpec(memory_space=pltpu.VMEM)] * len(outs),
        out_shape=outs,
        scratch_shapes=scratch,
        compiler_params=pltpu.CompilerParams(vmem_limit_bytes=vmem_mb * 2**20),
        cost_estimate=pl.CostEstimate(flops=2**30, bytes_accessed=work_mb * 2**20, transcendentals=2**20),
        name=name,
    )(*scalars, *operands, *sources)


def column_sum(values):
    return jnp.sum(values, axis=0, keepdims=True)


def softmax(scores):
    powers = jnp.exp(scores - jnp.max(scores, axis=-1, keepdims=True))
    return powers * (1.0 / jnp.sum(powers, axis=-1, keepdims=True))


def small_rows(small_ref):
    return lambda i: small_ref[i : i + 1]


def encoder_kernel(pack, n_source, padded, lat_rows, *refs):
    counts, latents, pix = refs[:3]
    sources, rest = refs[3 : 3 + n_source], refs[3 + n_source :]
    small_o, q_o, query_pix_o, probs_o, mixed_pix_o, mixed_o, resid_o, pre_o, act_o, first_o, low_o = rest[:11]
    scratch, sems = rest[11:16], rest[16]
    half = pack.width // 2
    for slot, index in enumerate((4, 2, 3, 0, 1)):
        pack.fetch(sources, index, scratch[slot], sems.at[slot])
    latent_in = latents[...].astype(F32)
    hat, _ = norm_parts(latent_in)
    kv = pack.ready(scratch[0], sems.at[0])
    shape = (small_o.shape[0], half - padded)
    eye = lax.broadcasted_iota(jnp.int32, shape, 0) == lax.broadcasted_iota(jnp.int32, shape, 1)
    small_o[...] = mm_t(eye.astype(F32).astype(BF), kv[:, padded:half])
    small = small_rows(small_o)
    in_low = (hat * small(0) + small(2)).astype(BF)
    query = mm(in_low, pack.ready(scratch[1], sems.at[1])).astype(BF)
    q_o[...] = query
    query_pix = mm(query, kv[:, :padded]).astype(BF)
    query_pix_o[...] = query_pix
    shape = probs_o.shape
    row, column = lax.broadcasted_iota(jnp.int32, shape, 0), lax.broadcasted_iota(jnp.int32, shape, 1)
    first, end, total = jnp.zeros(shape, jnp.int32), jnp.zeros(shape, jnp.int32), 0
    for image in range(shape[0] // lat_rows):
        here = (row >= image * lat_rows) & (row < (image + 1) * lat_rows)
        first = jnp.where(here, total, first)
        total = total + counts[0, image]
        end = jnp.where(here, total, end)
    scores = mm_t(query_pix, pix[...]) * pack.width**-0.5
    probs = softmax(jnp.where((column >= first) & (column < end), scores, MASKED))
    probs_o[...] = probs
    mixed_pix = mm(probs.astype(BF), pix[...]).astype(BF)
    mixed_pix_o[...] = mixed_pix
    mixed = mm_t(mixed_pix, kv[:, half : half + padded]).astype(BF)
    mixed_o[...] = mixed
    resid = latent_in + mm(mixed, pack.ready(scratch[2], sems.at[2]))
    resid_o[...] = resid
    hat, _ = norm_parts(resid)
    normed = (hat * small(1) + small(3)).astype(BF)
    pre = mm(normed, pack.ready(scratch[3], sems.at[3])) + small(4)
    pre_o[...] = pre
    act = gelu(pre).astype(BF)
    act_o[...] = act
    out = resid + mm(act, pack.ready(scratch[4], sems.at[4])) + small(5)
    first_o[...] = out
    hat, _ = norm_parts(out)
    low_o[...] = (hat * small(6) + small(8)).astype(BF)


def fill_every(every, own, others, lat_rows, rows):
    every[0:rows] = own[...]
    count = len(others) // (rows // lat_rows)
    for i, shard in enumerate(others):
        start = (1 + i % count) * rows + i // count * lat_rows
        every[start : start + lat_rows] = shard[...]


def attention_kernel(pack, n_source, n_other, lat_rows, *refs):
    own, others, rest = refs[0], refs[1 : 1 + n_other], refs[1 + n_other :]
    sources, rest = rest[:n_source], rest[n_source:]
    q_o, k_o, v_o, mixed_o = rest[:4]
    scratch, every, sems = rest[4:7], rest[7], rest[8]
    for index in range(3):
        pack.fetch(sources, index, scratch[index], sems.at[index])
    rows = own.shape[0]
    fill_every(every, own, others, lat_rows, rows)
    q_o[...] = mm(own[...], pack.ready(scratch[0], sems.at[0])).astype(BF)
    k_o[...] = mm(every[...], pack.ready(scratch[1], sems.at[1])).astype(BF).reshape(k_o.shape)
    v_o[...] = mm(every[...], pack.ready(scratch[2], sems.at[2])).astype(BF).reshape(k_o.shape)

    def some_heads(step, carry):
        places, loaded = [], []
        for head in range(HEADS_AT_ONCE):
            cols = pl.ds(pl.multiple_of((step * HEADS_AT_ONCE + head) * HEAD, HEAD), HEAD)
            for start in range(0, rows, lat_rows):
                part = pl.ds(start, lat_rows)
                places.append((part, cols))
                loaded.append((q_o[part, cols], k_o[:, part, cols].reshape(-1, HEAD), v_o[:, part, cols].reshape(-1, HEAD)))
        scores = [mm_t(q, k) * HEAD**-0.5 for q, k, _ in loaded]
        probs = [softmax(score).astype(BF) for score in scores]
        mixed = [mm(prob, v).astype(BF) for prob, (_, _, v) in zip(probs, loaded)]
        for place, value in zip(places, mixed):
            mixed_o[place] = value
        return carry

    lax.fori_loop(0, HEADS // HEADS_AT_ONCE, some_heads, 0)


def attention_back_kernel(pack, n_source, n_other, lat_rows, *refs):
    q, k_ref, v_ref, grad, own = refs[:5]
    others, rest = refs[5 : 5 + n_other], refs[5 + n_other :]
    sources, rest = rest[:n_source], rest[n_source:]
    outs = 2 + len(pack.grads(3))
    slot_o, slots_o, *grad_o = rest[:outs]
    scratch, (every, dq, dk, dv, sems) = rest[outs : outs + 3], rest[outs + 3 :]
    for index in range(3):
        pack.fetch(sources, index, scratch[index], sems.at[index])
    rows = q.shape[0]
    scale = HEAD**-0.5
    fill_every(every, own, others, lat_rows, rows)

    def some_heads(step, carry):
        places, loaded = [], []
        for head in range(HEADS_AT_ONCE):
            cols = pl.ds(pl.multiple_of((step * HEADS_AT_ONCE + head) * HEAD, HEAD), HEAD)
            for start in range(0, rows, lat_rows):
                part = pl.ds(start, lat_rows)
                places.append((part, cols))
                k, v = k_ref[:, part, cols].reshape(-1, HEAD), v_ref[:, part, cols].reshape(-1, HEAD)
                loaded.append((q[part, cols], k, v, grad[part, cols]))
        scores = [mm_t(query, k) * scale for query, k, _, _ in loaded]
        grad_probs = [mm_t(out_grad, v) for _, _, v, out_grad in loaded]
        results = []
        for score, grad_prob, (query, k, v, out_grad) in zip(scores, grad_probs, loaded):
            prob = softmax(score)
            inner = jnp.sum(prob * grad_prob, axis=-1, keepdims=True)
            grad_score = (prob * (grad_prob - inner) * scale).astype(BF)
            results.append((mm(grad_score, k), tm(grad_score, query), tm(prob.astype(BF), out_grad)))
        for (part, cols), (one, two, three) in zip(places, results):
            dq[part, cols] = one.astype(BF)
            dk[:, part, cols] = two.astype(BF).reshape(pack.fsdp, lat_rows, HEAD)
            dv[:, part, cols] = three.astype(BF).reshape(pack.fsdp, lat_rows, HEAD)
        return carry

    lax.fori_loop(0, HEADS // HEADS_AT_ONCE, some_heads, 0)
    d_q, d_k, d_v = dq[...], dk[...].reshape(-1, pack.width), dv[...].reshape(-1, pack.width)
    w_query = pack.ready(scratch[0], sems.at[0])
    w_key, w_value = pack.ready(scratch[1], sems.at[1]), pack.ready(scratch[2], sems.at[2])
    slot_o[...] = mm_t(d_q, w_query) + mm_t(d_k[:rows], w_key) + mm_t(d_v[:rows], w_value)
    others = mm_t(d_k[rows:], w_key) + mm_t(d_v[rows:], w_value)
    slots_o[...] = others.astype(BF).reshape(slots_o.shape)
    pack.put(grad_o, 0, [tm(left, d_q) for left in pack.columns(every.at[pl.ds(0, rows)])])
    columns = pack.columns(every)
    pack.put(grad_o, 1, [tm(left, d_k) for left in columns])
    pack.put(grad_o, 2, [tm(left, d_v) for left in columns])


def latent_kernel(pack, n_source, *refs):
    mixed, first_out, cotangent, small_ref = refs[:4]
    sources, rest = refs[4 : 4 + n_source], refs[4 + n_source :]
    outs = 4 + len(pack.grads(3))
    result_o, grad_o, d_mixed_o, sums_o, *grads_o = rest[:outs]
    scratch, (act_s, normed_s, sems) = rest[outs : outs + 3], rest[outs + 3 :]
    for index in range(3):
        pack.fetch(sources, index, scratch[index], sems.at[index])
    small = small_rows(small_ref)
    w_out = pack.ready(scratch[0], sems.at[0])
    resid = first_out[...] + mm(mixed[...], w_out)
    hat, inverse = norm_parts(resid)
    normed_s[...] = (hat * small(7) + small(9)).astype(BF)
    w_first = pack.ready(scratch[1], sems.at[1])
    pre = mm(normed_s[...], w_first) + small(10)
    act_s[...] = gelu(pre).astype(BF)
    w_second = pack.ready(scratch[2], sems.at[2])
    result_o[...] = (resid + mm(act_s[...], w_second) + small(11)).astype(BF)
    grad_low = cotangent[...]
    grad_out = grad_low.astype(F32)
    pack.put_product(grads_o, 1, act_s, grad_low)
    d_pre = mm_t(grad_low, w_second) * gelu_slope(pre)
    d_pre_low = d_pre.astype(BF)
    pack.put_product(grads_o, 0, normed_s, d_pre_low)
    d_normed = mm_t(d_pre_low, w_first)
    grad_mid = grad_out + norm_back(hat, inverse, small(7), d_normed)
    grad_o[...] = grad_mid
    grad_low = grad_mid.astype(BF)
    d_mixed_o[...] = mm_t(grad_low, w_out).astype(BF)
    pack.put_product(grads_o, 2, mixed, grad_low)
    sums_o[0:1] = column_sum(d_normed * hat)
    sums_o[1:2] = column_sum(d_normed)
    sums_o[2:3] = column_sum(d_pre)
    sums_o[3:4] = column_sum(grad_out)


def encoder_back_kernel(pack, n_source, n_other, images, *refs):
    slot, grad_mid, first_out, resid, pre_ref, act, small_ref = refs[:7]
    others, rest = refs[7 : 7 + n_other], refs[7 + n_other :]
    sources, rest = rest[:n_source], rest[n_source:]
    outs = 2 + len(pack.grads(2))
    grad_o, sums_o, *grads_o = rest[:outs]
    scratch, (normed_s, sems) = rest[outs : outs + 2], rest[outs + 2 :]
    for index in range(2):
        pack.fetch(sources, index, scratch[index], sems.at[index])
    small = small_rows(small_ref)
    parts, count = [], n_other // images
    for image in range(images):
        parts.append(sum(ref[...].astype(F32) for ref in others[image * count : (image + 1) * count]))
    d_normed = slot[...] + jnp.concatenate(parts, axis=0)
    hat, inverse = norm_parts(first_out[...])
    sums_o[0:1] = column_sum(d_normed * hat)
    sums_o[1:2] = column_sum(d_normed)
    grad_out = grad_mid[...] + norm_back(hat, inverse, small(6), d_normed)
    grad_low = grad_out.astype(BF)
    w_second = pack.ready(scratch[1], sems.at[1])
    d_pre = mm_t(grad_low, w_second) * gelu_slope(pre_ref[...])
    d_pre_low = d_pre.astype(BF)
    d_normed = mm_t(d_pre_low, pack.ready(scratch[0], sems.at[0]))
    hat, inverse = norm_parts(resid[...])
    grad_o[...] = grad_out + norm_back(hat, inverse, small(1), d_normed)
    normed_s[...] = (hat * small(1) + small(3)).astype(BF)
    pack.put_product(grads_o, 0, normed_s, d_pre_low)
    pack.put_product(grads_o, 1, act, grad_low)
    sums_o[2:3] = column_sum(d_normed * hat)
    sums_o[3:4] = column_sum(d_normed)
    sums_o[4:5] = column_sum(d_pre)
    sums_o[5:6] = column_sum(grad_out)


def cross_back_kernel(pack, n_source, padded, share, *refs):
    grad_ref, latents, mixed, mixed_pix, probs_ref, pix, query_pix, enc_q, small_ref, lat_sums, enc_sums, pix_hat = refs[:12]
    sources, rest = refs[12 : 12 + n_source], refs[12 + n_source :]
    outs = 3 + len(pack.grads(3))
    d_latents_o, d_pix_o, pix_sums_o, *grads_o = rest[:outs]
    scratch, (d_mixed_s, in_low_s, high_s, low_s, sems) = rest[outs : outs + 3], rest[outs + 3 :]
    for slot, index in enumerate((3, 4, 2)):
        pack.fetch(sources, index, scratch[slot], sems.at[slot])
    small = small_rows(small_ref)
    half = pack.width // 2
    scale = pack.width**-0.5
    grad_enc = grad_ref[...]
    grad_low = grad_enc.astype(BF)
    d_mixed_s[...] = mm_t(grad_low, pack.ready(scratch[0], sems.at[0])).astype(BF)
    kv = pack.ready(scratch[1], sems.at[1])
    mixed_back = mm(d_mixed_s[...], kv[:, half : half + padded]).astype(BF)
    d_probs = mm_t(mixed_back, pix[...])
    probs = probs_ref[...]
    inner = jnp.sum(probs * d_probs, axis=-1, keepdims=True)
    d_scores = (probs * (d_probs - inner) * scale).astype(BF)
    d_pix = tm(query_pix[...], d_scores) + tm(mixed_back, probs.astype(BF))
    kept, used = pix_hat.shape
    d_pix = d_pix[:kept]
    gain_sum = jnp.sum(d_pix * pix_hat[...], axis=-1, keepdims=True)
    bias_sum = jnp.sum(d_pix, axis=-1, keepdims=True)
    lane = lax.broadcasted_iota(jnp.int32, pix_sums_o.shape, 1)
    pix_sums_o[...] = jnp.where(lane == 0, gain_sum, jnp.where(lane == 1, bias_sum, 0.0))
    shard = lax.axis_index("fsdp")
    for target in range(pack.fsdp):
        slot = lax.rem(shard + pack.fsdp - target, pack.fsdp)
        last = min(used, (target + 1) * share)
        piece = d_pix[:, target * share : last]
        if last < (target + 1) * share:
            piece = jnp.concatenate([piece, jnp.zeros((kept, (target + 1) * share - last), F32)], axis=1)
        d_pix_o[slot] = piece
    d_query_pix = mm(d_scores, pix[...]).astype(BF)
    d_enc_q = mm_t(d_query_pix, kv[:, :padded]).astype(BF)
    hat, inverse = norm_parts(latents[...].astype(F32))
    in_low_s[...] = (hat * small(0) + small(2)).astype(BF)
    d_normed = mm_t(d_enc_q, pack.ready(scratch[2], sems.at[2]))
    d_latents_o[...] = grad_enc + norm_back(hat, inverse, small(0), d_normed)
    order = [column_sum(d_normed * hat), enc_sums[2:3], column_sum(d_normed), enc_sums[3:4], enc_sums[4:5], enc_sums[5:6]]
    order += [enc_sums[0:1], lat_sums[0:1], enc_sums[1:2], lat_sums[1:2], lat_sums[2:3], lat_sums[3:4]]
    sums = jnp.concatenate(order + [jnp.zeros((16 - len(order), pack.width), F32)], axis=0)
    high = sums.astype(BF)
    high_s[...] = high
    low_s[...] = (sums - high.astype(F32)).astype(BF)
    shape = (16, half - padded)
    eye = lax.broadcasted_iota(jnp.int32, shape, 0) == lax.broadcasted_iota(jnp.int32, shape, 1)
    eye = eye.astype(F32).astype(BF)
    blocks = []
    for left, high_c, right, low_c in zip(*(pack.columns(r) for r in (enc_q, high_s, d_mixed_s, low_s))):
        columns = [tm(left, d_query_pix), tm(high_c, eye), tm(right, mixed_pix[...]), tm(low_c, eye)]
        blocks.append(jnp.concatenate(columns, axis=1))
    pack.put(grads_o, 0, blocks)
    pack.put_product(grads_o, 1, in_low_s, d_enc_q)
    pack.put_product(grads_o, 2, mixed, grad_low)


def pad_lanes(values, width):
    return jnp.pad(values, [(0, 0)] * (values.ndim - 1) + [(0, width - values.shape[-1])])


def body(
    sizes,
    latents,
    pixels,
    lengths,
    pix_gain,
    pix_bias,
    pix_kv,
    enc_query,
    enc_out,
    enc_mlp,
    enc_gains,
    enc_biases,
    lat_qkv,
    lat_out,
    lat_mlp,
    lat_gains,
    lat_biases,
    cotangent,
):
    dp_size, fsdp_size = sizes
    devices = dp_size * fsdp_size
    my_fsdp = lax.axis_index("fsdp")
    me = lax.axis_index("dp") * fsdp_size + my_fsdp
    images, lat_rows, width = latents.shape
    rows = images * lat_rows
    pix_rows, features = pixels.shape
    padded = -(-features // LANES) * LANES
    own = width // devices

    _, _, far = bits_of(sizes)
    steps = range(1, len(far))
    half = width // 2

    small = jnp.concatenate([enc_gains, enc_biases, lat_gains, lat_biases], axis=0)
    n_small = small.shape[0]
    place_pix, place_small = jnp.eye(features, padded, dtype=BF), jnp.eye(n_small, half - padded, dtype=BF)
    kv_t = jnp.concatenate(
        [tm(pix_kv[0], place_pix), tm(small, place_small), pad_lanes(tm(pix_kv[1], place_pix), half)], axis=1
    ).astype(BF)
    enc_parts = gather_fsdp(jnp.concatenate([enc_mlp[0], enc_mlp[1], enc_query, enc_out, kv_t], axis=0), sizes)
    gain_f = pix_gain.astype(F32)
    pix_hat, pix_inverse = norm_parts(pixels.astype(F32))
    pix_low = pad_lanes((pix_hat * gain_f + pix_bias.astype(F32)).astype(BF), padded)[:USED]
    pix_hat_t = jnp.pad(pix_hat[:USED].T, ((0, -features % 8), (0, 0)))
    enc_parts, pix_low, pix_hat, pix_hat_t, pix_inverse, lat_qkv = seal(
        enc_parts, pix_low, pix_hat, pix_hat_t, pix_inverse, lat_qkv
    )

    enc_groups = far_step([v[None] for v in halves_of(order_fsdp(enc_parts, sizes, me))], 0, sizes, me)
    qkv_parts = gather_fsdp(lat_qkv.reshape(3 * own, width), sizes)
    enc_groups, qkv_parts, lat_out, lat_mlp = seal(enc_groups, qkv_parts, lat_out, lat_mlp)

    for place in steps:
        enc_groups = far_step(enc_groups, place, sizes, me)
    other_parts = gather_fsdp(jnp.concatenate([lat_out, lat_mlp[0], lat_mlp[1]], axis=0), sizes)
    qkv_groups = [v[None] for v in halves_of(order_fsdp(qkv_parts, sizes, me))]
    enc_groups, qkv_groups, other_parts = seal(enc_groups, qkv_groups, other_parts)

    enc_got = core_swap(enc_groups, sizes)
    qkv_groups = far_step(qkv_groups, 0, sizes, me)
    other_groups = [v[None] for v in halves_of(order_fsdp(other_parts, sizes, me))]
    enc_groups, enc_got, qkv_groups, other_groups = seal(enc_groups, enc_got, qkv_groups, other_groups)

    pack = Pack(sizes, own, width)
    for place in steps:
        qkv_groups = far_step(qkv_groups, place, sizes, me)
    enc_sources = sources_of(enc_groups, enc_got, 5, sizes, me)
    n_gain, n_bias = enc_gains.shape[0], enc_biases.shape[0]
    wide, dma = jax.ShapeDtypeStruct, pltpu.SemaphoreType.DMA

    small_all, enc_q, query_pix, probs, mixed_pix, enc_mixed, enc_resid, enc_pre, enc_act, first_out, lat_low = kernel_call(
        partial(encoder_kernel, pack, len(enc_sources), padded, lat_rows),
        "encoder",
        [latents.reshape(rows, width), pix_low],
        enc_sources,
        [wide((16, width), F32), wide((rows, width), BF), wide((rows, padded), BF), wide((rows, USED), F32)]
        + [wide((rows, padded), BF), wide((rows, width), BF), wide((rows, width), F32), wide((rows, width), F32)]
        + [wide((rows, width), BF), wide((rows, width), F32), wide((rows, width), BF)],
        [pack.scratch()] * 5 + [dma((5,))],
        36,
        36,
        scalars=[lengths],
    )
    lat_low, qkv_groups, other_groups = seal(lat_low, qkv_groups, other_groups)

    shards = []
    for image in range(images):
        part = lat_low[image * lat_rows : (image + 1) * lat_rows]
        shards += [slot_shift(part, fsdp_size, j) for j in range(1, fsdp_size)]
        if image == 0:
            qkv_got = core_swap(qkv_groups, sizes)
            qkv_got, other_groups = seal(qkv_got, other_groups)
        if image < len(far):
            other_groups = far_step(other_groups, image, sizes, me)
        lat_low, shards, qkv_got, other_groups = seal(lat_low, shards, qkv_got, other_groups)

    for place in range(images, len(far)):
        other_groups = far_step(other_groups, place, sizes, me)
    other_got = core_swap(other_groups, sizes)
    qkv_sources = sources_of(qkv_groups, qkv_got, 3, sizes, me)
    every = wide((fsdp_size, rows, width), BF)
    every_flat = pltpu.VMEM((fsdp_size * rows, width), BF)
    lat_q, lat_k, lat_v, lat_mixed = kernel_call(
        partial(attention_kernel, pack, len(qkv_sources), len(shards), lat_rows),
        "attention",
        [lat_low] + list(shards),
        qkv_sources,
        [wide((rows, width), BF), every, every, wide((rows, width), BF)],
        [pack.scratch()] * 3 + [every_flat, dma((3,))],
        32,
        40,
    )
    other_sources = sources_of(other_groups, other_got, 3, sizes, me)
    result, grad_mid, d_mixed, lat_sums, *grads_m = kernel_call(
        partial(latent_kernel, pack, len(other_sources)),
        "latent",
        [lat_mixed, first_out, cotangent.reshape(rows, width), small_all],
        other_sources,
        [wide((rows, width), BF), wide((rows, width), F32), wide((rows, width), BF), wide((8, width), F32)] + pack.grads(3),
        [pack.scratch()] * 3 + [pltpu.VMEM((rows, width), BF)] * 2 + [dma((3,))],
        36,
        36,
    )

    grads_m = core_terms(grads_m, sizes, me)
    slot, slots, *grads_q = kernel_call(
        partial(attention_back_kernel, pack, len(qkv_sources), len(shards), lat_rows),
        "attention_back",
        [lat_q, lat_k, lat_v, d_mixed, lat_low] + list(shards),
        qkv_sources,
        [wide((rows, width), F32), wide((fsdp_size - 1, rows, width), BF)] + pack.grads(3),
        [pack.scratch()] * 3
        + [every_flat, pltpu.VMEM((rows, width), BF)]
        + [pltpu.VMEM(every.shape, BF)] * 2
        + [dma((3,))],
        46,
        72,
    )
    slot, slots, grads_q = seal(slot, slots, grads_q)

    received = []
    for image in range(images):
        part = slots[:, image * lat_rows : (image + 1) * lat_rows]
        received += [slot_shift(part[j - 1], fsdp_size, fsdp_size - j) for j in range(1, fsdp_size)]
        if image < len(far):
            grads_m = far_pair(grads_m, image, sizes, me)
        slots, received, grads_m = seal(slots, received, grads_m)
    for place in range(images, len(far)):
        grads_m = far_pair(grads_m, place, sizes, me)
    l_other_grads = finish_sum(grads_m, sizes, my_fsdp)
    grads_q = core_terms(grads_q, sizes, me)
    grad_enc, enc_sums, *grads_e = kernel_call(
        partial(encoder_back_kernel, pack, len(enc_sources), len(received), images),
        "encoder_back",
        [slot, grad_mid, first_out, enc_resid, enc_pre, enc_act, small_all] + list(received),
        enc_sources,
        [wide((rows, width), F32), wide((8, width), F32)] + pack.grads(2),
        [pack.scratch()] * 2 + [pltpu.VMEM((rows, width), BF), dma((2,))],
        34,
        36,
    )
    grad_enc, grads_e, grads_q = seal(grad_enc, grads_e, grads_q)

    grads_q = far_pair(grads_q, 0, sizes, me)
    share = pix_rows // fsdp_size
    kept = pix_hat_t.shape[0]
    d_latents, pieces, d_pix_sums, *grads_f = kernel_call(
        partial(cross_back_kernel, pack, len(enc_sources), padded, share),
        "cross_back",
        [grad_enc, latents.reshape(rows, width), enc_mixed, mixed_pix, probs, pix_low, query_pix, enc_q, small_all]
        + [lat_sums, enc_sums, pix_hat_t],
        enc_sources,
        [wide((rows, width), F32), wide((fsdp_size, kept, share), F32), wide((kept, LANES), F32)] + pack.grads(3),
        [pack.scratch()] * 3
        + [pltpu.VMEM((rows, width), BF)] * 2
        + [pltpu.VMEM((16, width), BF)] * 2
        + [dma((3,))],
        44,
        50,
    )
    pieces, grads_f, d_pix_sums, grads_q = seal(pieces, grads_f, d_pix_sums, grads_q)

    low_bits, core, _ = bits_of(sizes)
    grads_e = core_terms([jnp.concatenate(both, axis=-3) for both in zip(grads_e, grads_f)], sizes, me)
    for place in steps:
        grads_q = far_pair(grads_q, place, sizes, me)
    d_pix_sums = total_over(d_pix_sums[:features, :2].T, [core], sizes)
    pieces, grads_e, grads_q, d_pix_sums = seal(pieces, grads_e, grads_q, d_pix_sums)

    d_pix_own = pieces[0]
    for j in range(1, fsdp_size):
        d_pix_own = d_pix_own + slot_shift(pieces[j].astype(BF), fsdp_size, fsdp_size - j).astype(F32)
    grads_e = far_pair(grads_e, 0, sizes, me)
    d_pix_own, grads_e, grads_q, d_pix_sums = seal(d_pix_own, grads_e, grads_q, d_pix_sums)

    l_qkv_grads = finish_sum(grads_q, sizes, my_fsdp)
    for place in steps:
        grads_e = far_pair(grads_e, place, sizes, me)
    l_qkv_grads, grads_e, d_pix_sums = seal(l_qkv_grads, grads_e, d_pix_sums)
    d_pix_sums = total_over(d_pix_sums, far + low_bits, sizes)
    enc_grads = finish_sum(grads_e, sizes, my_fsdp)
    hat_own = lax.dynamic_slice_in_dim(pix_hat, my_fsdp * share, share, 0)
    inverse_own = lax.dynamic_slice_in_dim(pix_inverse, my_fsdp * share, share, 0)
    d_pixels = norm_back(hat_own, inverse_own, gain_f, d_pix_own[:features].T)
    kv_own = enc_grads[2]
    d_pix_kv = jnp.stack([kv_own[:, :features].T, kv_own[:, width // 2 : width // 2 + features].T])
    start = width // 2 + padded
    small_own = (kv_own[:, padded : padded + n_small] + kv_own[:, start : start + n_small]).T
    return (
        result.reshape(latents.shape),
        d_latents.reshape(latents.shape),
        d_pixels,
        d_pix_sums[0],
        d_pix_sums[1],
        d_pix_kv,
        enc_grads[3],
        enc_grads[4],
        enc_grads[:2],
        small_own[:n_gain],
        small_own[n_gain : n_gain + n_bias],
        l_qkv_grads,
        l_other_grads[2],
        l_other_grads[:2],
        small_own[n_gain + n_bias : 2 * n_gain + n_bias],
        small_own[2 * n_gain + n_bias :],
    )


def solution(mesh):
    split, rows, columns = P("dp", "fsdp", None), P(AXES, None), P(None, AXES)
    middle = P(None, AXES, None)
    weights = (P(None, None, AXES), rows, rows, middle, columns, columns, middle, rows, middle, columns, columns)
    return jax.shard_map(
        partial(body, (mesh.shape["dp"], mesh.shape["fsdp"])),
        mesh=mesh,
        in_specs=(split, P("dp", None), P("dp", None), P(), P()) + weights + (split,),
        out_specs=(split, split, rows, P(), P()) + weights,
        check_vma=False,
    )
```

```python
from functools import partial

import jax
import jax.numpy as jnp
from jax import lax
from jax.experimental.layout import Layout, with_layout_constraint
from jax.experimental import pallas as pl
from jax.experimental.pallas import tpu as pltpu
from jax.sharding import PartitionSpec as P

HEADS = 8
HEAD = 128
USED = 1792
EPSILON = 1e-05
MASKED = -1e30
AXES = ("dp", "fsdp")
LANES = 128
HEADS_AT_ONCE = 2
BF = jnp.bfloat16
F32 = jnp.float32


def dot(left, right, dims):
    return lax.dot_general(left, right, ((dims[0], dims[1]), ((), ())), preferred_element_type=F32)


def mm(left, right):
    return dot(left, right, ((left.ndim - 1,), (0,)))


def mm_t(left, right):
    return dot(left, right, ((left.ndim - 1,), (1,)))


def tm(left, right):
    return dot(left, right, ((0,), (0,)))


def norm_parts(values):
    average = jnp.mean(values, axis=-1, keepdims=True)
    centered = values - average
    variance = jnp.mean(centered * centered, axis=-1, keepdims=True)
    inverse = lax.rsqrt(variance + EPSILON)
    return centered * inverse, inverse


def norm_back(hat, inverse, gains, grad_out):
    grad_hat = grad_out * gains
    first = jnp.mean(grad_hat, axis=-1, keepdims=True)
    second = jnp.mean(grad_hat * hat, axis=-1, keepdims=True)
    return inverse * (grad_hat - first - hat * second)


def gelu(values):
    return 0.5 * values * (1.0 + lax.erf(values * (0.5**0.5)))


def gelu_slope(values):
    density = jnp.exp(-0.5 * values * values) * ((0.5 / jnp.pi) ** 0.5)
    return 0.5 * (1.0 + lax.erf(values * (0.5**0.5))) + values * density


def xor_permute(values, sizes, step):
    dp_size, fsdp_size = sizes
    total = dp_size * fsdp_size
    return lax.ppermute(values, AXES, [(i, i ^ step) for i in range(total)])


def seal(*values):
    return lax.optimization_barrier(values)


def bits_of(sizes):
    low = sizes[1].bit_length() - 1
    every = list(range((sizes[0] * sizes[1]).bit_length() - 1))
    return every[:low], every[low], every[low + 1 :]


def gather_fsdp(values, sizes):
    return [values] + [xor_permute(values, sizes, k) for k in range(1, sizes[1])]


def slot_shift(values, size, j):
    return lax.ppermute(values, "fsdp", [(i, (i + j) % size) for i in range(size)])


def hop(values, pairs):
    return lax.ppermute(values, "fsdp", pairs)


UP, DOWN = [(0, 1), (1, 2), (2, 3)], [(3, 2), (2, 1), (1, 0)]


def exchange_one(values):
    return [hop(values, UP), hop(values, DOWN)]


def exchange_two(first, shard):
    up, down = first
    far = jnp.where(shard == 1, up, down)
    return first + [hop(up, UP[1:]), hop(down, DOWN[1:]), hop(far, [(1, 3), (2, 0)])]


def fill_every(every, own, parts, n_shard):
    rows = own.shape[0]
    every[0:rows] = own[...]
    if len(parts) == n_shard - 1:
        slots = [part[...] for part in parts]
    else:
        shard = lax.axis_index("fsdp")
        up, down, up_two, down_two, far = [part[...] for part in parts]
        slots = [jnp.where(shard == 0, far, up), jnp.where(shard <= 1, down_two, up_two), jnp.where(shard == 3, far, down)]
    for j, slot in enumerate(slots):
        every[(j + 1) * rows : (j + 2) * rows] = slot


def collect_one(slots, shard):
    far = jnp.where(shard == 0, slots[0], slots[2])
    return [hop(slots[1], UP[:2]), hop(slots[1], DOWN[:2]), hop(far, [(0, 2), (3, 1)])]


def collect_two(slots, first, shard):
    up, down, far = [part.astype(F32) for part in first]
    up = slots[2].astype(F32) + up + jnp.where(shard == 2, far, 0.0)
    down = slots[0].astype(F32) + down + jnp.where(shard == 1, far, 0.0)
    return [hop(up.astype(BF), UP), hop(down.astype(BF), DOWN)]


def order_fsdp(parts, sizes, me):
    low, _, _ = bits_of(sizes)
    for bit in low:
        mine = ((me >> bit) & 1) == 1
        parts = [jnp.where(mine, parts[k ^ (1 << bit)], parts[k]) for k in range(len(parts))]
    return jnp.stack(parts)


def merge(own, got, bit, above, me):
    mine = ((me >> bit) & 1) == 1
    view = (2**above, -1) + own.shape[1:]
    own, got = own.reshape(view), got.reshape(view)
    both = jnp.stack([jnp.where(mine, got, own), jnp.where(mine, own, got)], axis=1)
    return both.reshape((-1,) + own.shape[2:])


def far_step(groups, place, sizes, me):
    _, _, far = bits_of(sizes)
    result = []
    for values, order in zip(groups, (far, far[::-1])):
        bit, held = order[place], order[:place]
        got = xor_permute(values, sizes, 1 << bit)
        result.append(merge(values, got, bit, sum(1 for other in held if other > bit), me))
    return result


def core_swap(whole, sizes):
    _, core, _ = bits_of(sizes)
    return xor_permute(whole, sizes, 1 << core)


def sources_of(whole, got, count, sizes, me):
    own = whole.shape[2] // count
    if own % 16 == 0:
        return [whole, got]
    _, core, _ = bits_of(sizes)
    mine = ((me >> core) & 1) == 1
    both = jnp.stack([jnp.where(mine, got, whole), jnp.where(mine, whole, got)], axis=1)
    parts = [both[:, :, :, i * own : (i + 1) * own] for i in range(count)]
    return [part.reshape(-1, part.shape[-1]) for part in parts]


def halves_of(values):
    half = values.shape[-1] // 2
    return [values[..., :half], values[..., half:]]


def core_terms(grads, sizes, me):
    _, core, _ = bits_of(sizes)
    if len(grads) == 1:
        mine = (me >> core) & 1
        count, width = grads[0].shape[0], grads[0].shape[-1]
        view = jnp.swapaxes(grads[0].reshape(count, sizes[0] // 2, 2, -1, width), 0, 1)
        send = lax.dynamic_index_in_dim(view, 1 - mine, 2, keepdims=False)
        keep = lax.dynamic_index_in_dim(view, mine, 2, keepdims=False)
    else:
        send, keep = grads
    got = xor_permute(send, sizes, 1 << core)
    return [list(terms) for terms in zip(halves_of(keep), halves_of(got))]


def sum_of(terms):
    total = terms[0].astype(F32)
    for term in terms[1:]:
        total = total + term.astype(F32)
    return total


def far_terms(terms, bit, held, sizes, me):
    above = sum(1 for other in held if other > bit)
    mine = (me >> bit) & 1

    def half(term, side):
        view = term.reshape((2**above, 2, -1) + term.shape[1:])
        part = lax.dynamic_index_in_dim(view, side, 1, keepdims=False)
        return part.reshape((-1,) + term.shape[1:])

    send = sum_of([half(term, 1 - mine) for term in terms]).astype(BF)
    return [half(term, mine) for term in terms] + [xor_permute(send, sizes, 1 << bit)]


def far_pair(groups, place, sizes, me):
    _, _, far = bits_of(sizes)
    result = []
    for terms, order in zip(groups, (far, far[::-1])):
        held = [bit for bit in far if bit not in order[:place]]
        result.append(far_terms(terms, order[place], held, sizes, me))
    return result


def finish_sum(groups, sizes, my_fsdp):
    def part(term, shard):
        view = term[0].reshape(term.shape[1], sizes[1], -1, term.shape[-1])
        return lax.dynamic_index_in_dim(view, shard, 1, keepdims=False)

    def both(shard):
        return jnp.concatenate([sum_of([part(term, shard) for term in terms]) for terms in groups], axis=-1)

    got = [xor_permute(both(my_fsdp ^ k).astype(BF), sizes, k) for k in range(1, sizes[1])]
    return sum_of([both(my_fsdp)] + got)


def total_over(values, bits, sizes):
    for bit in bits:
        values = values + xor_permute(values, sizes, 1 << bit)
    return values


class Pack:
    def __init__(self, sizes, own, width):
        self.far, self.fsdp, self.own, self.width = sizes[0] // 2, sizes[1], own, width
        self.block = width // sizes[0]
        self.packed = own % 16 == 0
        self.split = self.block % LANES == 0

    def scratch(self):
        shape = (self.far, 2, self.fsdp, self.own, self.width) if self.packed else (self.width, self.width)
        return pltpu.VMEM(shape, BF)

    def fetch(self, sources, index, scratch, sem):
        if not self.packed:
            pltpu.make_async_copy(sources[index], scratch, sem).start()
            return
        core = lax.axis_index("dp") & 1
        rows = pl.ds(index * self.own, self.own)
        for source, side in ((sources[0], core), (sources[1], 1 - core)):
            pltpu.make_async_copy(source.at[:, :, rows, :], scratch.at[:, side], sem).start()

    def ready(self, scratch, sem):
        pltpu.make_async_copy(scratch, scratch, sem).wait()
        return scratch[...].reshape(self.width, self.width)

    def build(self, sources, index, scratch):
        if not self.packed:
            return sources[index][...]
        core = lax.axis_index("dp") & 1
        rows = pl.ds(index * self.own, self.own)
        for source, side in ((sources[0], core), (sources[1], 1 - core)):
            scratch[:, side] = source[:, :, rows, :]
        return scratch[...].reshape(self.width, self.width)

    def grads(self, count):
        if not self.split:
            return [jax.ShapeDtypeStruct((count, self.width, self.width), BF)]
        return [jax.ShapeDtypeStruct((self.far, count, self.block, self.width), BF)] * 2

    def columns(self, ref):
        if not self.split:
            return [ref[...]]
        core = lax.axis_index("dp") & 1
        result = []
        for side in (1 - core, core):
            starts = [pl.multiple_of((2 * i + side) * self.block, self.block) for i in range(self.far)]
            result.append(jnp.concatenate([ref[:, pl.ds(start, self.block)] for start in starts], axis=1))
        return result

    def put(self, flush, refs, twins, index, values):
        for ref, twin, value in zip(refs, twins, values):
            value = value.astype(BF)
            if self.split:
                twin[:, index] = value.reshape(self.far, self.block, self.width)
                flush(twin.at[:, index], ref.at[:, index])
            else:
                twin[index] = value
                flush(twin.at[index], ref.at[index])

    def put_product(self, flush, refs, twins, index, left_ref, right):
        self.put(flush, refs, twins, index, [tm(left, right) for left in self.columns(left_ref)])


class Flush:
    def __init__(self, sems):
        self.sems, self.copies = sems, []

    def __call__(self, source, target):
        copy = pltpu.make_async_copy(source, target, self.sems.at[len(self.copies)])
        copy.start()
        self.copies.append(copy)

    def finish(self):
        for copy in self.copies:
            copy.wait()


COPIES = 16


def kernel_call(kernel, name, operands, sources, near, far, scratch, vmem_mb, work_mb, scalars=(), held=True):
    specs = [pl.BlockSpec(memory_space=pltpu.SMEM)] * len(scalars)
    specs += [pl.BlockSpec(memory_space=pltpu.VMEM)] * len(operands)
    specs += [pl.BlockSpec(memory_space=pltpu.VMEM if held else pl.ANY)] * len(sources)
    out_specs = [pl.BlockSpec(memory_space=pltpu.VMEM)] * len(near) + [pl.BlockSpec(memory_space=pltpu.HBM)] * len(far)
    return pl.pallas_call(
        kernel,
        in_specs=specs,
        out_specs=out_specs,
        out_shape=list(near) + list(far),
        scratch_shapes=[pltpu.VMEM(f.shape, f.dtype) for f in far] + scratch + [pltpu.SemaphoreType.DMA((COPIES,))],
        compiler_params=pltpu.CompilerParams(vmem_limit_bytes=vmem_mb * 2**20),
        cost_estimate=pl.CostEstimate(flops=2**30, bytes_accessed=work_mb * 2**20, transcendentals=2**20),
        name=name,
    )(*scalars, *operands, *sources)


def column_sum(values):
    return jnp.sum(values, axis=0, keepdims=True)


def softmax(scores):
    powers = jnp.exp(scores - jnp.max(scores, axis=-1, keepdims=True))
    return powers * (1.0 / jnp.sum(powers, axis=-1, keepdims=True))


def small_rows(small_ref):
    return lambda i: small_ref[i : i + 1]


def encoder_kernel(pack, n_source, padded, lat_rows, *refs):
    counts, latents, pix = refs[:3]
    sources, rest = refs[3 : 3 + n_source], refs[3 + n_source :]
    (small_o, low_o), outs, twins = rest[:2], rest[2:11], rest[11:20]
    q_o, query_pix_o, probs_o, mixed_pix_o, mixed_o, resid_o, pre_o, act_o, first_o = twins
    scratch, flush = rest[20:25], Flush(rest[25])
    half = pack.width // 2
    latent_in = latents[...].astype(F32)
    hat, _ = norm_parts(latent_in)
    kv = pack.build(sources, 4, scratch[0])
    shape = (small_o.shape[0], half - padded)
    eye = lax.broadcasted_iota(jnp.int32, shape, 0) == lax.broadcasted_iota(jnp.int32, shape, 1)
    small_o[...] = mm_t(eye.astype(F32).astype(BF), kv[:, padded:half])
    small = small_rows(small_o)
    in_low = (hat * small(0) + small(2)).astype(BF)
    query = mm(in_low, pack.build(sources, 2, scratch[1])).astype(BF)
    q_o[...] = query
    flush(twins[0], outs[0])
    query_pix = mm(query, kv[:, :padded]).astype(BF)
    query_pix_o[...] = query_pix
    flush(twins[1], outs[1])
    shape = probs_o.shape
    row, column = lax.broadcasted_iota(jnp.int32, shape, 0), lax.broadcasted_iota(jnp.int32, shape, 1)
    first, end, total = jnp.zeros(shape, jnp.int32), jnp.zeros(shape, jnp.int32), 0
    for image in range(shape[0] // lat_rows):
        here = (row >= image * lat_rows) & (row < (image + 1) * lat_rows)
        first = jnp.where(here, total, first)
        total = total + counts[0, image]
        end = jnp.where(here, total, end)
    scores = mm_t(query_pix, pix[...]) * pack.width**-0.5
    probs = softmax(jnp.where((column >= first) & (column < end), scores, MASKED))
    probs_o[...] = probs
    flush(twins[2], outs[2])
    mixed_pix = mm(probs.astype(BF), pix[...]).astype(BF)
    mixed_pix_o[...] = mixed_pix
    flush(twins[3], outs[3])
    mixed = mm_t(mixed_pix, kv[:, half : half + padded]).astype(BF)
    mixed_o[...] = mixed
    flush(twins[4], outs[4])
    resid = latent_in + mm(mixed, pack.build(sources, 3, scratch[2]))
    resid_o[...] = resid
    flush(twins[5], outs[5])
    hat, _ = norm_parts(resid)
    normed = (hat * small(1) + small(3)).astype(BF)
    pre = mm(normed, pack.build(sources, 0, scratch[3])) + small(4)
    pre_o[...] = pre
    flush(twins[6], outs[6])
    act = gelu(pre).astype(BF)
    act_o[...] = act
    flush(twins[7], outs[7])
    out = resid + mm(act, pack.build(sources, 1, scratch[4])) + small(5)
    first_o[...] = out
    flush(twins[8], outs[8])
    hat, _ = norm_parts(out)
    low_o[...] = (hat * small(6) + small(8)).astype(BF)
    flush.finish()


def attention_kernel(pack, n_source, n_other, lat_rows, *refs):
    own, others, rest = refs[0], refs[1 : 1 + n_other], refs[1 + n_other :]
    sources, rest = rest[:n_source], rest[n_source:]
    mixed_o, outs, twins = rest[0], rest[1:5], rest[5:9]
    every, q_o, k_o, v_o = twins
    scratch, flush = rest[9:12], Flush(rest[12])
    rows = own.shape[0]
    fill_every(every, own, others, pack.fsdp)
    q_o[...] = mm(own[...], pack.build(sources, 0, scratch[0])).astype(BF)
    k_o[...] = mm(every[...], pack.build(sources, 1, scratch[1])).astype(BF).reshape(k_o.shape)
    v_o[...] = mm(every[...], pack.build(sources, 2, scratch[2])).astype(BF).reshape(k_o.shape)
    for twin, out in zip(twins, outs):
        flush(twin, out)

    def some_heads(step, carry):
        places, loaded = [], []
        for head in range(HEADS_AT_ONCE):
            cols = pl.ds(pl.multiple_of((step * HEADS_AT_ONCE + head) * HEAD, HEAD), HEAD)
            for start in range(0, rows, lat_rows):
                part = pl.ds(start, lat_rows)
                places.append((part, cols))
                loaded.append((q_o[part, cols], k_o[:, part, cols].reshape(-1, HEAD), v_o[:, part, cols].reshape(-1, HEAD)))
        scores = [mm_t(q, k) * HEAD**-0.5 for q, k, _ in loaded]
        probs = [softmax(score).astype(BF) for score in scores]
        mixed = [mm(prob, v).astype(BF) for prob, (_, _, v) in zip(probs, loaded)]
        for place, value in zip(places, mixed):
            mixed_o[place] = value
        return carry

    lax.fori_loop(0, HEADS // HEADS_AT_ONCE, some_heads, 0)
    flush.finish()


def attention_back_kernel(pack, n_source, lat_rows, *refs):
    q, k_ref, v_ref, grad, every = refs[:5]
    rest = refs[5:]
    sources, rest = rest[:n_source], rest[n_source:]
    count = len(pack.grads(3))
    slots_o, slot_h, grads_h = rest[0], rest[1], rest[2 : 2 + count]
    slot_o, grads_o, rest = rest[2 + count], rest[3 + count : 3 + 2 * count], rest[3 + 2 * count :]
    scratch, (dq, dk, dv, sems, out_sems) = rest[:3], rest[3:]
    flush = Flush(out_sems)
    for index in range(3):
        pack.fetch(sources, index, scratch[index], sems.at[index])
    rows = q.shape[0]
    scale = HEAD**-0.5

    def some_heads(step, carry):
        places, loaded = [], []
        for head in range(HEADS_AT_ONCE):
            cols = pl.ds(pl.multiple_of((step * HEADS_AT_ONCE + head) * HEAD, HEAD), HEAD)
            for start in range(0, rows, lat_rows):
                part = pl.ds(start, lat_rows)
                places.append((part, cols))
                k, v = k_ref[:, part, cols].reshape(-1, HEAD), v_ref[:, part, cols].reshape(-1, HEAD)
                loaded.append((q[part, cols], k, v, grad[part, cols]))
        scores = [mm_t(query, k) * scale for query, k, _, _ in loaded]
        grad_probs = [mm_t(out_grad, v) for _, _, v, out_grad in loaded]
        results = []
        for score, grad_prob, (query, k, v, out_grad) in zip(scores, grad_probs, loaded):
            prob = softmax(score)
            inner = jnp.sum(prob * grad_prob, axis=-1, keepdims=True)
            grad_score = (prob * (grad_prob - inner) * scale).astype(BF)
            results.append((mm(grad_score, k), tm(grad_score, query), tm(prob.astype(BF), out_grad)))
        for (part, cols), (one, two, three) in zip(places, results):
            dq[part, cols] = one.astype(BF)
            dk[:, part, cols] = two.astype(BF).reshape(pack.fsdp, lat_rows, HEAD)
            dv[:, part, cols] = three.astype(BF).reshape(pack.fsdp, lat_rows, HEAD)
        return carry

    lax.fori_loop(0, HEADS // HEADS_AT_ONCE, some_heads, 0)
    d_q, d_k, d_v = dq[...], dk[...].reshape(-1, pack.width), dv[...].reshape(-1, pack.width)
    w_query = pack.ready(scratch[0], sems.at[0])
    w_key, w_value = pack.ready(scratch[1], sems.at[1]), pack.ready(scratch[2], sems.at[2])
    slot_o[...] = mm_t(d_q, w_query) + mm_t(d_k[:rows], w_key) + mm_t(d_v[:rows], w_value)
    others = mm_t(d_k[rows:], w_key) + mm_t(d_v[rows:], w_value)
    slots_o[...] = others.astype(BF).reshape(slots_o.shape)
    flush(slot_o, slot_h)
    pack.put(flush, grads_h, grads_o, 0, [tm(left, d_q) for left in pack.columns(every.at[pl.ds(0, rows)])])
    columns = pack.columns(every)
    pack.put(flush, grads_h, grads_o, 1, [tm(left, d_k) for left in columns])
    pack.put(flush, grads_h, grads_o, 2, [tm(left, d_v) for left in columns])
    flush.finish()


def latent_kernel(pack, n_source, *refs):
    mixed, first_out, cotangent, small_ref = refs[:4]
    sources, rest = refs[4 : 4 + n_source], refs[4 + n_source :]
    (d_mixed_o, sums_o), rest = rest[:2], rest[2:]
    count = 2 + len(pack.grads(3))
    (result_h, grad_h, *grads_h), (result_o, grad_o, *grads_o) = rest[:count], rest[count : 2 * count]
    scratch, (act_s, normed_s, out_sems) = rest[2 * count : 2 * count + 3], rest[2 * count + 3 :]
    flush = Flush(out_sems)
    small = small_rows(small_ref)
    w_out = pack.build(sources, 0, scratch[0])
    resid = first_out[...] + mm(mixed[...], w_out)
    hat, inverse = norm_parts(resid)
    normed_s[...] = (hat * small(7) + small(9)).astype(BF)
    w_first = pack.build(sources, 1, scratch[1])
    pre = mm(normed_s[...], w_first) + small(10)
    act_s[...] = gelu(pre).astype(BF)
    w_second = pack.build(sources, 2, scratch[2])
    result_o[...] = (resid + mm(act_s[...], w_second) + small(11)).astype(BF)
    flush(result_o, result_h)
    grad_low = cotangent[...]
    grad_out = grad_low.astype(F32)
    pack.put_product(flush, grads_h, grads_o, 1, act_s, grad_low)
    d_pre = mm_t(grad_low, w_second) * gelu_slope(pre)
    d_pre_low = d_pre.astype(BF)
    pack.put_product(flush, grads_h, grads_o, 0, normed_s, d_pre_low)
    d_normed = mm_t(d_pre_low, w_first)
    grad_mid = grad_out + norm_back(hat, inverse, small(7), d_normed)
    grad_o[...] = grad_mid
    flush(grad_o, grad_h)
    grad_low = grad_mid.astype(BF)
    d_mixed_o[...] = mm_t(grad_low, w_out).astype(BF)
    pack.put_product(flush, grads_h, grads_o, 2, mixed, grad_low)
    sums_o[0:1] = column_sum(d_normed * hat)
    sums_o[1:2] = column_sum(d_normed)
    sums_o[2:3] = column_sum(d_pre)
    sums_o[3:4] = column_sum(grad_out)
    flush.finish()


def encoder_back_kernel(pack, n_source, n_other, *refs):
    slot, grad_mid, first_out, resid, pre_ref, act, small_ref = refs[:7]
    others, rest = refs[7 : 7 + n_other], refs[7 + n_other :]
    sources, rest = rest[:n_source], rest[n_source:]
    (grad_o, sums_o), rest = rest[:2], rest[2:]
    count = len(pack.grads(2))
    grads_h, grads_o, rest = rest[:count], rest[count : 2 * count], rest[2 * count :]
    scratch, (normed_s, sems, out_sems) = rest[:2], rest[2:]
    flush = Flush(out_sems)
    for index in range(2):
        pack.fetch(sources, index, scratch[index], sems.at[index])
    small = small_rows(small_ref)
    d_normed = slot[...] + sum(ref[...].astype(F32) for ref in others)
    hat, inverse = norm_parts(first_out[...])
    sums_o[0:1] = column_sum(d_normed * hat)
    sums_o[1:2] = column_sum(d_normed)
    grad_out = grad_mid[...] + norm_back(hat, inverse, small(6), d_normed)
    grad_low = grad_out.astype(BF)
    w_second = pack.ready(scratch[1], sems.at[1])
    d_pre = mm_t(grad_low, w_second) * gelu_slope(pre_ref[...])
    d_pre_low = d_pre.astype(BF)
    d_normed = mm_t(d_pre_low, pack.ready(scratch[0], sems.at[0]))
    hat, inverse = norm_parts(resid[...])
    grad_o[...] = grad_out + norm_back(hat, inverse, small(1), d_normed)
    normed_s[...] = (hat * small(1) + small(3)).astype(BF)
    pack.put_product(flush, grads_h, grads_o, 0, normed_s, d_pre_low)
    pack.put_product(flush, grads_h, grads_o, 1, act, grad_low)
    sums_o[2:3] = column_sum(d_normed * hat)
    sums_o[3:4] = column_sum(d_normed)
    sums_o[4:5] = column_sum(d_pre)
    sums_o[5:6] = column_sum(grad_out)
    flush.finish()


def cross_back_kernel(pack, n_source, padded, share, *refs):
    grad_ref, latents, mixed, mixed_pix, probs_ref, pix, query_pix, enc_q, small_ref, lat_sums, enc_sums, pix_hat = refs[:12]
    sources, rest = refs[12 : 12 + n_source], refs[12 + n_source :]
    (d_pix_o, pix_sums_o), rest = rest[:2], rest[2:]
    count = 1 + len(pack.grads(3))
    (d_latents_h, *grads_h), (d_latents_o, *grads_o) = rest[:count], rest[count : 2 * count]
    scratch, rest = rest[2 * count : 2 * count + 3], rest[2 * count + 3 :]
    d_mixed_s, in_low_s, high_s, low_s, sems, out_sems = rest
    flush = Flush(out_sems)
    for slot, index in enumerate((3, 4, 2)):
        pack.fetch(sources, index, scratch[slot], sems.at[slot])
    small = small_rows(small_ref)
    half = pack.width // 2
    scale = pack.width**-0.5
    grad_enc = grad_ref[...]
    grad_low = grad_enc.astype(BF)
    d_mixed_s[...] = mm_t(grad_low, pack.ready(scratch[0], sems.at[0])).astype(BF)
    kv = pack.ready(scratch[1], sems.at[1])
    mixed_back = mm(d_mixed_s[...], kv[:, half : half + padded]).astype(BF)
    d_probs = mm_t(mixed_back, pix[...])
    probs = probs_ref[...]
    inner = jnp.sum(probs * d_probs, axis=-1, keepdims=True)
    d_scores = (probs * (d_probs - inner) * scale).astype(BF)
    d_pix = tm(query_pix[...], d_scores) + tm(mixed_back, probs.astype(BF))
    kept, used = pix_hat.shape
    d_pix = d_pix[:kept]
    gain_sum = jnp.sum(d_pix * pix_hat[...], axis=-1, keepdims=True)
    bias_sum = jnp.sum(d_pix, axis=-1, keepdims=True)
    lane = lax.broadcasted_iota(jnp.int32, pix_sums_o.shape, 1)
    pix_sums_o[...] = jnp.where(lane == 0, gain_sum, jnp.where(lane == 1, bias_sum, 0.0))
    shard = lax.axis_index("fsdp")
    for target in range(pack.fsdp):
        slot = lax.rem(shard + pack.fsdp - target, pack.fsdp)
        last = min(used, (target + 1) * share)
        piece = d_pix[:, target * share : last]
        if last < (target + 1) * share:
            piece = jnp.concatenate([piece, jnp.zeros((kept, (target + 1) * share - last), F32)], axis=1)
        d_pix_o[slot] = piece
    d_query_pix = mm(d_scores, pix[...]).astype(BF)
    d_enc_q = mm_t(d_query_pix, kv[:, :padded]).astype(BF)
    hat, inverse = norm_parts(latents[...].astype(F32))
    in_low_s[...] = (hat * small(0) + small(2)).astype(BF)
    d_normed = mm_t(d_enc_q, pack.ready(scratch[2], sems.at[2]))
    d_latents_o[...] = grad_enc + norm_back(hat, inverse, small(0), d_normed)
    flush(d_latents_o, d_latents_h)
    order = [column_sum(d_normed * hat), enc_sums[2:3], column_sum(d_normed), enc_sums[3:4], enc_sums[4:5], enc_sums[5:6]]
    order += [enc_sums[0:1], lat_sums[0:1], enc_sums[1:2], lat_sums[1:2], lat_sums[2:3], lat_sums[3:4]]
    sums = jnp.concatenate(order + [jnp.zeros((16 - len(order), pack.width), F32)], axis=0)
    high = sums.astype(BF)
    high_s[...] = high
    low_s[...] = (sums - high.astype(F32)).astype(BF)
    shape = (16, half - padded)
    eye = lax.broadcasted_iota(jnp.int32, shape, 0) == lax.broadcasted_iota(jnp.int32, shape, 1)
    eye = eye.astype(F32).astype(BF)
    blocks = []
    for left, high_c, right, low_c in zip(*(pack.columns(r) for r in (enc_q, high_s, d_mixed_s, low_s))):
        columns = [tm(left, d_query_pix), tm(high_c, eye), tm(right, mixed_pix[...]), tm(low_c, eye)]
        blocks.append(jnp.concatenate(columns, axis=1))
    pack.put(flush, grads_h, grads_o, 0, blocks)
    pack.put_product(flush, grads_h, grads_o, 1, in_low_s, d_enc_q)
    pack.put_product(flush, grads_h, grads_o, 2, mixed, grad_low)
    flush.finish()


def pack_kernel(own, padded, *refs):
    gains_biases, pix_kv, query, out, mlp, packed = refs[:4], *refs[4:]
    half = packed.shape[1] // 2

    def turned(values, columns):
        rows = values.shape[0]
        eye = lax.broadcasted_iota(jnp.int32, (rows, columns), 0) == lax.broadcasted_iota(jnp.int32, (rows, columns), 1)
        return tm(values, eye.astype(F32).astype(BF)).astype(BF)

    packed[0:own], packed[own : 2 * own] = mlp[0], mlp[1]
    packed[2 * own : 3 * own], packed[3 * own : 4 * own] = query[...], out[...]
    small = jnp.concatenate([ref[...].astype(F32) for ref in gains_biases], axis=0).astype(BF)
    last = packed.at[pl.ds(4 * own, own)]
    last[:, 0:padded] = turned(pix_kv[0], padded)
    last[:, padded:half] = turned(small, half - padded)
    last[:, half : half + padded] = turned(pix_kv[1], padded)
    last[:, half + padded :] = jnp.zeros((own, half - padded), BF)


def pad_lanes(values, width):
    return jnp.pad(values, [(0, 0)] * (values.ndim - 1) + [(0, width - values.shape[-1])])


def body(
    sizes,
    latents,
    pixels,
    lengths,
    pix_gain,
    pix_bias,
    pix_kv,
    enc_query,
    enc_out,
    enc_mlp,
    enc_gains,
    enc_biases,
    lat_qkv,
    lat_out,
    lat_mlp,
    lat_gains,
    lat_biases,
    cotangent,
):
    dp_size, fsdp_size = sizes
    devices = dp_size * fsdp_size
    my_fsdp = lax.axis_index("fsdp")
    me = lax.axis_index("dp") * fsdp_size + my_fsdp
    images, lat_rows, width = latents.shape
    rows = images * lat_rows
    pix_rows, features = pixels.shape
    padded = -(-features // LANES) * LANES
    own = width // devices

    _, _, far = bits_of(sizes)
    steps = range(1, len(far))
    half = width // 2

    wide, dma = jax.ShapeDtypeStruct, pltpu.SemaphoreType.DMA
    enc_pack = pl.pallas_call(
        partial(pack_kernel, own, padded), out_shape=wide((5 * own, width), BF), name="pack"
    )(enc_gains, enc_biases, lat_gains, lat_biases, pix_kv, enc_query, enc_out, enc_mlp)
    enc_parts = gather_fsdp(enc_pack, sizes)
    gain_f = pix_gain.astype(F32)
    pix_hat, pix_inverse = norm_parts(pixels.astype(F32))
    pix_low = pad_lanes((pix_hat * gain_f + pix_bias.astype(F32)).astype(BF), padded)[:USED]
    pix_hat_t = jnp.pad(pix_hat[:USED].T, ((0, -features % 8), (0, 0)))
    enc_parts, pix_low, pix_hat, pix_hat_t, pix_inverse, lat_qkv = seal(
        enc_parts, pix_low, pix_hat, pix_hat_t, pix_inverse, lat_qkv
    )

    enc_groups = far_step([v[None] for v in halves_of(order_fsdp(enc_parts, sizes, me))], 0, sizes, me)
    qkv_parts = gather_fsdp(lat_qkv.reshape(3 * own, width), sizes)
    enc_groups, qkv_parts, lat_out, lat_mlp = seal(enc_groups, qkv_parts, lat_out, lat_mlp)

    for place in steps:
        enc_groups = far_step(enc_groups, place, sizes, me)
    other_parts = gather_fsdp(jnp.concatenate([lat_out, lat_mlp[0], lat_mlp[1]], axis=0), sizes)
    qkv_groups = [v[None] for v in halves_of(order_fsdp(qkv_parts, sizes, me))]
    enc_groups, qkv_groups, other_parts = seal(enc_groups, qkv_groups, other_parts)

    enc_whole = jnp.concatenate(enc_groups, axis=-1)
    enc_got = core_swap(enc_whole, sizes)
    qkv_groups = far_step(qkv_groups, 0, sizes, me)
    other_groups = [v[None] for v in halves_of(order_fsdp(other_parts, sizes, me))]
    enc_whole, enc_got, qkv_groups, other_groups = seal(enc_whole, enc_got, qkv_groups, other_groups)

    pack = Pack(sizes, own, width)
    for place in steps:
        qkv_groups = far_step(qkv_groups, place, sizes, me)
    enc_sources = sources_of(enc_whole, enc_got, 5, sizes, me)
    n_gain, n_bias = enc_gains.shape[0], enc_biases.shape[0]

    small_all, lat_low, enc_q, query_pix, probs, mixed_pix, enc_mixed, enc_resid, enc_pre, enc_act, first_out = kernel_call(
        partial(encoder_kernel, pack, len(enc_sources), padded, lat_rows),
        "encoder",
        [latents.reshape(rows, width), pix_low],
        enc_sources,
        [wide((16, width), F32), wide((rows, width), BF)],
        [wide((rows, width), BF), wide((rows, padded), BF), wide((rows, USED), F32), wide((rows, padded), BF)]
        + [wide((rows, width), BF), wide((rows, width), F32), wide((rows, width), F32), wide((rows, width), BF)]
        + [wide((rows, width), F32)],
        [pack.scratch()] * 5,
        48,
        36,
        scalars=[lengths],
    )
    qkv_whole = jnp.concatenate(qkv_groups, axis=-1)
    lat_low, qkv_whole, other_groups = seal(lat_low, qkv_whole, other_groups)

    in_two = fsdp_size == 4
    if in_two:
        shards = exchange_one(lat_low)
    else:
        shards = [slot_shift(lat_low, fsdp_size, j) for j in range(1, fsdp_size)]
    qkv_got = core_swap(qkv_whole, sizes)
    other_groups = far_step(other_groups, 0, sizes, me)
    lat_low, shards, qkv_got, other_groups = seal(lat_low, shards, qkv_got, other_groups)
    if in_two:
        shards = exchange_two(list(shards), my_fsdp)
    for place in steps:
        other_groups = far_step(other_groups, place, sizes, me)
    other_whole = jnp.concatenate(other_groups, axis=-1)
    shards, other_whole = seal(list(shards), other_whole)
    other_got = core_swap(other_whole, sizes)
    qkv_sources = sources_of(qkv_whole, qkv_got, 3, sizes, me)
    every = wide((fsdp_size, rows, width), BF)
    lat_mixed, lat_every, lat_q, lat_k, lat_v = kernel_call(
        partial(attention_kernel, pack, len(qkv_sources), len(shards), lat_rows),
        "attention",
        [lat_low] + shards,
        qkv_sources,
        [wide((rows, width), BF)],
        [wide((fsdp_size * rows, width), BF), wide((rows, width), BF), every, every],
        [pack.scratch()] * 3,
        40,
        40,
    )
    other_sources = sources_of(other_whole, other_got, 3, sizes, me)
    d_mixed, lat_sums, result, grad_mid, *grads_m = kernel_call(
        partial(latent_kernel, pack, len(other_sources)),
        "latent",
        [lat_mixed, first_out, cotangent.reshape(rows, width), small_all],
        other_sources,
        [wide((rows, width), BF), wide((8, width), F32)],
        [wide((rows, width), BF), wide((rows, width), F32)] + pack.grads(3),
        [pack.scratch()] * 3 + [pltpu.VMEM((rows, width), BF)] * 2,
        44,
        36,
    )

    grads_m = core_terms(grads_m, sizes, me)
    slots, slot, *grads_q = kernel_call(
        partial(attention_back_kernel, pack, len(qkv_sources), lat_rows),
        "attention_back",
        [lat_q, lat_k, lat_v, d_mixed, lat_every],
        qkv_sources,
        [wide((fsdp_size - 1, rows, width), BF)],
        [wide((rows, width), F32)] + pack.grads(3),
        [pack.scratch()] * 3
        + [pltpu.VMEM((rows, width), BF)]
        + [pltpu.VMEM(every.shape, BF)] * 2
        + [dma((3,))],
        48,
        72,
        held=False,
    )
    slots, grads_q = seal(slots, grads_q)

    slots = [slots[j] for j in range(fsdp_size - 1)]
    if in_two:
        received = collect_one(slots, my_fsdp)
    else:
        received = [slot_shift(slots[j - 1], fsdp_size, fsdp_size - j) for j in range(1, fsdp_size)]
    grads_m = far_pair(grads_m, 0, sizes, me)
    slots, received, grads_m = seal(slots, received, grads_m)
    if in_two:
        received = collect_two(slots, received, my_fsdp)
    for place in steps:
        grads_m = far_pair(grads_m, place, sizes, me)
    grads_q = core_terms(grads_q, sizes, me)
    received, grads_m, grads_q = seal(received, grads_m, grads_q)
    received = list(received)
    grad_enc, enc_sums, *grads_e = kernel_call(
        partial(encoder_back_kernel, pack, len(enc_sources), len(received)),
        "encoder_back",
        [slot, grad_mid, first_out, enc_resid, enc_pre, enc_act, small_all] + received,
        enc_sources,
        [wide((rows, width), F32), wide((8, width), F32)],
        pack.grads(2),
        [pack.scratch()] * 2 + [pltpu.VMEM((rows, width), BF), dma((2,))],
        40,
        36,
        held=False,
    )
    l_other_grads = finish_sum(grads_m, sizes, my_fsdp)
    grads_q = far_pair(grads_q, 0, sizes, me)
    share = pix_rows // fsdp_size
    kept = pix_hat_t.shape[0]
    pieces, d_pix_sums, d_latents, *grads_f = kernel_call(
        partial(cross_back_kernel, pack, len(enc_sources), padded, share),
        "cross_back",
        [grad_enc, latents.reshape(rows, width), enc_mixed, mixed_pix, probs, pix_low, query_pix, enc_q, small_all]
        + [lat_sums, enc_sums, pix_hat_t],
        enc_sources,
        [wide((fsdp_size, kept, share), F32), wide((kept, LANES), F32)],
        [wide((rows, width), F32)] + pack.grads(3),
        [pack.scratch()] * 3
        + [pltpu.VMEM((rows, width), BF)] * 2
        + [pltpu.VMEM((16, width), BF)] * 2
        + [dma((3,))],
        48,
        50,
        held=False,
    )
    pieces, grads_e, grads_f, d_pix_sums, grads_q, l_other_grads = seal(
        pieces, grads_e, grads_f, d_pix_sums, grads_q, l_other_grads
    )

    low_bits, core, _ = bits_of(sizes)
    grads_e, grads_f = core_terms(grads_e, sizes, me), core_terms(grads_f, sizes, me)
    for place in steps:
        grads_q = far_pair(grads_q, place, sizes, me)
    d_pix_sums = total_over(d_pix_sums[:features, :2].T, low_bits, sizes)
    pieces, grads_e, grads_f, grads_q, d_pix_sums = seal(pieces, grads_e, grads_f, grads_q, d_pix_sums)

    grads_e = [[jnp.concatenate(both, axis=1) for both in zip(e, f)] for e, f in zip(grads_e, grads_f)]
    d_pix_own = pieces[0]
    for j in range(1, fsdp_size):
        d_pix_own = d_pix_own + slot_shift(pieces[j].astype(BF), fsdp_size, fsdp_size - j).astype(F32)
    grads_e = far_pair(grads_e, 0, sizes, me)
    d_pix_own, grads_e, grads_q, d_pix_sums = seal(d_pix_own, grads_e, grads_q, d_pix_sums)

    l_qkv_grads = finish_sum(grads_q, sizes, my_fsdp)
    for place in steps:
        grads_e = far_pair(grads_e, place, sizes, me)
    l_qkv_grads, grads_e, d_pix_sums = seal(l_qkv_grads, grads_e, d_pix_sums)
    d_pix_sums = total_over(d_pix_sums, [core] + far, sizes)
    enc_grads = finish_sum(grads_e, sizes, my_fsdp)
    hat_own = lax.dynamic_slice_in_dim(pix_hat, my_fsdp * share, share, 0)
    inverse_own = lax.dynamic_slice_in_dim(pix_inverse, my_fsdp * share, share, 0)
    d_pixels = norm_back(hat_own, inverse_own, gain_f, d_pix_own[:features].T)
    kv_own = enc_grads[2]
    d_pix_kv = jnp.stack([kv_own[:, :features].T, kv_own[:, width // 2 : width // 2 + features].T])
    start = width // 2 + padded
    n_small = 2 * (n_gain + n_bias)
    small_own = (kv_own[:, padded : padded + n_small] + kv_own[:, start : start + n_small]).T
    return (
        result.reshape(latents.shape),
        d_latents.reshape(latents.shape),
        d_pixels,
        d_pix_sums[0],
        d_pix_sums[1],
        d_pix_kv,
        enc_grads[3],
        enc_grads[4],
        enc_grads[:2],
        small_own[:n_gain],
        small_own[n_gain : n_gain + n_bias],
        l_qkv_grads,
        l_other_grads[2],
        l_other_grads[:2],
        small_own[n_gain + n_bias : 2 * n_gain + n_bias],
        small_own[2 * n_gain + n_bias :],
    )


def solution(mesh):
    split, rows, columns = P("dp", "fsdp", None), P(AXES, None), P(None, AXES)
    middle = P(None, AXES, None)
    weights = (P(None, None, AXES), rows, rows, middle, columns, columns, middle, rows, middle, columns, columns)
    return jax.shard_map(
        partial(body, (mesh.shape["dp"], mesh.shape["fsdp"])),
        mesh=mesh,
        in_specs=(split, P("dp", None), P("dp", None), P(), P()) + weights + (split,),
        out_specs=(split, split, rows, P(), P()) + weights,
        check_vma=False,
    )
```

```python
from functools import partial

import jax
import jax.numpy as jnp
from jax import lax
from jax.experimental.layout import Layout, with_layout_constraint
from jax.experimental import pallas as pl
from jax.experimental.pallas import tpu as pltpu
from jax.sharding import PartitionSpec as P

HEADS = 8
HEAD = 128
USED = 1792
EPSILON = 1e-05
MASKED = -1e30
AXES = ("dp", "fsdp")
LANES = 128
HEADS_AT_ONCE = 2
BF = jnp.bfloat16
F32 = jnp.float32


def dot(left, right, dims):
    return lax.dot_general(left, right, ((dims[0], dims[1]), ((), ())), preferred_element_type=F32)


def mm(left, right):
    return dot(left, right, ((left.ndim - 1,), (0,)))


def mm_t(left, right):
    return dot(left, right, ((left.ndim - 1,), (1,)))


def tm(left, right):
    return dot(left, right, ((0,), (0,)))


def norm_parts(values):
    average = jnp.mean(values, axis=-1, keepdims=True)
    centered = values - average
    variance = jnp.mean(centered * centered, axis=-1, keepdims=True)
    inverse = lax.rsqrt(variance + EPSILON)
    return centered * inverse, inverse


def norm_back(hat, inverse, gains, grad_out):
    grad_hat = grad_out * gains
    first = jnp.mean(grad_hat, axis=-1, keepdims=True)
    second = jnp.mean(grad_hat * hat, axis=-1, keepdims=True)
    return inverse * (grad_hat - first - hat * second)


def gelu(values):
    return 0.5 * values * (1.0 + lax.erf(values * (0.5**0.5)))


def gelu_slope(values):
    density = jnp.exp(-0.5 * values * values) * ((0.5 / jnp.pi) ** 0.5)
    return 0.5 * (1.0 + lax.erf(values * (0.5**0.5))) + values * density


def xor_permute(values, sizes, step):
    dp_size, fsdp_size = sizes
    total = dp_size * fsdp_size
    return lax.ppermute(values, AXES, [(i, i ^ step) for i in range(total)])


def seal(*values):
    return lax.optimization_barrier(values)


def bits_of(sizes):
    low = sizes[1].bit_length() - 1
    every = list(range((sizes[0] * sizes[1]).bit_length() - 1))
    return every[:low], every[low], every[low + 1 :]


def gather_fsdp(values, sizes):
    return [values] + [xor_permute(values, sizes, k) for k in range(1, sizes[1])]


def slot_shift(values, size, j):
    return lax.ppermute(values, "fsdp", [(i, (i + j) % size) for i in range(size)])


def hop(values, pairs):
    return lax.ppermute(values, "fsdp", pairs)


UP, DOWN = [(0, 1), (1, 2), (2, 3)], [(3, 2), (2, 1), (1, 0)]


def exchange_one(values):
    return [hop(values, UP), hop(values, DOWN)]


def exchange_two(first, shard):
    up, down = first
    far = jnp.where(shard == 1, up, down)
    return first + [hop(up, UP[1:]), hop(down, DOWN[1:]), hop(far, [(1, 3), (2, 0)])]


def gather_slots(values, size):
    return [values] + [slot_shift(values, size, j) for j in range(1, size)]


def slots_of(parts, shard):
    up, down, up_two, down_two, far = parts
    return [jnp.where(shard == 0, far, up), jnp.where(shard <= 1, down_two, up_two), jnp.where(shard == 3, far, down)]


def order_slots(slots, shard):
    size = len(slots)
    parts = [slots[-t % size] for t in range(size)]
    for bit in range(size.bit_length() - 1):
        mine = ((shard >> bit) & 1) == 1
        parts = [jnp.where(mine, parts[(t - (1 << bit)) % size], parts[t]) for t in range(size)]
    return jnp.stack(parts)


def fill_every(every, own, parts, n_shard):
    rows = own.shape[0]
    every[0:rows] = own[...]
    if len(parts) == n_shard - 1:
        slots = [part[...] for part in parts]
    else:
        shard = lax.axis_index("fsdp")
        slots = slots_of([part[...] for part in parts], shard)
    for j, slot in enumerate(slots):
        every[(j + 1) * rows : (j + 2) * rows] = slot


def collect_one(slots, shard):
    far = jnp.where(shard == 0, slots[0], slots[2])
    return [hop(slots[1], UP[:2]), hop(slots[1], DOWN[:2]), hop(far, [(0, 2), (3, 1)])]


def collect_two(slots, first, shard):
    up, down, far = [part.astype(F32) for part in first]
    up = slots[2].astype(F32) + up + jnp.where(shard == 2, far, 0.0)
    down = slots[0].astype(F32) + down + jnp.where(shard == 1, far, 0.0)
    return [hop(up.astype(BF), UP), hop(down.astype(BF), DOWN)]


def order_fsdp(parts, sizes, me):
    low, _, _ = bits_of(sizes)
    for bit in low:
        mine = ((me >> bit) & 1) == 1
        parts = [jnp.where(mine, parts[k ^ (1 << bit)], parts[k]) for k in range(len(parts))]
    return jnp.stack(parts)


def merge(own, got, bit, above, me):
    mine = ((me >> bit) & 1) == 1
    view = (2**above, -1) + own.shape[1:]
    own, got = own.reshape(view), got.reshape(view)
    both = jnp.stack([jnp.where(mine, got, own), jnp.where(mine, own, got)], axis=1)
    return both.reshape((-1,) + own.shape[2:])


def far_step(groups, place, sizes, me):
    _, _, far = bits_of(sizes)
    result = []
    for values, order in zip(groups, (far, far[::-1])):
        bit, held = order[place], order[:place]
        got = xor_permute(values, sizes, 1 << bit)
        result.append(merge(values, got, bit, sum(1 for other in held if other > bit), me))
    return result


def core_swap(whole, sizes):
    _, core, _ = bits_of(sizes)
    return xor_permute(whole, sizes, 1 << core)


def sources_of(whole, got, count, sizes, me):
    own = whole.shape[2] // count
    if own % 16 == 0:
        return [whole, got]
    _, core, _ = bits_of(sizes)
    mine = ((me >> core) & 1) == 1
    both = jnp.stack([jnp.where(mine, got, whole), jnp.where(mine, whole, got)], axis=1)
    parts = [both[:, :, :, i * own : (i + 1) * own] for i in range(count)]
    return [part.reshape(-1, part.shape[-1]) for part in parts]


def halves_of(values):
    half = values.shape[-1] // 2
    return [values[..., :half], values[..., half:]]


def core_terms(grads, sizes, me):
    _, core, _ = bits_of(sizes)
    if len(grads) == 1:
        mine = (me >> core) & 1
        count, width = grads[0].shape[0], grads[0].shape[-1]
        view = jnp.swapaxes(grads[0].reshape(count, sizes[0] // 2, 2, -1, width), 0, 1)
        send = lax.dynamic_index_in_dim(view, 1 - mine, 2, keepdims=False)
        keep = lax.dynamic_index_in_dim(view, mine, 2, keepdims=False)
    else:
        send, keep = grads
    got = xor_permute(send, sizes, 1 << core)
    return [list(terms) for terms in zip(halves_of(keep), halves_of(got))]


def sum_of(terms):
    total = terms[0].astype(F32)
    for term in terms[1:]:
        total = total + term.astype(F32)
    return total


def far_terms(terms, bit, held, sizes, me):
    above = sum(1 for other in held if other > bit)
    mine = (me >> bit) & 1

    def half(term, side):
        view = term.reshape((2**above, 2, -1) + term.shape[1:])
        part = lax.dynamic_index_in_dim(view, side, 1, keepdims=False)
        return part.reshape((-1,) + term.shape[1:])

    send = sum_of([half(term, 1 - mine) for term in terms]).astype(BF)
    return [half(term, mine) for term in terms] + [xor_permute(send, sizes, 1 << bit)]


def far_pair(groups, place, sizes, me):
    _, _, far = bits_of(sizes)
    result = []
    for terms, order in zip(groups, (far, far[::-1])):
        held = [bit for bit in far if bit not in order[:place]]
        result.append(far_terms(terms, order[place], held, sizes, me))
    return result


def fsdp_part(groups, shard, sizes):
    def part(term):
        view = term[0].reshape(term.shape[1], sizes[1], -1, term.shape[-1])
        return lax.dynamic_index_in_dim(view, shard, 1, keepdims=False)

    return jnp.concatenate([sum_of([part(term) for term in terms]) for terms in groups], axis=-1)


def fsdp_swap(groups, sizes, my_fsdp):
    return [xor_permute(fsdp_part(groups, my_fsdp ^ k, sizes).astype(BF), sizes, k) for k in range(1, sizes[1])]


def fsdp_sum(own, got):
    return sum_of([own] + list(got))


def total_over(values, bits, sizes):
    for bit in bits:
        values = values + xor_permute(values, sizes, 1 << bit)
    return values


class Pack:
    def __init__(self, sizes, own, width):
        self.far, self.fsdp, self.own, self.width = sizes[0] // 2, sizes[1], own, width
        self.block = width // sizes[0]
        self.packed = own % 16 == 0
        self.split = self.block % LANES == 0

    def scratch(self):
        shape = (self.far, 2, self.fsdp, self.own, self.width) if self.packed else (self.width, self.width)
        return pltpu.VMEM(shape, BF)

    def fetch(self, sources, index, scratch, sem):
        if not self.packed:
            pltpu.make_async_copy(sources[index], scratch, sem).start()
            return
        core = lax.axis_index("dp") & 1
        rows = pl.ds(index * self.own, self.own)
        for source, side in ((sources[0], core), (sources[1], 1 - core)):
            pltpu.make_async_copy(source.at[:, :, rows, :], scratch.at[:, side], sem).start()

    def ready(self, scratch, sem):
        pltpu.make_async_copy(scratch, scratch, sem).wait()
        return scratch[...].reshape(self.width, self.width)

    def build(self, sources, index, scratch):
        if not self.packed:
            return sources[index][...]
        core = lax.axis_index("dp") & 1
        rows = pl.ds(index * self.own, self.own)
        for source, side in ((sources[0], core), (sources[1], 1 - core)):
            scratch[:, side] = source[:, :, rows, :]
        return scratch[...].reshape(self.width, self.width)

    def grads(self, count):
        if not self.split:
            return [jax.ShapeDtypeStruct((count, self.width, self.width), BF)]
        return [jax.ShapeDtypeStruct((self.far, count, self.block, self.width), BF)] * 2

    def columns(self, ref):
        if not self.split:
            return [ref[...]]
        core = lax.axis_index("dp") & 1
        result = []
        for side in (1 - core, core):
            starts = [pl.multiple_of((2 * i + side) * self.block, self.block) for i in range(self.far)]
            result.append(jnp.concatenate([ref[:, pl.ds(start, self.block)] for start in starts], axis=1))
        return result

    def put(self, refs, index, values):
        for ref, value in zip(refs, values):
            value = value.astype(BF)
            if self.split:
                ref[:, index] = value.reshape(self.far, self.block, self.width)
            else:
                ref[index] = value

    def put_product(self, refs, index, left_ref, right):
        self.put(refs, index, [tm(left, right) for left in self.columns(left_ref)])


def kernel_call(kernel, name, operands, sources, outs, scratch, vmem_mb, work_mb, scalars=(), held=True):
    specs = [pl.BlockSpec(memory_space=pltpu.SMEM)] * len(scalars)
    specs += [pl.BlockSpec(memory_space=pltpu.VMEM)] * len(operands)
    specs += [pl.BlockSpec(memory_space=pltpu.VMEM if held else pl.ANY)] * len(sources)
    return pl.pallas_call(
        kernel,
        in_specs=specs,
        out_specs=[pl.BlockSpec(memory_space=pltpu.VMEM)] * len(outs),
        out_shape=list(outs),
        scratch_shapes=scratch,
        compiler_params=pltpu.CompilerParams(vmem_limit_bytes=vmem_mb * 2**20),
        cost_estimate=pl.CostEstimate(flops=2**30, bytes_accessed=work_mb * 2**20, transcendentals=2**20),
        name=name,
    )(*scalars, *operands, *sources)


def column_sum(values):
    return jnp.sum(values, axis=0, keepdims=True)


def softmax(scores):
    powers = jnp.exp(scores - jnp.max(scores, axis=-1, keepdims=True))
    return powers * (1.0 / jnp.sum(powers, axis=-1, keepdims=True))


def small_rows(small_ref):
    return lambda i: small_ref[i : i + 1]


def encoder_kernel(pack, n_source, padded, lat_rows, *refs):
    counts, latents, pix = refs[:3]
    sources, rest = refs[3 : 3 + n_source], refs[3 + n_source :]
    small_o, low_o, q_o, query_pix_o, probs_o, mixed_pix_o, mixed_o, resid_o, pre_o, act_o, first_o = rest[:11]
    scratch = rest[11:16]
    half = pack.width // 2
    latent_in = latents[...].astype(F32)
    hat, _ = norm_parts(latent_in)
    kv = pack.build(sources, 4, scratch[0])
    shape = (small_o.shape[0], half - padded)
    eye = lax.broadcasted_iota(jnp.int32, shape, 0) == lax.broadcasted_iota(jnp.int32, shape, 1)
    small_o[...] = mm_t(eye.astype(F32).astype(BF), kv[:, padded:half])
    small = small_rows(small_o)
    in_low = (hat * small(0) + small(2)).astype(BF)
    query = mm(in_low, pack.build(sources, 2, scratch[1])).astype(BF)
    q_o[...] = query
    query_pix = mm(query, kv[:, :padded]).astype(BF)
    query_pix_o[...] = query_pix
    shape = probs_o.shape
    row, column = lax.broadcasted_iota(jnp.int32, shape, 0), lax.broadcasted_iota(jnp.int32, shape, 1)
    first, end, total = jnp.zeros(shape, jnp.int32), jnp.zeros(shape, jnp.int32), 0
    for image in range(shape[0] // lat_rows):
        here = (row >= image * lat_rows) & (row < (image + 1) * lat_rows)
        first = jnp.where(here, total, first)
        total = total + counts[0, image]
        end = jnp.where(here, total, end)
    scores = mm_t(query_pix, pix[...]) * pack.width**-0.5
    probs = softmax(jnp.where((column >= first) & (column < end), scores, MASKED))
    probs_o[...] = probs
    mixed_pix = mm(probs.astype(BF), pix[...]).astype(BF)
    mixed_pix_o[...] = mixed_pix
    mixed = mm_t(mixed_pix, kv[:, half : half + padded]).astype(BF)
    mixed_o[...] = mixed
    resid = latent_in + mm(mixed, pack.build(sources, 3, scratch[2]))
    resid_o[...] = resid
    hat, _ = norm_parts(resid)
    normed = (hat * small(1) + small(3)).astype(BF)
    pre = mm(normed, pack.build(sources, 0, scratch[3])) + small(4)
    pre_o[...] = pre
    act = gelu(pre).astype(BF)
    act_o[...] = act
    out = resid + mm(act, pack.build(sources, 1, scratch[4])) + small(5)
    first_o[...] = out
    hat, _ = norm_parts(out)
    low_o[...] = (hat * small(6) + small(8)).astype(BF)


def attention_kernel(pack, n_source, n_other, lat_rows, *refs):
    own, others, rest = refs[0], refs[1 : 1 + n_other], refs[1 + n_other :]
    sources, rest = rest[:n_source], rest[n_source:]
    mixed_o, every, q_o, k_o, v_o = rest[:5]
    scratch = rest[5:8]
    rows = own.shape[0]
    fill_every(every, own, others, pack.fsdp)
    q_o[...] = mm(own[...], pack.build(sources, 0, scratch[0])).astype(BF)
    k_o[...] = mm(every[...], pack.build(sources, 1, scratch[1])).astype(BF).reshape(k_o.shape)
    v_o[...] = mm(every[...], pack.build(sources, 2, scratch[2])).astype(BF).reshape(k_o.shape)

    def some_heads(step, carry):
        places, loaded = [], []
        for head in range(HEADS_AT_ONCE):
            cols = pl.ds(pl.multiple_of((step * HEADS_AT_ONCE + head) * HEAD, HEAD), HEAD)
            for start in range(0, rows, lat_rows):
                part = pl.ds(start, lat_rows)
                places.append((part, cols))
                loaded.append((q_o[part, cols], k_o[:, part, cols].reshape(-1, HEAD), v_o[:, part, cols].reshape(-1, HEAD)))
        scores = [mm_t(q, k) * HEAD**-0.5 for q, k, _ in loaded]
        probs = [softmax(score).astype(BF) for score in scores]
        mixed = [mm(prob, v).astype(BF) for prob, (_, _, v) in zip(probs, loaded)]
        for place, value in zip(places, mixed):
            mixed_o[place] = value
        return carry

    lax.fori_loop(0, HEADS // HEADS_AT_ONCE, some_heads, 0)


def attention_back_kernel(pack, n_source, lat_rows, *refs):
    q, k_ref, v_ref, grad, every = refs[:5]
    rest = refs[5:]
    sources, rest = rest[:n_source], rest[n_source:]
    outs = 2 + len(pack.grads(3))
    slots_o, slot_o, *grads_o = rest[:outs]
    scratch, (dq, dk, dv, sems) = rest[outs : outs + 3], rest[outs + 3 :]
    for index in range(3):
        pack.fetch(sources, index, scratch[index], sems.at[index])
    rows = q.shape[0]
    scale = HEAD**-0.5

    def some_heads(step, carry):
        places, loaded = [], []
        for head in range(HEADS_AT_ONCE):
            cols = pl.ds(pl.multiple_of((step * HEADS_AT_ONCE + head) * HEAD, HEAD), HEAD)
            for start in range(0, rows, lat_rows):
                part = pl.ds(start, lat_rows)
                places.append((part, cols))
                k, v = k_ref[:, part, cols].reshape(-1, HEAD), v_ref[:, part, cols].reshape(-1, HEAD)
                loaded.append((q[part, cols], k, v, grad[part, cols]))
        scores = [mm_t(query, k) * scale for query, k, _, _ in loaded]
        grad_probs = [mm_t(out_grad, v) for _, _, v, out_grad in loaded]
        results = []
        for score, grad_prob, (query, k, v, out_grad) in zip(scores, grad_probs, loaded):
            prob = softmax(score)
            inner = jnp.sum(prob * grad_prob, axis=-1, keepdims=True)
            grad_score = (prob * (grad_prob - inner) * scale).astype(BF)
            results.append((mm(grad_score, k), tm(grad_score, query), tm(prob.astype(BF), out_grad)))
        for (part, cols), (one, two, three) in zip(places, results):
            dq[part, cols] = one.astype(BF)
            dk[:, part, cols] = two.astype(BF).reshape(pack.fsdp, lat_rows, HEAD)
            dv[:, part, cols] = three.astype(BF).reshape(pack.fsdp, lat_rows, HEAD)
        return carry

    lax.fori_loop(0, HEADS // HEADS_AT_ONCE, some_heads, 0)
    d_q, d_k, d_v = dq[...], dk[...].reshape(-1, pack.width), dv[...].reshape(-1, pack.width)
    w_query = pack.ready(scratch[0], sems.at[0])
    w_key, w_value = pack.ready(scratch[1], sems.at[1]), pack.ready(scratch[2], sems.at[2])
    slot_o[...] = mm_t(d_q, w_query) + mm_t(d_k[:rows], w_key) + mm_t(d_v[:rows], w_value)
    others = mm_t(d_k[rows:], w_key) + mm_t(d_v[rows:], w_value)
    slots_o[...] = others.astype(BF).reshape(slots_o.shape)
    pack.put(grads_o, 0, [tm(left, d_q) for left in pack.columns(every.at[pl.ds(0, rows)])])
    columns = pack.columns(every)
    pack.put(grads_o, 1, [tm(left, d_k) for left in columns])
    pack.put(grads_o, 2, [tm(left, d_v) for left in columns])


def latent_kernel(pack, n_source, *refs):
    mixed, first_out, cotangent, small_ref = refs[:4]
    sources, rest = refs[4 : 4 + n_source], refs[4 + n_source :]
    outs = 4 + len(pack.grads(3))
    d_mixed_o, sums_o, result_o, grad_o, *grads_o = rest[:outs]
    scratch, (act_s, normed_s) = rest[outs : outs + 3], rest[outs + 3 :]
    small = small_rows(small_ref)
    w_out = pack.build(sources, 0, scratch[0])
    resid = first_out[...] + mm(mixed[...], w_out)
    hat, inverse = norm_parts(resid)
    normed_s[...] = (hat * small(7) + small(9)).astype(BF)
    w_first = pack.build(sources, 1, scratch[1])
    pre = mm(normed_s[...], w_first) + small(10)
    act_s[...] = gelu(pre).astype(BF)
    w_second = pack.build(sources, 2, scratch[2])
    result_o[...] = (resid + mm(act_s[...], w_second) + small(11)).astype(BF)
    grad_low = cotangent[...]
    grad_out = grad_low.astype(F32)
    pack.put_product(grads_o, 1, act_s, grad_low)
    d_pre = mm_t(grad_low, w_second) * gelu_slope(pre)
    d_pre_low = d_pre.astype(BF)
    pack.put_product(grads_o, 0, normed_s, d_pre_low)
    d_normed = mm_t(d_pre_low, w_first)
    grad_mid = grad_out + norm_back(hat, inverse, small(7), d_normed)
    grad_o[...] = grad_mid
    grad_low = grad_mid.astype(BF)
    d_mixed_o[...] = mm_t(grad_low, w_out).astype(BF)
    pack.put_product(grads_o, 2, mixed, grad_low)
    sums_o[0:1] = column_sum(d_normed * hat)
    sums_o[1:2] = column_sum(d_normed)
    sums_o[2:3] = column_sum(d_pre)
    sums_o[3:4] = column_sum(grad_out)


def encoder_back_kernel(pack, n_source, n_other, *refs):
    slot, grad_mid, first_out, resid, pre_ref, act, small_ref = refs[:7]
    others, rest = refs[7 : 7 + n_other], refs[7 + n_other :]
    sources, rest = rest[:n_source], rest[n_source:]
    outs = 2 + len(pack.grads(2))
    grad_o, sums_o, *grads_o = rest[:outs]
    scratch, (normed_s, sems) = rest[outs : outs + 2], rest[outs + 2 :]
    for index in range(2):
        pack.fetch(sources, index, scratch[index], sems.at[index])
    small = small_rows(small_ref)
    d_normed = slot[...] + sum(ref[...].astype(F32) for ref in others)
    hat, inverse = norm_parts(first_out[...])
    sums_o[0:1] = column_sum(d_normed * hat)
    sums_o[1:2] = column_sum(d_normed)
    grad_out = grad_mid[...] + norm_back(hat, inverse, small(6), d_normed)
    grad_low = grad_out.astype(BF)
    w_second = pack.ready(scratch[1], sems.at[1])
    d_pre = mm_t(grad_low, w_second) * gelu_slope(pre_ref[...])
    d_pre_low = d_pre.astype(BF)
    d_normed = mm_t(d_pre_low, pack.ready(scratch[0], sems.at[0]))
    hat, inverse = norm_parts(resid[...])
    grad_o[...] = grad_out + norm_back(hat, inverse, small(1), d_normed)
    normed_s[...] = (hat * small(1) + small(3)).astype(BF)
    pack.put_product(grads_o, 0, normed_s, d_pre_low)
    pack.put_product(grads_o, 1, act, grad_low)
    sums_o[2:3] = column_sum(d_normed * hat)
    sums_o[3:4] = column_sum(d_normed)
    sums_o[4:5] = column_sum(d_pre)
    sums_o[5:6] = column_sum(grad_out)


def cross_back_kernel(pack, n_source, padded, share, *refs):
    grad_ref, latents, mixed, mixed_pix, probs_ref, pix, query_pix, enc_q, small_ref, lat_sums, enc_sums, pix_hat = refs[:12]
    sources, rest = refs[12 : 12 + n_source], refs[12 + n_source :]
    outs = 3 + len(pack.grads(3))
    d_pix_o, pix_sums_o, d_latents_o, *grads_o = rest[:outs]
    scratch, (d_mixed_s, in_low_s, high_s, low_s, sems) = rest[outs : outs + 3], rest[outs + 3 :]
    for slot, index in enumerate((3, 4, 2)):
        pack.fetch(sources, index, scratch[slot], sems.at[slot])
    small = small_rows(small_ref)
    half = pack.width // 2
    scale = pack.width**-0.5
    grad_enc = grad_ref[...]
    grad_low = grad_enc.astype(BF)
    d_mixed_s[...] = mm_t(grad_low, pack.ready(scratch[0], sems.at[0])).astype(BF)
    kv = pack.ready(scratch[1], sems.at[1])
    mixed_back = mm(d_mixed_s[...], kv[:, half : half + padded]).astype(BF)
    d_probs = mm_t(mixed_back, pix[...])
    probs = probs_ref[...]
    inner = jnp.sum(probs * d_probs, axis=-1, keepdims=True)
    d_scores = (probs * (d_probs - inner) * scale).astype(BF)
    d_pix = tm(query_pix[...], d_scores) + tm(mixed_back, probs.astype(BF))
    kept, used = pix_hat.shape
    d_pix = d_pix[:kept]
    gain_sum = jnp.sum(d_pix * pix_hat[...], axis=-1, keepdims=True)
    bias_sum = jnp.sum(d_pix, axis=-1, keepdims=True)
    lane = lax.broadcasted_iota(jnp.int32, pix_sums_o.shape, 1)
    pix_sums_o[...] = jnp.where(lane == 0, gain_sum, jnp.where(lane == 1, bias_sum, 0.0))
    shard = lax.axis_index("fsdp")
    for target in range(pack.fsdp):
        slot = lax.rem(shard + pack.fsdp - target, pack.fsdp)
        last = min(used, (target + 1) * share)
        piece = d_pix[:, target * share : last]
        if last < (target + 1) * share:
            piece = jnp.concatenate([piece, jnp.zeros((kept, (target + 1) * share - last), F32)], axis=1)
        d_pix_o[slot] = piece
    d_query_pix = mm(d_scores, pix[...]).astype(BF)
    d_enc_q = mm_t(d_query_pix, kv[:, :padded]).astype(BF)
    hat, inverse = norm_parts(latents[...].astype(F32))
    in_low_s[...] = (hat * small(0) + small(2)).astype(BF)
    d_normed = mm_t(d_enc_q, pack.ready(scratch[2], sems.at[2]))
    d_latents_o[...] = grad_enc + norm_back(hat, inverse, small(0), d_normed)
    order = [column_sum(d_normed * hat), enc_sums[2:3], column_sum(d_normed), enc_sums[3:4], enc_sums[4:5], enc_sums[5:6]]
    order += [enc_sums[0:1], lat_sums[0:1], enc_sums[1:2], lat_sums[1:2], lat_sums[2:3], lat_sums[3:4]]
    sums = jnp.concatenate(order + [jnp.zeros((16 - len(order), pack.width), F32)], axis=0)
    high = sums.astype(BF)
    high_s[...] = high
    low_s[...] = (sums - high.astype(F32)).astype(BF)
    shape = (16, half - padded)
    eye = lax.broadcasted_iota(jnp.int32, shape, 0) == lax.broadcasted_iota(jnp.int32, shape, 1)
    eye = eye.astype(F32).astype(BF)
    blocks = []
    for left, high_c, right, low_c in zip(*(pack.columns(r) for r in (enc_q, high_s, d_mixed_s, low_s))):
        columns = [tm(left, d_query_pix), tm(high_c, eye), tm(right, mixed_pix[...]), tm(low_c, eye)]
        blocks.append(jnp.concatenate(columns, axis=1))
    pack.put(grads_o, 0, blocks)
    pack.put_product(grads_o, 1, in_low_s, d_enc_q)
    pack.put_product(grads_o, 2, mixed, grad_low)


def pack_kernel(own, padded, *refs):
    gains_biases, pix_kv, query, out, mlp, packed = refs[:4], *refs[4:]
    half = packed.shape[1] // 2

    def turned(values, columns):
        rows = values.shape[0]
        eye = lax.broadcasted_iota(jnp.int32, (rows, columns), 0) == lax.broadcasted_iota(jnp.int32, (rows, columns), 1)
        return tm(values, eye.astype(F32).astype(BF)).astype(BF)

    packed[0:own], packed[own : 2 * own] = mlp[0], mlp[1]
    packed[2 * own : 3 * own], packed[3 * own : 4 * own] = query[...], out[...]
    small = jnp.concatenate([ref[...].astype(F32) for ref in gains_biases], axis=0).astype(BF)
    last = packed.at[pl.ds(4 * own, own)]
    last[:, 0:padded] = turned(pix_kv[0], padded)
    last[:, padded:half] = turned(small, half - padded)
    last[:, half : half + padded] = turned(pix_kv[1], padded)
    last[:, half + padded :] = jnp.zeros((own, half - padded), BF)


def pad_lanes(values, width):
    return jnp.pad(values, [(0, 0)] * (values.ndim - 1) + [(0, width - values.shape[-1])])


def body(
    sizes,
    latents,
    pixels,
    lengths,
    pix_gain,
    pix_bias,
    pix_kv,
    enc_query,
    enc_out,
    enc_mlp,
    enc_gains,
    enc_biases,
    lat_qkv,
    lat_out,
    lat_mlp,
    lat_gains,
    lat_biases,
    cotangent,
):
    dp_size, fsdp_size = sizes
    devices = dp_size * fsdp_size
    my_fsdp = lax.axis_index("fsdp")
    me = lax.axis_index("dp") * fsdp_size + my_fsdp
    images, lat_rows, width = latents.shape
    rows = images * lat_rows
    pix_rows, features = pixels.shape
    padded = -(-features // LANES) * LANES
    own = width // devices

    _, _, far = bits_of(sizes)
    steps = range(1, len(far))
    half = width // 2

    wide, dma = jax.ShapeDtypeStruct, pltpu.SemaphoreType.DMA
    enc_pack = pl.pallas_call(
        partial(pack_kernel, own, padded), out_shape=wide((5 * own, width), BF), name="pack"
    )(enc_gains, enc_biases, lat_gains, lat_biases, pix_kv, enc_query, enc_out, enc_mlp)
    in_two = fsdp_size == 4
    enc_parts = exchange_one(enc_pack) if in_two else gather_slots(enc_pack, fsdp_size)
    gain_f = pix_gain.astype(F32)
    pix_hat, pix_inverse = norm_parts(pixels.astype(F32))
    pix_low = pad_lanes((pix_hat * gain_f + pix_bias.astype(F32)).astype(BF), padded)[:USED]
    pix_hat_t = jnp.pad(pix_hat[:USED].T, ((0, -features % 8), (0, 0)))
    if in_two:
        enc_parts, enc_pack = seal(enc_parts, enc_pack)
        enc_parts = [enc_pack] + slots_of(exchange_two(list(enc_parts), my_fsdp), my_fsdp)
    enc_parts, pix_low, pix_hat, pix_hat_t, pix_inverse, lat_qkv = seal(
        enc_parts, pix_low, pix_hat, pix_hat_t, pix_inverse, lat_qkv
    )

    enc_groups = far_step([v[None] for v in halves_of(order_slots(list(enc_parts), my_fsdp))], 0, sizes, me)
    lat_pack = jnp.concatenate([lat_qkv.reshape(3 * own, width), lat_out, lat_mlp[0], lat_mlp[1]], axis=0)
    lat_one = slot_shift(lat_pack, fsdp_size, 1)
    enc_groups, lat_pack, lat_one = seal(enc_groups, lat_pack, lat_one)

    for place in steps:
        enc_groups = far_step(enc_groups, place, sizes, me)
    lat_parts = [lat_pack, lat_one] + [slot_shift(lat_pack, fsdp_size, j) for j in range(2, fsdp_size)]
    enc_groups, lat_parts = seal(enc_groups, lat_parts)
    lat_whole = order_slots(list(lat_parts), my_fsdp)[None]
    qkv_groups = halves_of(lat_whole[:, :, : 3 * own])

    enc_whole = jnp.concatenate(enc_groups, axis=-1)
    enc_got = core_swap(enc_whole, sizes)
    qkv_groups = far_step(qkv_groups, 0, sizes, me)
    other_groups = halves_of(lat_whole[:, :, 3 * own :])
    enc_whole, enc_got, qkv_groups, other_groups = seal(enc_whole, enc_got, qkv_groups, other_groups)

    pack = Pack(sizes, own, width)
    for place in steps:
        qkv_groups = far_step(qkv_groups, place, sizes, me)
    enc_sources = sources_of(enc_whole, enc_got, 5, sizes, me)
    n_gain, n_bias = enc_gains.shape[0], enc_biases.shape[0]

    small_all, lat_low, enc_q, query_pix, probs, mixed_pix, enc_mixed, enc_resid, enc_pre, enc_act, first_out = kernel_call(
        partial(encoder_kernel, pack, len(enc_sources), padded, lat_rows),
        "encoder",
        [latents.reshape(rows, width), pix_low],
        enc_sources,
        [wide((16, width), F32), wide((rows, width), BF)]
        + [wide((rows, width), BF), wide((rows, padded), BF), wide((rows, USED), F32), wide((rows, padded), BF)]
        + [wide((rows, width), BF), wide((rows, width), F32), wide((rows, width), F32), wide((rows, width), BF)]
        + [wide((rows, width), F32)],
        [pack.scratch()] * 5,
        48,
        36,
        scalars=[lengths],
    )
    qkv_whole = jnp.concatenate(qkv_groups, axis=-1)
    lat_low, qkv_whole, other_groups = seal(lat_low, qkv_whole, other_groups)

    if in_two:
        shards = exchange_one(lat_low)
    else:
        shards = [slot_shift(lat_low, fsdp_size, j) for j in range(1, fsdp_size)]
    qkv_got = core_swap(qkv_whole, sizes)
    other_groups = far_step(other_groups, 0, sizes, me)
    lat_low, shards, qkv_got, other_groups = seal(lat_low, shards, qkv_got, other_groups)
    if in_two:
        shards = exchange_two(list(shards), my_fsdp)
    for place in steps:
        other_groups = far_step(other_groups, place, sizes, me)
    other_whole = jnp.concatenate(other_groups, axis=-1)
    shards, other_whole = seal(list(shards), other_whole)
    other_got = core_swap(other_whole, sizes)
    qkv_sources = sources_of(qkv_whole, qkv_got, 3, sizes, me)
    every = wide((fsdp_size, rows, width), BF)
    lat_mixed, lat_every, lat_q, lat_k, lat_v = kernel_call(
        partial(attention_kernel, pack, len(qkv_sources), len(shards), lat_rows),
        "attention",
        [lat_low] + shards,
        qkv_sources,
        [wide((rows, width), BF)]
        + [wide((fsdp_size * rows, width), BF), wide((rows, width), BF), every, every],
        [pack.scratch()] * 3,
        40,
        40,
    )
    other_sources = sources_of(other_whole, other_got, 3, sizes, me)
    d_mixed, lat_sums, result, grad_mid, *grads_m = kernel_call(
        partial(latent_kernel, pack, len(other_sources)),
        "latent",
        [lat_mixed, first_out, cotangent.reshape(rows, width), small_all],
        other_sources,
        [wide((rows, width), BF), wide((8, width), F32)]
        + [wide((rows, width), BF), wide((rows, width), F32)] + pack.grads(3),
        [pack.scratch()] * 3 + [pltpu.VMEM((rows, width), BF)] * 2,
        44,
        36,
    )

    grads_m = core_terms(grads_m, sizes, me)
    slots, slot, *grads_q = kernel_call(
        partial(attention_back_kernel, pack, len(qkv_sources), lat_rows),
        "attention_back",
        [lat_q, lat_k, lat_v, d_mixed, lat_every],
        qkv_sources,
        [wide((fsdp_size - 1, rows, width), BF)]
        + [wide((rows, width), F32)] + pack.grads(3),
        [pack.scratch()] * 3
        + [pltpu.VMEM((rows, width), BF)]
        + [pltpu.VMEM(every.shape, BF)] * 2
        + [dma((3,))],
        48,
        72,
        held=False,
    )
    slots, grads_q = seal(slots, grads_q)

    slots = [slots[j] for j in range(fsdp_size - 1)]
    if in_two:
        received = collect_one(slots, my_fsdp)
    else:
        received = [slot_shift(slots[j - 1], fsdp_size, fsdp_size - j) for j in range(1, fsdp_size)]
    grads_m = far_pair(grads_m, 0, sizes, me)
    slots, received, grads_m = seal(slots, received, grads_m)
    if in_two:
        received = collect_two(slots, received, my_fsdp)
    for place in steps:
        grads_m = far_pair(grads_m, place, sizes, me)
    grads_q = core_terms(grads_q, sizes, me)
    received, grads_m, grads_q = seal(received, grads_m, grads_q)
    received = list(received)
    grad_enc, enc_sums, *grads_e = kernel_call(
        partial(encoder_back_kernel, pack, len(enc_sources), len(received)),
        "encoder_back",
        [slot, grad_mid, first_out, enc_resid, enc_pre, enc_act, small_all] + received,
        enc_sources,
        [wide((rows, width), F32), wide((8, width), F32)] + pack.grads(2),
        [pack.scratch()] * 2 + [pltpu.VMEM((rows, width), BF), dma((2,))],
        40,
        36,
        held=False,
    )
    grad_enc, grads_m, grads_q = seal(grad_enc, grads_m, grads_q)
    l_other_own, l_other_got = fsdp_part(grads_m, my_fsdp, sizes), fsdp_swap(grads_m, sizes, my_fsdp)
    grads_q = far_pair(grads_q, 0, sizes, me)
    share = pix_rows // fsdp_size
    kept = pix_hat_t.shape[0]
    pieces, d_pix_sums, d_latents, *grads_f = kernel_call(
        partial(cross_back_kernel, pack, len(enc_sources), padded, share),
        "cross_back",
        [grad_enc, latents.reshape(rows, width), enc_mixed, mixed_pix, probs, pix_low, query_pix, enc_q, small_all]
        + [lat_sums, enc_sums, pix_hat_t],
        enc_sources,
        [wide((fsdp_size, kept, share), F32), wide((kept, LANES), F32)]
        + [wide((rows, width), F32)] + pack.grads(3),
        [pack.scratch()] * 3
        + [pltpu.VMEM((rows, width), BF)] * 2
        + [pltpu.VMEM((16, width), BF)] * 2
        + [dma((3,))],
        48,
        50,
        held=False,
    )
    pieces, grads_e, grads_f, d_pix_sums, grads_q, l_other_got = seal(
        pieces, grads_e, grads_f, d_pix_sums, grads_q, l_other_got
    )

    low_bits, core, _ = bits_of(sizes)
    grads_e, grads_f = core_terms(grads_e, sizes, me), core_terms(grads_f, sizes, me)
    for place in steps:
        grads_q = far_pair(grads_q, place, sizes, me)
    d_pix_sums = total_over(d_pix_sums[:features, :2].T, low_bits[::-1][:1], sizes)
    pieces, grads_e, grads_f, grads_q, d_pix_sums = seal(pieces, grads_e, grads_f, grads_q, d_pix_sums)

    grads_e = [[jnp.concatenate(both, axis=1) for both in zip(e, f)] for e, f in zip(grads_e, grads_f)]
    d_pix_own = pieces[0]
    for j in range(1, fsdp_size):
        d_pix_own = d_pix_own + slot_shift(pieces[j].astype(BF), fsdp_size, fsdp_size - j).astype(F32)
    grads_e = far_pair(grads_e, 0, sizes, me)
    d_pix_own, grads_e, grads_q, d_pix_sums = seal(d_pix_own, grads_e, grads_q, d_pix_sums)

    l_qkv_own, l_qkv_got = fsdp_part(grads_q, my_fsdp, sizes), fsdp_swap(grads_q, sizes, my_fsdp)
    for place in steps:
        grads_e = far_pair(grads_e, place, sizes, me)
    l_qkv_got, l_other_got, grads_e, d_pix_sums = seal(l_qkv_got, l_other_got, grads_e, d_pix_sums)
    d_pix_sums = total_over(d_pix_sums, [core] + far + low_bits[::-1][1:], sizes)
    enc_got = fsdp_swap(grads_e, sizes, my_fsdp)
    l_other_grads = fsdp_sum(l_other_own, l_other_got)
    l_qkv_grads = fsdp_sum(l_qkv_own, l_qkv_got)
    enc_grads = fsdp_sum(fsdp_part(grads_e, my_fsdp, sizes), enc_got)
    hat_own = lax.dynamic_slice_in_dim(pix_hat, my_fsdp * share, share, 0)
    inverse_own = lax.dynamic_slice_in_dim(pix_inverse, my_fsdp * share, share, 0)
    d_pixels = norm_back(hat_own, inverse_own, gain_f, d_pix_own[:features].T)
    kv_own = enc_grads[2]
    d_pix_kv = jnp.stack([kv_own[:, :features].T, kv_own[:, width // 2 : width // 2 + features].T])
    start = width // 2 + padded
    n_small = 2 * (n_gain + n_bias)
    small_own = (kv_own[:, padded : padded + n_small] + kv_own[:, start : start + n_small]).T
    return (
        result.reshape(latents.shape),
        d_latents.reshape(latents.shape),
        d_pixels,
        d_pix_sums[0],
        d_pix_sums[1],
        d_pix_kv,
        enc_grads[3],
        enc_grads[4],
        enc_grads[:2],
        small_own[:n_gain],
        small_own[n_gain : n_gain + n_bias],
        l_qkv_grads,
        l_other_grads[2],
        l_other_grads[:2],
        small_own[n_gain + n_bias : 2 * n_gain + n_bias],
        small_own[2 * n_gain + n_bias :],
    )


def solution(mesh):
    split, rows, columns = P("dp", "fsdp", None), P(AXES, None), P(None, AXES)
    middle = P(None, AXES, None)
    weights = (P(None, None, AXES), rows, rows, middle, columns, columns, middle, rows, middle, columns, columns)
    return jax.shard_map(
        partial(body, (mesh.shape["dp"], mesh.shape["fsdp"])),
        mesh=mesh,
        in_specs=(split, P("dp", None), P("dp", None), P(), P()) + weights + (split,),
        out_specs=(split, split, rows, P(), P()) + weights,
        check_vma=False,
    )
```

```python
from functools import partial

import jax
import jax.numpy as jnp
from jax import lax
from jax.experimental.layout import Layout, with_layout_constraint
from jax.experimental import pallas as pl
from jax.experimental.pallas import tpu as pltpu
from jax.sharding import PartitionSpec as P

HEADS = 8
HEAD = 128
USED = 1792
EPSILON = 1e-05
MASKED = -1e30
AXES = ("dp", "fsdp")
LANES = 128
HEADS_AT_ONCE = 8
BF = jnp.bfloat16
F32 = jnp.float32


def dot(left, right, dims):
    return lax.dot_general(left, right, ((dims[0], dims[1]), ((), ())), preferred_element_type=F32)


def mm(left, right):
    return dot(left, right, ((left.ndim - 1,), (0,)))


def mm_t(left, right):
    return dot(left, right, ((left.ndim - 1,), (1,)))


def tm(left, right):
    return dot(left, right, ((0,), (0,)))


def norm_parts(values):
    average = jnp.mean(values, axis=-1, keepdims=True)
    centered = values - average
    variance = jnp.mean(centered * centered, axis=-1, keepdims=True)
    inverse = lax.rsqrt(variance + EPSILON)
    return centered * inverse, inverse


def norm_back(hat, inverse, gains, grad_out):
    grad_hat = grad_out * gains
    first = jnp.mean(grad_hat, axis=-1, keepdims=True)
    second = jnp.mean(grad_hat * hat, axis=-1, keepdims=True)
    return inverse * (grad_hat - first - hat * second)


def gelu(values):
    return 0.5 * values * (1.0 + lax.erf(values * (0.5**0.5)))


def gelu_slope(values):
    density = jnp.exp(-0.5 * values * values) * ((0.5 / jnp.pi) ** 0.5)
    return 0.5 * (1.0 + lax.erf(values * (0.5**0.5))) + values * density


def xor_permute(values, sizes, step):
    dp_size, fsdp_size = sizes
    total = dp_size * fsdp_size
    return lax.ppermute(values, AXES, [(i, i ^ step) for i in range(total)])


def seal(*values):
    return lax.optimization_barrier(values)


def bits_of(sizes):
    low = sizes[1].bit_length() - 1
    every = list(range((sizes[0] * sizes[1]).bit_length() - 1))
    return every[:low], every[low], every[low + 1 :]


def gather_fsdp(values, sizes):
    return [values] + [xor_permute(values, sizes, k) for k in range(1, sizes[1])]


def slot_shift(values, size, j):
    return lax.ppermute(values, "fsdp", [(i, (i + j) % size) for i in range(size)])


def hop(values, pairs):
    return lax.ppermute(values, "fsdp", pairs)


UP, DOWN = [(0, 1), (1, 2), (2, 3)], [(3, 2), (2, 1), (1, 0)]


def exchange_one(values):
    return [hop(values, UP), hop(values, DOWN)]


def exchange_two(first, shard):
    up, down = first
    far = jnp.where(shard == 1, up, down)
    return first + [hop(up, UP[1:]), hop(down, DOWN[1:]), hop(far, [(1, 3), (2, 0)])]


def gather_slots(values, size):
    return [values] + [slot_shift(values, size, j) for j in range(1, size)]


def slots_of(parts, shard):
    up, down, up_two, down_two, far = parts
    return [jnp.where(shard == 0, far, up), jnp.where(shard <= 1, down_two, up_two), jnp.where(shard == 3, far, down)]


def order_slots(slots, shard):
    size = len(slots)
    parts = [slots[-t % size] for t in range(size)]
    for bit in range(size.bit_length() - 1):
        mine = ((shard >> bit) & 1) == 1
        parts = [jnp.where(mine, parts[(t - (1 << bit)) % size], parts[t]) for t in range(size)]
    return jnp.stack(parts)


def fill_every(every, own, parts, n_shard):
    rows = own.shape[0]
    every[0:rows] = own[...]
    if len(parts) == n_shard - 1:
        slots = [part[...] for part in parts]
    else:
        shard = lax.axis_index("fsdp")
        slots = slots_of([part[...] for part in parts], shard)
    for j, slot in enumerate(slots):
        every[(j + 1) * rows : (j + 2) * rows] = slot


def collect_one(slots, shard):
    far = jnp.where(shard == 0, slots[0], slots[2])
    return [hop(slots[1], UP[:2]), hop(slots[1], DOWN[:2]), hop(far, [(0, 2), (3, 1)])]


def collect_two(slots, first, shard):
    up, down, far = [part.astype(F32) for part in first]
    up = slots[2].astype(F32) + up + jnp.where(shard == 2, far, 0.0)
    down = slots[0].astype(F32) + down + jnp.where(shard == 1, far, 0.0)
    return [hop(up.astype(BF), UP), hop(down.astype(BF), DOWN)]


def order_fsdp(parts, sizes, me):
    low, _, _ = bits_of(sizes)
    for bit in low:
        mine = ((me >> bit) & 1) == 1
        parts = [jnp.where(mine, parts[k ^ (1 << bit)], parts[k]) for k in range(len(parts))]
    return jnp.stack(parts)


def merge(own, got, bit, above, me):
    mine = ((me >> bit) & 1) == 1
    view = (2**above, -1) + own.shape[1:]
    own, got = own.reshape(view), got.reshape(view)
    both = jnp.stack([jnp.where(mine, got, own), jnp.where(mine, own, got)], axis=1)
    return both.reshape((-1,) + own.shape[2:])


def far_step(groups, place, sizes, me):
    _, _, far = bits_of(sizes)
    result = []
    for values, order in zip(groups, (far, far[::-1])):
        bit, held = order[place], order[:place]
        got = xor_permute(values, sizes, 1 << bit)
        result.append(merge(values, got, bit, sum(1 for other in held if other > bit), me))
    return result


def core_swap(whole, sizes):
    _, core, _ = bits_of(sizes)
    return xor_permute(whole, sizes, 1 << core)


def sources_of(whole, got, count, sizes, me):
    own = whole.shape[2] // count
    if own % 16 == 0:
        return [whole, got]
    _, core, _ = bits_of(sizes)
    mine = ((me >> core) & 1) == 1
    both = jnp.stack([jnp.where(mine, got, whole), jnp.where(mine, whole, got)], axis=1)
    parts = [both[:, :, :, i * own : (i + 1) * own] for i in range(count)]
    return [part.reshape(-1, part.shape[-1]) for part in parts]


def halves_of(values):
    half = values.shape[-1] // 2
    return [values[..., :half], values[..., half:]]


def core_terms(grads, sizes, me):
    _, core, _ = bits_of(sizes)
    if len(grads) == 1:
        mine = (me >> core) & 1
        count, width = grads[0].shape[0], grads[0].shape[-1]
        view = jnp.swapaxes(grads[0].reshape(count, sizes[0] // 2, 2, -1, width), 0, 1)
        send = lax.dynamic_index_in_dim(view, 1 - mine, 2, keepdims=False)
        keep = lax.dynamic_index_in_dim(view, mine, 2, keepdims=False)
    else:
        send, keep = grads
    got = xor_permute(send, sizes, 1 << core)
    return [list(terms) for terms in zip(halves_of(keep), halves_of(got))]


def sum_of(terms):
    total = terms[0].astype(F32)
    for term in terms[1:]:
        total = total + term.astype(F32)
    return total


def far_terms(terms, bit, held, sizes, me):
    above = sum(1 for other in held if other > bit)
    mine = (me >> bit) & 1

    def half(term, side):
        view = term.reshape((2**above, 2, -1) + term.shape[1:])
        part = lax.dynamic_index_in_dim(view, side, 1, keepdims=False)
        return part.reshape((-1,) + term.shape[1:])

    send = sum_of([half(term, 1 - mine) for term in terms]).astype(BF)
    return [half(term, mine) for term in terms] + [xor_permute(send, sizes, 1 << bit)]


def far_pair(groups, place, sizes, me):
    _, _, far = bits_of(sizes)
    result = []
    for terms, order in zip(groups, (far, far[::-1])):
        held = [bit for bit in far if bit not in order[:place]]
        result.append(far_terms(terms, order[place], held, sizes, me))
    return result


def fsdp_part(groups, shard, sizes):
    def part(term):
        view = term[0].reshape(term.shape[1], sizes[1], -1, term.shape[-1])
        return lax.dynamic_index_in_dim(view, shard, 1, keepdims=False)

    return jnp.concatenate([sum_of([part(term) for term in terms]) for terms in groups], axis=-1)


def fsdp_swap(groups, sizes, my_fsdp):
    return [xor_permute(fsdp_part(groups, my_fsdp ^ k, sizes).astype(BF), sizes, k) for k in range(1, sizes[1])]


def fsdp_sum(own, got):
    return sum_of([own] + list(got))


def total_over(values, bits, sizes):
    for bit in bits:
        values = values + xor_permute(values, sizes, 1 << bit)
    return values


class Pack:
    def __init__(self, sizes, own, width):
        self.far, self.fsdp, self.own, self.width = sizes[0] // 2, sizes[1], own, width
        self.block = width // sizes[0]
        self.packed = own % 16 == 0
        self.split = self.block % LANES == 0

    def scratch(self):
        shape = (self.far, 2, self.fsdp, self.own, self.width) if self.packed else (self.width, self.width)
        return pltpu.VMEM(shape, BF)

    def fetch(self, sources, index, scratch, sem):
        if not self.packed:
            pltpu.make_async_copy(sources[index], scratch, sem).start()
            return
        core = lax.axis_index("dp") & 1
        rows = pl.ds(index * self.own, self.own)
        for source, side in ((sources[0], core), (sources[1], 1 - core)):
            pltpu.make_async_copy(source.at[:, :, rows, :], scratch.at[:, side], sem).start()

    def ready(self, scratch, sem):
        pltpu.make_async_copy(scratch, scratch, sem).wait()
        return scratch[...].reshape(self.width, self.width)

    def build(self, sources, index, scratch):
        if not self.packed:
            return sources[index][...]
        core = lax.axis_index("dp") & 1
        rows = pl.ds(index * self.own, self.own)
        for source, side in ((sources[0], core), (sources[1], 1 - core)):
            scratch[:, side] = source[:, :, rows, :]
        return scratch[...].reshape(self.width, self.width)

    def grads(self, count):
        if not self.split:
            return [jax.ShapeDtypeStruct((count, self.width, self.width), BF)]
        return [jax.ShapeDtypeStruct((self.far, count, self.block, self.width), BF)] * 2

    def columns(self, ref):
        if not self.split:
            return [ref[...]]
        core = lax.axis_index("dp") & 1
        result = []
        for side in (1 - core, core):
            starts = [pl.multiple_of((2 * i + side) * self.block, self.block) for i in range(self.far)]
            result.append(jnp.concatenate([ref[:, pl.ds(start, self.block)] for start in starts], axis=1))
        return result

    def put(self, refs, index, values):
        for ref, value in zip(refs, values):
            value = value.astype(BF)
            if self.split:
                ref[:, index] = value.reshape(self.far, self.block, self.width)
            else:
                ref[index] = value

    def put_product(self, refs, index, left_ref, right):
        self.put(refs, index, [tm(left, right) for left in self.columns(left_ref)])


def kernel_call(kernel, name, operands, sources, outs, scratch, vmem_mb, work_mb, scalars=(), held=True):
    specs = [pl.BlockSpec(memory_space=pltpu.SMEM)] * len(scalars)
    specs += [pl.BlockSpec(memory_space=pltpu.VMEM)] * len(operands)
    specs += [pl.BlockSpec(memory_space=pltpu.VMEM if held else pl.ANY)] * len(sources)
    return pl.pallas_call(
        kernel,
        in_specs=specs,
        out_specs=[pl.BlockSpec(memory_space=pltpu.VMEM)] * len(outs),
        out_shape=list(outs),
        scratch_shapes=scratch,
        compiler_params=pltpu.CompilerParams(vmem_limit_bytes=vmem_mb * 2**20),
        cost_estimate=pl.CostEstimate(flops=2**30, bytes_accessed=work_mb * 2**20, transcendentals=2**20),
        name=name,
    )(*scalars, *operands, *sources)


def column_sum(values):
    return jnp.sum(values, axis=0, keepdims=True)


def softmax(scores):
    powers = jnp.exp(scores - jnp.max(scores, axis=-1, keepdims=True))
    return powers * (1.0 / jnp.sum(powers, axis=-1, keepdims=True))


def small_rows(small_ref):
    return lambda i: small_ref[i : i + 1]


def encoder_kernel(pack, n_source, padded, lat_rows, *refs):
    counts, latents, pix = refs[:3]
    sources, rest = refs[3 : 3 + n_source], refs[3 + n_source :]
    small_o, low_o, q_o, query_pix_o, probs_o, mixed_pix_o, mixed_o, resid_o, pre_o, act_o, first_o = rest[:11]
    scratch = rest[11:16]
    half = pack.width // 2
    latent_in = latents[...].astype(F32)
    hat, _ = norm_parts(latent_in)
    kv = pack.build(sources, 4, scratch[0])
    shape = (small_o.shape[0], half - padded)
    eye = lax.broadcasted_iota(jnp.int32, shape, 0) == lax.broadcasted_iota(jnp.int32, shape, 1)
    small_o[...] = mm_t(eye.astype(F32).astype(BF), kv[:, padded:half])
    small = small_rows(small_o)
    in_low = (hat * small(0) + small(2)).astype(BF)
    query = mm(in_low, pack.build(sources, 2, scratch[1])).astype(BF)
    q_o[...] = query
    query_pix = mm(query, kv[:, :padded]).astype(BF)
    query_pix_o[...] = query_pix
    shape = probs_o.shape
    row, column = lax.broadcasted_iota(jnp.int32, shape, 0), lax.broadcasted_iota(jnp.int32, shape, 1)
    first, end, total = jnp.zeros(shape, jnp.int32), jnp.zeros(shape, jnp.int32), 0
    for image in range(shape[0] // lat_rows):
        here = (row >= image * lat_rows) & (row < (image + 1) * lat_rows)
        first = jnp.where(here, total, first)
        total = total + counts[0, image]
        end = jnp.where(here, total, end)
    scores = mm_t(query_pix, pix[...]) * pack.width**-0.5
    probs = softmax(jnp.where((column >= first) & (column < end), scores, MASKED))
    probs_o[...] = probs
    mixed_pix = mm(probs.astype(BF), pix[...]).astype(BF)
    mixed_pix_o[...] = mixed_pix
    mixed = mm_t(mixed_pix, kv[:, half : half + padded]).astype(BF)
    mixed_o[...] = mixed
    resid = latent_in + mm(mixed, pack.build(sources, 3, scratch[2]))
    resid_o[...] = resid
    hat, _ = norm_parts(resid)
    normed = (hat * small(1) + small(3)).astype(BF)
    pre = mm(normed, pack.build(sources, 0, scratch[3])) + small(4)
    pre_o[...] = pre
    act = gelu(pre).astype(BF)
    act_o[...] = act
    out = resid + mm(act, pack.build(sources, 1, scratch[4])) + small(5)
    first_o[...] = out
    hat, _ = norm_parts(out)
    low_o[...] = (hat * small(6) + small(8)).astype(BF)


def attention_kernel(pack, n_source, n_other, lat_rows, *refs):
    own, others, rest = refs[0], refs[1 : 1 + n_other], refs[1 + n_other :]
    sources, rest = rest[:n_source], rest[n_source:]
    mixed_o, every, q_o, k_o, v_o = rest[:5]
    scratch, sems = rest[5:8], rest[8]
    for index in range(3):
        pack.fetch(sources, index, scratch[index], sems.at[index])
    rows = own.shape[0]
    fill_every(every, own, others, pack.fsdp)
    q_o[...] = mm(own[...], pack.ready(scratch[0], sems.at[0])).astype(BF)
    k_o[...] = mm(every[...], pack.ready(scratch[1], sems.at[1])).astype(BF).reshape(k_o.shape)
    v_o[...] = mm(every[...], pack.ready(scratch[2], sems.at[2])).astype(BF).reshape(k_o.shape)

    def some_heads(step, carry):
        places, loaded = [], []
        for head in range(HEADS_AT_ONCE):
            cols = pl.ds(pl.multiple_of((step * HEADS_AT_ONCE + head) * HEAD, HEAD), HEAD)
            for start in range(0, rows, lat_rows):
                part = pl.ds(start, lat_rows)
                places.append((part, cols))
                loaded.append((q_o[part, cols], k_o[:, part, cols].reshape(-1, HEAD), v_o[:, part, cols].reshape(-1, HEAD)))
        scores = [mm_t(q, k) * HEAD**-0.5 for q, k, _ in loaded]
        probs = [softmax(score).astype(BF) for score in scores]
        mixed = [mm(prob, v).astype(BF) for prob, (_, _, v) in zip(probs, loaded)]
        for place, value in zip(places, mixed):
            mixed_o[place] = value
        return carry

    lax.fori_loop(0, HEADS // HEADS_AT_ONCE, some_heads, 0)


def attention_back_kernel(pack, n_source, lat_rows, *refs):
    q, k_ref, v_ref, grad, every = refs[:5]
    rest = refs[5:]
    sources, rest = rest[:n_source], rest[n_source:]
    outs = 2 + len(pack.grads(3))
    slots_o, slot_o, *grads_o = rest[:outs]
    scratch, (dq, dk, dv, sems) = rest[outs : outs + 3], rest[outs + 3 :]
    for index in range(3):
        pack.fetch(sources, index, scratch[index], sems.at[index])
    rows = q.shape[0]
    scale = HEAD**-0.5

    def some_heads(step, carry):
        places, loaded = [], []
        for head in range(HEADS_AT_ONCE):
            cols = pl.ds(pl.multiple_of((step * HEADS_AT_ONCE + head) * HEAD, HEAD), HEAD)
            for start in range(0, rows, lat_rows):
                part = pl.ds(start, lat_rows)
                places.append((part, cols))
                k, v = k_ref[:, part, cols].reshape(-1, HEAD), v_ref[:, part, cols].reshape(-1, HEAD)
                loaded.append((q[part, cols], k, v, grad[part, cols]))
        scores = [mm_t(query, k) * scale for query, k, _, _ in loaded]
        grad_probs = [mm_t(out_grad, v) for _, _, v, out_grad in loaded]
        results = []
        for score, grad_prob, (query, k, v, out_grad) in zip(scores, grad_probs, loaded):
            prob = softmax(score)
            inner = jnp.sum(prob * grad_prob, axis=-1, keepdims=True)
            grad_score = (prob * (grad_prob - inner) * scale).astype(BF)
            results.append((mm(grad_score, k), tm(grad_score, query), tm(prob.astype(BF), out_grad)))
        for (part, cols), (one, two, three) in zip(places, results):
            dq[part, cols] = one.astype(BF)
            dk[:, part, cols] = two.astype(BF).reshape(pack.fsdp, lat_rows, HEAD)
            dv[:, part, cols] = three.astype(BF).reshape(pack.fsdp, lat_rows, HEAD)
        return carry

    lax.fori_loop(0, HEADS // HEADS_AT_ONCE, some_heads, 0)
    d_q, d_k, d_v = dq[...], dk[...].reshape(-1, pack.width), dv[...].reshape(-1, pack.width)
    w_query = pack.ready(scratch[0], sems.at[0])
    w_key, w_value = pack.ready(scratch[1], sems.at[1]), pack.ready(scratch[2], sems.at[2])
    slot_o[...] = mm_t(d_q, w_query) + mm_t(d_k[:rows], w_key) + mm_t(d_v[:rows], w_value)
    others = mm_t(d_k[rows:], w_key) + mm_t(d_v[rows:], w_value)
    slots_o[...] = others.astype(BF).reshape(slots_o.shape)
    pack.put(grads_o, 0, [tm(left, d_q) for left in pack.columns(every.at[pl.ds(0, rows)])])
    columns = pack.columns(every)
    pack.put(grads_o, 1, [tm(left, d_k) for left in columns])
    pack.put(grads_o, 2, [tm(left, d_v) for left in columns])


def latent_kernel(pack, n_source, *refs):
    mixed, first_out, cotangent, small_ref = refs[:4]
    sources, rest = refs[4 : 4 + n_source], refs[4 + n_source :]
    outs = 4 + len(pack.grads(3))
    d_mixed_o, sums_o, result_o, grad_o, *grads_o = rest[:outs]
    scratch, (act_s, normed_s, sems) = rest[outs : outs + 3], rest[outs + 3 :]
    for index in range(3):
        pack.fetch(sources, index, scratch[index], sems.at[index])
    small = small_rows(small_ref)
    w_out = pack.ready(scratch[0], sems.at[0])
    resid = first_out[...] + mm(mixed[...], w_out)
    hat, inverse = norm_parts(resid)
    normed_s[...] = (hat * small(7) + small(9)).astype(BF)
    w_first = pack.ready(scratch[1], sems.at[1])
    pre = mm(normed_s[...], w_first) + small(10)
    act_s[...] = gelu(pre).astype(BF)
    w_second = pack.ready(scratch[2], sems.at[2])
    result_o[...] = (resid + mm(act_s[...], w_second) + small(11)).astype(BF)
    grad_low = cotangent[...]
    grad_out = grad_low.astype(F32)
    pack.put_product(grads_o, 1, act_s, grad_low)
    d_pre = mm_t(grad_low, w_second) * gelu_slope(pre)
    d_pre_low = d_pre.astype(BF)
    pack.put_product(grads_o, 0, normed_s, d_pre_low)
    d_normed = mm_t(d_pre_low, w_first)
    grad_mid = grad_out + norm_back(hat, inverse, small(7), d_normed)
    grad_o[...] = grad_mid
    grad_low = grad_mid.astype(BF)
    d_mixed_o[...] = mm_t(grad_low, w_out).astype(BF)
    pack.put_product(grads_o, 2, mixed, grad_low)
    sums_o[0:1] = column_sum(d_normed * hat)
    sums_o[1:2] = column_sum(d_normed)
    sums_o[2:3] = column_sum(d_pre)
    sums_o[3:4] = column_sum(grad_out)


def encoder_back_kernel(pack, n_source, n_other, *refs):
    slot, grad_mid, first_out, resid, pre_ref, act, small_ref = refs[:7]
    others, rest = refs[7 : 7 + n_other], refs[7 + n_other :]
    sources, rest = rest[:n_source], rest[n_source:]
    outs = 2 + len(pack.grads(2))
    grad_o, sums_o, *grads_o = rest[:outs]
    scratch, (normed_s, sems) = rest[outs : outs + 2], rest[outs + 2 :]
    for index in range(2):
        pack.fetch(sources, index, scratch[index], sems.at[index])
    small = small_rows(small_ref)
    d_normed = slot[...] + sum(ref[...].astype(F32) for ref in others)
    hat, inverse = norm_parts(first_out[...])
    sums_o[0:1] = column_sum(d_normed * hat)
    sums_o[1:2] = column_sum(d_normed)
    grad_out = grad_mid[...] + norm_back(hat, inverse, small(6), d_normed)
    grad_low = grad_out.astype(BF)
    w_second = pack.ready(scratch[1], sems.at[1])
    d_pre = mm_t(grad_low, w_second) * gelu_slope(pre_ref[...])
    d_pre_low = d_pre.astype(BF)
    d_normed = mm_t(d_pre_low, pack.ready(scratch[0], sems.at[0]))
    hat, inverse = norm_parts(resid[...])
    grad_o[...] = grad_out + norm_back(hat, inverse, small(1), d_normed)
    normed_s[...] = (hat * small(1) + small(3)).astype(BF)
    pack.put_product(grads_o, 0, normed_s, d_pre_low)
    pack.put_product(grads_o, 1, act, grad_low)
    sums_o[2:3] = column_sum(d_normed * hat)
    sums_o[3:4] = column_sum(d_normed)
    sums_o[4:5] = column_sum(d_pre)
    sums_o[5:6] = column_sum(grad_out)


def cross_back_kernel(pack, n_source, padded, share, *refs):
    grad_ref, latents, mixed, mixed_pix, probs_ref, pix, query_pix, enc_q, small_ref, lat_sums, enc_sums, pix_hat = refs[:12]
    sources, rest = refs[12 : 12 + n_source], refs[12 + n_source :]
    outs = 3 + len(pack.grads(3))
    d_pix_o, pix_sums_o, d_latents_o, *grads_o = rest[:outs]
    scratch, (d_mixed_s, in_low_s, high_s, low_s, sems) = rest[outs : outs + 3], rest[outs + 3 :]
    for slot, index in enumerate((3, 4, 2)):
        pack.fetch(sources, index, scratch[slot], sems.at[slot])
    small = small_rows(small_ref)
    half = pack.width // 2
    scale = pack.width**-0.5
    grad_enc = grad_ref[...]
    grad_low = grad_enc.astype(BF)
    d_mixed_s[...] = mm_t(grad_low, pack.ready(scratch[0], sems.at[0])).astype(BF)
    kv = pack.ready(scratch[1], sems.at[1])
    mixed_back = mm(d_mixed_s[...], kv[:, half : half + padded]).astype(BF)
    d_probs = mm_t(mixed_back, pix[...])
    probs = probs_ref[...]
    inner = jnp.sum(probs * d_probs, axis=-1, keepdims=True)
    d_scores = (probs * (d_probs - inner) * scale).astype(BF)
    d_pix = tm(query_pix[...], d_scores) + tm(mixed_back, probs.astype(BF))
    kept, used = pix_hat.shape
    d_pix = d_pix[:kept]
    gain_sum = jnp.sum(d_pix * pix_hat[...], axis=-1, keepdims=True)
    bias_sum = jnp.sum(d_pix, axis=-1, keepdims=True)
    lane = lax.broadcasted_iota(jnp.int32, pix_sums_o.shape, 1)
    pix_sums_o[...] = jnp.where(lane == 0, gain_sum, jnp.where(lane == 1, bias_sum, 0.0))
    shard = lax.axis_index("fsdp")
    for target in range(pack.fsdp):
        slot = lax.rem(shard + pack.fsdp - target, pack.fsdp)
        last = min(used, (target + 1) * share)
        piece = d_pix[:, target * share : last]
        if last < (target + 1) * share:
            piece = jnp.concatenate([piece, jnp.zeros((kept, (target + 1) * share - last), F32)], axis=1)
        d_pix_o[slot] = piece
    d_query_pix = mm(d_scores, pix[...]).astype(BF)
    d_enc_q = mm_t(d_query_pix, kv[:, :padded]).astype(BF)
    hat, inverse = norm_parts(latents[...].astype(F32))
    in_low_s[...] = (hat * small(0) + small(2)).astype(BF)
    d_normed = mm_t(d_enc_q, pack.ready(scratch[2], sems.at[2]))
    d_latents_o[...] = grad_enc + norm_back(hat, inverse, small(0), d_normed)
    order = [column_sum(d_normed * hat), enc_sums[2:3], column_sum(d_normed), enc_sums[3:4], enc_sums[4:5], enc_sums[5:6]]
    order += [enc_sums[0:1], lat_sums[0:1], enc_sums[1:2], lat_sums[1:2], lat_sums[2:3], lat_sums[3:4]]
    sums = jnp.concatenate(order + [jnp.zeros((16 - len(order), pack.width), F32)], axis=0)
    high = sums.astype(BF)
    high_s[...] = high
    low_s[...] = (sums - high.astype(F32)).astype(BF)
    shape = (16, half - padded)
    eye = lax.broadcasted_iota(jnp.int32, shape, 0) == lax.broadcasted_iota(jnp.int32, shape, 1)
    eye = eye.astype(F32).astype(BF)
    blocks = []
    for left, high_c, right, low_c in zip(*(pack.columns(r) for r in (enc_q, high_s, d_mixed_s, low_s))):
        columns = [tm(left, d_query_pix), tm(high_c, eye), tm(right, mixed_pix[...]), tm(low_c, eye)]
        blocks.append(jnp.concatenate(columns, axis=1))
    pack.put(grads_o, 0, blocks)
    pack.put_product(grads_o, 1, in_low_s, d_enc_q)
    pack.put_product(grads_o, 2, mixed, grad_low)


def pack_kernel(own, padded, *refs):
    gains_biases, pix_kv, query, out, mlp, packed = refs[:4], *refs[4:]
    half = packed.shape[1] // 2

    def turned(values, columns, rowwise=False):
        rows = values.shape[1 if rowwise else 0]
        eye = lax.broadcasted_iota(jnp.int32, (rows, columns), 0) == lax.broadcasted_iota(jnp.int32, (rows, columns), 1)
        return (mm if rowwise else tm)(values, eye.astype(F32).astype(BF)).astype(BF)

    packed[0:own], packed[own : 2 * own] = mlp[0], mlp[1]
    packed[2 * own : 3 * own], packed[3 * own : 4 * own] = query[...], out[...]
    small = jnp.concatenate([ref[...].astype(F32) for ref in gains_biases], axis=0).astype(BF)
    last = packed.at[pl.ds(4 * own, own)]
    last[:, 0:padded] = turned(pix_kv[0], padded, True)
    last[:, padded:half] = turned(small, half - padded)
    last[:, half : half + padded] = turned(pix_kv[1], padded, True)
    last[:, half + padded :] = jnp.zeros((own, half - padded), BF)


def pad_lanes(values, width):
    return jnp.pad(values, [(0, 0)] * (values.ndim - 1) + [(0, width - values.shape[-1])])


def body(
    sizes,
    latents,
    pixels,
    lengths,
    pix_gain,
    pix_bias,
    pix_kv,
    enc_query,
    enc_out,
    enc_mlp,
    enc_gains,
    enc_biases,
    lat_qkv,
    lat_out,
    lat_mlp,
    lat_gains,
    lat_biases,
    cotangent,
):
    dp_size, fsdp_size = sizes
    devices = dp_size * fsdp_size
    my_fsdp = lax.axis_index("fsdp")
    me = lax.axis_index("dp") * fsdp_size + my_fsdp
    images, lat_rows, width = latents.shape
    rows = images * lat_rows
    pix_rows, features = pixels.shape
    padded = -(-features // LANES) * LANES
    own = width // devices

    _, _, far = bits_of(sizes)
    steps = range(1, len(far))
    half = width // 2

    wide, dma = jax.ShapeDtypeStruct, pltpu.SemaphoreType.DMA
    enc_pack = pl.pallas_call(
        partial(pack_kernel, own, padded), out_shape=wide((5 * own, width), BF), name="pack"
    )(enc_gains, enc_biases, lat_gains, lat_biases, jnp.transpose(pix_kv, (0, 2, 1)), enc_query, enc_out, enc_mlp)
    in_two = fsdp_size == 4
    enc_parts = exchange_one(enc_pack) if in_two else gather_slots(enc_pack, fsdp_size)
    gain_f = pix_gain.astype(F32)
    pix_hat, pix_inverse = norm_parts(pixels.astype(F32))
    pix_low = pad_lanes((pix_hat * gain_f + pix_bias.astype(F32)).astype(BF), padded)[:USED]
    pix_hat_t = jnp.pad(pix_hat[:USED].T, ((0, -features % 8), (0, 0)))
    if in_two:
        enc_parts, enc_pack = seal(enc_parts, enc_pack)
        enc_parts = [enc_pack] + slots_of(exchange_two(list(enc_parts), my_fsdp), my_fsdp)
    enc_parts, pix_low, pix_hat, pix_hat_t, pix_inverse, lat_qkv = seal(
        enc_parts, pix_low, pix_hat, pix_hat_t, pix_inverse, lat_qkv
    )

    enc_groups = far_step([v[None] for v in halves_of(order_slots(list(enc_parts), my_fsdp))], 0, sizes, me)
    lat_pack = jnp.concatenate([lat_qkv.reshape(3 * own, width), lat_out, lat_mlp[0], lat_mlp[1]], axis=0)
    lat_one = slot_shift(lat_pack, fsdp_size, 1)
    enc_groups, lat_pack, lat_one = seal(enc_groups, lat_pack, lat_one)

    for place in steps:
        enc_groups = far_step(enc_groups, place, sizes, me)
    lat_parts = [lat_pack, lat_one] + [slot_shift(lat_pack, fsdp_size, j) for j in range(2, fsdp_size)]
    enc_groups, lat_parts = seal(enc_groups, lat_parts)
    lat_whole = order_slots(list(lat_parts), my_fsdp)[None]
    qkv_groups = halves_of(lat_whole[:, :, : 3 * own])

    enc_whole = jnp.concatenate(enc_groups, axis=-1)
    enc_got = core_swap(enc_whole, sizes)
    qkv_groups = far_step(qkv_groups, 0, sizes, me)
    other_groups = halves_of(lat_whole[:, :, 3 * own :])
    enc_whole, enc_got, qkv_groups, other_groups = seal(enc_whole, enc_got, qkv_groups, other_groups)

    pack = Pack(sizes, own, width)
    for place in steps:
        qkv_groups = far_step(qkv_groups, place, sizes, me)
    enc_sources = sources_of(enc_whole, enc_got, 5, sizes, me)
    n_gain, n_bias = enc_gains.shape[0], enc_biases.shape[0]

    small_all, lat_low, enc_q, query_pix, probs, mixed_pix, enc_mixed, enc_resid, enc_pre, enc_act, first_out = kernel_call(
        partial(encoder_kernel, pack, len(enc_sources), padded, lat_rows),
        "encoder",
        [latents.reshape(rows, width), pix_low],
        enc_sources,
        [wide((16, width), F32), wide((rows, width), BF)]
        + [wide((rows, width), BF), wide((rows, padded), BF), wide((rows, USED), F32), wide((rows, padded), BF)]
        + [wide((rows, width), BF), wide((rows, width), F32), wide((rows, width), F32), wide((rows, width), BF)]
        + [wide((rows, width), F32)],
        [pack.scratch()] * 5,
        48,
        36,
        scalars=[lengths],
    )
    qkv_whole = jnp.concatenate(qkv_groups, axis=-1)
    lat_low, qkv_whole, other_groups = seal(lat_low, qkv_whole, other_groups)

    if in_two:
        shards = exchange_one(lat_low)
    else:
        shards = [slot_shift(lat_low, fsdp_size, j) for j in range(1, fsdp_size)]
    qkv_got = core_swap(qkv_whole, sizes)
    other_groups = far_step(other_groups, 0, sizes, me)
    lat_low, shards, qkv_got, other_groups = seal(lat_low, shards, qkv_got, other_groups)
    if in_two:
        shards = exchange_two(list(shards), my_fsdp)
    for place in steps:
        other_groups = far_step(other_groups, place, sizes, me)
    other_whole = jnp.concatenate(other_groups, axis=-1)
    shards, other_whole = seal(list(shards), other_whole)
    other_got = core_swap(other_whole, sizes)
    qkv_sources = sources_of(qkv_whole, qkv_got, 3, sizes, me)
    every = wide((fsdp_size, rows, width), BF)
    lat_mixed, lat_every, lat_q, lat_k, lat_v = kernel_call(
        partial(attention_kernel, pack, len(qkv_sources), len(shards), lat_rows),
        "attention",
        [lat_low] + shards,
        qkv_sources,
        [wide((rows, width), BF)]
        + [wide((fsdp_size * rows, width), BF), wide((rows, width), BF), every, every],
        [pack.scratch()] * 3 + [dma((3,))],
        40,
        40,
        held=False,
    )
    other_sources = sources_of(other_whole, other_got, 3, sizes, me)
    d_mixed, lat_sums, result, grad_mid, *grads_m = kernel_call(
        partial(latent_kernel, pack, len(other_sources)),
        "latent",
        [lat_mixed, first_out, cotangent.reshape(rows, width), small_all],
        other_sources,
        [wide((rows, width), BF), wide((8, width), F32)]
        + [wide((rows, width), BF), wide((rows, width), F32)] + pack.grads(3),
        [pack.scratch()] * 3 + [pltpu.VMEM((rows, width), BF)] * 2 + [dma((3,))],
        44,
        36,
        held=False,
    )

    grads_m = core_terms(grads_m, sizes, me)
    slots, slot, *grads_q = kernel_call(
        partial(attention_back_kernel, pack, len(qkv_sources), lat_rows),
        "attention_back",
        [lat_q, lat_k, lat_v, d_mixed, lat_every],
        qkv_sources,
        [wide((fsdp_size - 1, rows, width), BF)]
        + [wide((rows, width), F32)] + pack.grads(3),
        [pack.scratch()] * 3
        + [pltpu.VMEM((rows, width), BF)]
        + [pltpu.VMEM(every.shape, BF)] * 2
        + [dma((3,))],
        48,
        72,
        held=False,
    )
    slots, grads_q = seal(slots, grads_q)

    slots = [slots[j] for j in range(fsdp_size - 1)]
    if in_two:
        received = collect_one(slots, my_fsdp)
    else:
        received = [slot_shift(slots[j - 1], fsdp_size, fsdp_size - j) for j in range(1, fsdp_size)]
    grads_m = far_pair(grads_m, 0, sizes, me)
    slots, received, grads_m = seal(slots, received, grads_m)
    if in_two:
        received = collect_two(slots, received, my_fsdp)
    for place in steps:
        grads_m = far_pair(grads_m, place, sizes, me)
    grads_q = core_terms(grads_q, sizes, me)
    received, grads_m, grads_q = seal(received, grads_m, grads_q)
    received = list(received)
    grad_enc, enc_sums, *grads_e = kernel_call(
        partial(encoder_back_kernel, pack, len(enc_sources), len(received)),
        "encoder_back",
        [slot, grad_mid, first_out, enc_resid, enc_pre, enc_act, small_all] + received,
        enc_sources,
        [wide((rows, width), F32), wide((8, width), F32)] + pack.grads(2),
        [pack.scratch()] * 2 + [pltpu.VMEM((rows, width), BF), dma((2,))],
        40,
        36,
        held=False,
    )
    grad_enc, grads_m, grads_q = seal(grad_enc, grads_m, grads_q)
    l_other_own, l_other_got = fsdp_part(grads_m, my_fsdp, sizes), fsdp_swap(grads_m, sizes, my_fsdp)
    grads_q = far_pair(grads_q, 0, sizes, me)
    share = pix_rows // fsdp_size
    kept = pix_hat_t.shape[0]
    pieces, d_pix_sums, d_latents, *grads_f = kernel_call(
        partial(cross_back_kernel, pack, len(enc_sources), padded, share),
        "cross_back",
        [grad_enc, latents.reshape(rows, width), enc_mixed, mixed_pix, probs, pix_low, query_pix, enc_q, small_all]
        + [lat_sums, enc_sums, pix_hat_t],
        enc_sources,
        [wide((fsdp_size, kept, share), F32), wide((kept, LANES), F32)]
        + [wide((rows, width), F32)] + pack.grads(3),
        [pack.scratch()] * 3
        + [pltpu.VMEM((rows, width), BF)] * 2
        + [pltpu.VMEM((16, width), BF)] * 2
        + [dma((3,))],
        48,
        50,
        held=False,
    )
    pieces, grads_e, grads_f, d_pix_sums, grads_q, l_other_got = seal(
        pieces, grads_e, grads_f, d_pix_sums, grads_q, l_other_got
    )

    low_bits, core, _ = bits_of(sizes)
    grads_e, grads_f = core_terms(grads_e, sizes, me), core_terms(grads_f, sizes, me)
    for place in steps:
        grads_q = far_pair(grads_q, place, sizes, me)
    d_pix_sums = total_over(d_pix_sums[:features, :2].T, low_bits[::-1][:1], sizes)
    pieces, grads_e, grads_f, grads_q, d_pix_sums = seal(pieces, grads_e, grads_f, grads_q, d_pix_sums)

    grads_e = [[jnp.concatenate(both, axis=1) for both in zip(e, f)] for e, f in zip(grads_e, grads_f)]
    d_pix_own = pieces[0]
    for j in range(1, fsdp_size):
        d_pix_own = d_pix_own + slot_shift(pieces[j].astype(BF), fsdp_size, fsdp_size - j).astype(F32)
    grads_e = far_pair(grads_e, 0, sizes, me)
    d_pix_own, grads_e, grads_q, d_pix_sums = seal(d_pix_own, grads_e, grads_q, d_pix_sums)

    l_qkv_own, l_qkv_got = fsdp_part(grads_q, my_fsdp, sizes), fsdp_swap(grads_q, sizes, my_fsdp)
    for place in steps:
        grads_e = far_pair(grads_e, place, sizes, me)
    l_qkv_got, l_other_got, grads_e, d_pix_sums = seal(l_qkv_got, l_other_got, grads_e, d_pix_sums)
    d_pix_sums = total_over(d_pix_sums, low_bits[::-1][1:] + [core] + far, sizes)
    enc_got = fsdp_swap(grads_e, sizes, my_fsdp)
    l_other_grads = fsdp_sum(l_other_own, l_other_got)
    l_qkv_grads = fsdp_sum(l_qkv_own, l_qkv_got)
    enc_grads = fsdp_sum(fsdp_part(grads_e, my_fsdp, sizes), enc_got)
    hat_own = lax.dynamic_slice_in_dim(pix_hat, my_fsdp * share, share, 0)
    inverse_own = lax.dynamic_slice_in_dim(pix_inverse, my_fsdp * share, share, 0)
    d_pixels = norm_back(hat_own, inverse_own, gain_f, d_pix_own[:features].T)
    kv_own = enc_grads[2]
    d_pix_kv = jnp.stack([kv_own[:, :features].T, kv_own[:, width // 2 : width // 2 + features].T])
    start = width // 2 + padded
    n_small = 2 * (n_gain + n_bias)
    small_own = (kv_own[:, padded : padded + n_small] + kv_own[:, start : start + n_small]).T
    return (
        result.reshape(latents.shape),
        d_latents.reshape(latents.shape),
        d_pixels,
        d_pix_sums[0],
        d_pix_sums[1],
        d_pix_kv,
        enc_grads[3],
        enc_grads[4],
        enc_grads[:2],
        small_own[:n_gain],
        small_own[n_gain : n_gain + n_bias],
        l_qkv_grads,
        l_other_grads[2],
        l_other_grads[:2],
        small_own[n_gain + n_bias : 2 * n_gain + n_bias],
        small_own[2 * n_gain + n_bias :],
    )


def solution(mesh):
    split, rows, columns = P("dp", "fsdp", None), P(AXES, None), P(None, AXES)
    middle = P(None, AXES, None)
    weights = (P(None, None, AXES), rows, rows, middle, columns, columns, middle, rows, middle, columns, columns)
    return jax.shard_map(
        partial(body, (mesh.shape["dp"], mesh.shape["fsdp"])),
        mesh=mesh,
        in_specs=(split, P("dp", None), P("dp", None), P(), P()) + weights + (split,),
        out_specs=(split, split, rows, P(), P()) + weights,
        check_vma=False,
    )
```

```python
from functools import partial

import jax
import jax.numpy as jnp
from jax import lax
from jax.experimental.layout import Layout, with_layout_constraint
from jax.experimental import pallas as pl
from jax.experimental.pallas import tpu as pltpu
from jax.sharding import PartitionSpec as P

HEADS = 8
HEAD = 128
USED = 1792
EPSILON = 1e-05
MASKED = -1e30
AXES = ("dp", "fsdp")
LANES = 128
HEADS_AT_ONCE = 8
BF = jnp.bfloat16
F32 = jnp.float32


def dot(left, right, dims):
    return lax.dot_general(left, right, ((dims[0], dims[1]), ((), ())), preferred_element_type=F32)


def mm(left, right):
    return dot(left, right, ((left.ndim - 1,), (0,)))


def mm_t(left, right):
    return dot(left, right, ((left.ndim - 1,), (1,)))


def tm(left, right):
    return dot(left, right, ((0,), (0,)))


def norm_parts(values):
    average = jnp.mean(values, axis=-1, keepdims=True)
    centered = values - average
    variance = jnp.mean(centered * centered, axis=-1, keepdims=True)
    inverse = lax.rsqrt(variance + EPSILON)
    return centered * inverse, inverse


def norm_back(hat, inverse, gains, grad_out):
    grad_hat = grad_out * gains
    first = jnp.mean(grad_hat, axis=-1, keepdims=True)
    second = jnp.mean(grad_hat * hat, axis=-1, keepdims=True)
    return inverse * (grad_hat - first - hat * second)


def gelu(values):
    return 0.5 * values * (1.0 + lax.erf(values * (0.5**0.5)))


def gelu_slope(values):
    density = jnp.exp(-0.5 * values * values) * ((0.5 / jnp.pi) ** 0.5)
    return 0.5 * (1.0 + lax.erf(values * (0.5**0.5))) + values * density


def xor_permute(values, sizes, step):
    dp_size, fsdp_size = sizes
    total = dp_size * fsdp_size
    return lax.ppermute(values, AXES, [(i, i ^ step) for i in range(total)])


def seal(*values):
    return lax.optimization_barrier(values)


def bits_of(sizes):
    low = sizes[1].bit_length() - 1
    every = list(range((sizes[0] * sizes[1]).bit_length() - 1))
    return every[:low], every[low], every[low + 1 :]


def gather_fsdp(values, sizes):
    return [values] + [xor_permute(values, sizes, k) for k in range(1, sizes[1])]


def slot_shift(values, size, j):
    return lax.ppermute(values, "fsdp", [(i, (i + j) % size) for i in range(size)])


def hop(values, pairs):
    return lax.ppermute(values, "fsdp", pairs)


UP, DOWN = [(0, 1), (1, 2), (2, 3)], [(3, 2), (2, 1), (1, 0)]


def exchange_one(values):
    return [hop(values, UP), hop(values, DOWN)]


def exchange_two(first, shard):
    up, down = first
    far = jnp.where(shard == 1, up, down)
    return first + [hop(up, UP[1:]), hop(down, DOWN[1:]), hop(far, [(1, 3), (2, 0)])]


def gather_slots(values, size):
    return [values] + [slot_shift(values, size, j) for j in range(1, size)]


def slots_of(parts, shard):
    up, down, up_two, down_two, far = parts
    return [jnp.where(shard == 0, far, up), jnp.where(shard <= 1, down_two, up_two), jnp.where(shard == 3, far, down)]


def order_slots(slots, shard):
    size = len(slots)
    parts = [slots[-t % size] for t in range(size)]
    for bit in range(size.bit_length() - 1):
        mine = ((shard >> bit) & 1) == 1
        parts = [jnp.where(mine, parts[(t - (1 << bit)) % size], parts[t]) for t in range(size)]
    return jnp.stack(parts)


def fill_every(every, own, parts, n_shard):
    rows = own.shape[0]
    every[0:rows] = own[...]
    if len(parts) == n_shard - 1:
        slots = [part[...] for part in parts]
    else:
        shard = lax.axis_index("fsdp")
        slots = slots_of([part[...] for part in parts], shard)
    for j, slot in enumerate(slots):
        every[(j + 1) * rows : (j + 2) * rows] = slot


def collect_one(slots, shard):
    far = jnp.where(shard == 0, slots[0], slots[2])
    return [hop(slots[1], UP[:2]), hop(slots[1], DOWN[:2]), hop(far, [(0, 2), (3, 1)])]


def collect_two(slots, first, shard):
    up, down, far = [part.astype(F32) for part in first]
    up = slots[2].astype(F32) + up + jnp.where(shard == 2, far, 0.0)
    down = slots[0].astype(F32) + down + jnp.where(shard == 1, far, 0.0)
    return [hop(up.astype(BF), UP), hop(down.astype(BF), DOWN)]


def order_fsdp(parts, sizes, me):
    low, _, _ = bits_of(sizes)
    for bit in low:
        mine = ((me >> bit) & 1) == 1
        parts = [jnp.where(mine, parts[k ^ (1 << bit)], parts[k]) for k in range(len(parts))]
    return jnp.stack(parts)


def merge(own, got, bit, above, me):
    mine = ((me >> bit) & 1) == 1
    view = (2**above, -1) + own.shape[1:]
    own, got = own.reshape(view), got.reshape(view)
    both = jnp.stack([jnp.where(mine, got, own), jnp.where(mine, own, got)], axis=1)
    return both.reshape((-1,) + own.shape[2:])


def far_step(groups, place, sizes, me):
    _, _, far = bits_of(sizes)
    result = []
    for values, order in zip(groups, (far, far[::-1])):
        bit, held = order[place], order[:place]
        got = xor_permute(values, sizes, 1 << bit)
        result.append(merge(values, got, bit, sum(1 for other in held if other > bit), me))
    return result


def core_swap(whole, sizes):
    _, core, _ = bits_of(sizes)
    return xor_permute(whole, sizes, 1 << core)


def sources_of(whole, got, count, sizes, me):
    own = whole.shape[2] // count
    if own % 16 == 0:
        return [whole, got]
    _, core, _ = bits_of(sizes)
    mine = ((me >> core) & 1) == 1
    both = jnp.stack([jnp.where(mine, got, whole), jnp.where(mine, whole, got)], axis=1)
    parts = [both[:, :, :, i * own : (i + 1) * own] for i in range(count)]
    return [part.reshape(-1, part.shape[-1]) for part in parts]


def halves_of(values):
    half = values.shape[-1] // 2
    return [values[..., :half], values[..., half:]]


def core_terms(grads, sizes, me):
    _, core, _ = bits_of(sizes)
    if len(grads) == 1:
        mine = (me >> core) & 1
        count, width = grads[0].shape[0], grads[0].shape[-1]
        view = jnp.swapaxes(grads[0].reshape(count, sizes[0] // 2, 2, -1, width), 0, 1)
        send = lax.dynamic_index_in_dim(view, 1 - mine, 2, keepdims=False)
        keep = lax.dynamic_index_in_dim(view, mine, 2, keepdims=False)
    else:
        send, keep = grads
    got = xor_permute(send, sizes, 1 << core)
    return [list(terms) for terms in zip(halves_of(keep), halves_of(got))]


def sum_of(terms):
    total = terms[0].astype(F32)
    for term in terms[1:]:
        total = total + term.astype(F32)
    return total


def far_terms(terms, bit, held, sizes, me):
    above = sum(1 for other in held if other > bit)
    mine = (me >> bit) & 1

    def half(term, side):
        view = term.reshape((2**above, 2, -1) + term.shape[1:])
        part = lax.dynamic_index_in_dim(view, side, 1, keepdims=False)
        return part.reshape((-1,) + term.shape[1:])

    send = sum_of([half(term, 1 - mine) for term in terms]).astype(BF)
    return [half(term, mine) for term in terms] + [xor_permute(send, sizes, 1 << bit)]


def far_pair(groups, place, sizes, me):
    _, _, far = bits_of(sizes)
    result = []
    for terms, order in zip(groups, (far, far[::-1])):
        held = [bit for bit in far if bit not in order[:place]]
        result.append(far_terms(terms, order[place], held, sizes, me))
    return result


def fsdp_part(groups, shard, sizes):
    def part(term):
        view = term[0].reshape(term.shape[1], sizes[1], -1, term.shape[-1])
        return lax.dynamic_index_in_dim(view, shard, 1, keepdims=False)

    return jnp.concatenate([sum_of([part(term) for term in terms]) for terms in groups], axis=-1)


def fsdp_swap(groups, sizes, my_fsdp):
    return [xor_permute(fsdp_part(groups, my_fsdp ^ k, sizes).astype(BF), sizes, k) for k in range(1, sizes[1])]


def fsdp_sum(own, got):
    return sum_of([own] + list(got))


def total_over(values, bits, sizes):
    for bit in bits:
        values = values + xor_permute(values, sizes, 1 << bit)
    return values


class Pack:
    def __init__(self, sizes, own, width):
        self.far, self.fsdp, self.own, self.width = sizes[0] // 2, sizes[1], own, width
        self.block = width // sizes[0]
        self.packed = own % 16 == 0
        self.split = self.block % LANES == 0

    def scratch(self):
        shape = (self.far, 2, self.fsdp, self.own, self.width) if self.packed else (self.width, self.width)
        return pltpu.VMEM(shape, BF)

    def fetch(self, sources, index, scratch, sem):
        if not self.packed:
            pltpu.make_async_copy(sources[index], scratch, sem).start()
            return
        core = lax.axis_index("dp") & 1
        rows = pl.ds(index * self.own, self.own)
        for source, side in ((sources[0], core), (sources[1], 1 - core)):
            pltpu.make_async_copy(source.at[:, :, rows, :], scratch.at[:, side], sem).start()

    def ready(self, scratch, sem):
        pltpu.make_async_copy(scratch, scratch, sem).wait()
        return scratch[...].reshape(self.width, self.width)

    def build(self, sources, index, scratch):
        if not self.packed:
            return sources[index][...]
        core = lax.axis_index("dp") & 1
        rows = pl.ds(index * self.own, self.own)
        for source, side in ((sources[0], core), (sources[1], 1 - core)):
            scratch[:, side] = source[:, :, rows, :]
        return scratch[...].reshape(self.width, self.width)

    def grads(self, count):
        if not self.split:
            return [jax.ShapeDtypeStruct((count, self.width, self.width), BF)]
        return [jax.ShapeDtypeStruct((self.far, count, self.block, self.width), BF)] * 2

    def columns(self, ref):
        if not self.split:
            return [ref[...]]
        core = lax.axis_index("dp") & 1
        result = []
        for side in (1 - core, core):
            starts = [pl.multiple_of((2 * i + side) * self.block, self.block) for i in range(self.far)]
            result.append(jnp.concatenate([ref[:, pl.ds(start, self.block)] for start in starts], axis=1))
        return result

    def put(self, refs, index, values):
        for ref, value in zip(refs, values):
            value = value.astype(BF)
            if self.split:
                ref[:, index] = value.reshape(self.far, self.block, self.width)
            else:
                ref[index] = value

    def put_product(self, refs, index, left_ref, right):
        self.put(refs, index, [tm(left, right) for left in self.columns(left_ref)])


def kernel_call(kernel, name, operands, sources, outs, scratch, vmem_mb, work_mb, scalars=(), held=True):
    specs = [pl.BlockSpec(memory_space=pltpu.SMEM)] * len(scalars)
    specs += [pl.BlockSpec(memory_space=pltpu.VMEM)] * len(operands)
    specs += [pl.BlockSpec(memory_space=pltpu.VMEM if held else pl.ANY)] * len(sources)
    return pl.pallas_call(
        kernel,
        in_specs=specs,
        out_specs=[pl.BlockSpec(memory_space=pltpu.VMEM)] * len(outs),
        out_shape=list(outs),
        scratch_shapes=scratch,
        compiler_params=pltpu.CompilerParams(vmem_limit_bytes=vmem_mb * 2**20),
        cost_estimate=pl.CostEstimate(flops=2**30, bytes_accessed=work_mb * 2**20, transcendentals=2**20),
        name=name,
    )(*scalars, *operands, *sources)


def column_sum(values):
    return jnp.sum(values, axis=0, keepdims=True)


def softmax(scores):
    powers = jnp.exp(scores - jnp.max(scores, axis=-1, keepdims=True))
    return powers * (1.0 / jnp.sum(powers, axis=-1, keepdims=True))


def small_rows(small_ref):
    return lambda i: small_ref[i : i + 1]


def encoder_kernel(pack, n_source, padded, lat_rows, *refs):
    counts, latents, pix = refs[:3]
    sources, rest = refs[3 : 3 + n_source], refs[3 + n_source :]
    small_o, low_o, q_o, query_pix_o, probs_o, mixed_pix_o, mixed_o, resid_o, pre_o, act_o, first_o = rest[:11]
    scratch = rest[11:16]
    half = pack.width // 2
    latent_in = latents[...].astype(F32)
    hat, _ = norm_parts(latent_in)
    kv = pack.build(sources, 4, scratch[0])
    shape = (small_o.shape[0], half - padded)
    eye = lax.broadcasted_iota(jnp.int32, shape, 0) == lax.broadcasted_iota(jnp.int32, shape, 1)
    small_o[...] = mm_t(eye.astype(F32).astype(BF), kv[:, padded:half])
    small = small_rows(small_o)
    in_low = (hat * small(0) + small(2)).astype(BF)
    query = mm(in_low, pack.build(sources, 2, scratch[1])).astype(BF)
    q_o[...] = query
    query_pix = mm(query, kv[:, :padded]).astype(BF)
    query_pix_o[...] = query_pix
    shape = probs_o.shape
    row, column = lax.broadcasted_iota(jnp.int32, shape, 0), lax.broadcasted_iota(jnp.int32, shape, 1)
    first, end, total = jnp.zeros(shape, jnp.int32), jnp.zeros(shape, jnp.int32), 0
    for image in range(shape[0] // lat_rows):
        here = (row >= image * lat_rows) & (row < (image + 1) * lat_rows)
        first = jnp.where(here, total, first)
        total = total + counts[0, image]
        end = jnp.where(here, total, end)
    scores = mm_t(query_pix, pix[...]) * pack.width**-0.5
    probs = softmax(jnp.where((column >= first) & (column < end), scores, MASKED))
    probs_o[...] = probs
    mixed_pix = mm(probs.astype(BF), pix[...]).astype(BF)
    mixed_pix_o[...] = mixed_pix
    mixed = mm_t(mixed_pix, kv[:, half : half + padded]).astype(BF)
    mixed_o[...] = mixed
    resid = latent_in + mm(mixed, pack.build(sources, 3, scratch[2]))
    resid_o[...] = resid
    hat, _ = norm_parts(resid)
    normed = (hat * small(1) + small(3)).astype(BF)
    pre = mm(normed, pack.build(sources, 0, scratch[3])) + small(4)
    pre_o[...] = pre
    act = gelu(pre).astype(BF)
    act_o[...] = act
    out = resid + mm(act, pack.build(sources, 1, scratch[4])) + small(5)
    first_o[...] = out
    hat, _ = norm_parts(out)
    low_o[...] = (hat * small(6) + small(8)).astype(BF)


def attention_kernel(pack, n_source, n_other, lat_rows, *refs):
    own, others, rest = refs[0], refs[1 : 1 + n_other], refs[1 + n_other :]
    sources, rest = rest[:n_source], rest[n_source:]
    mixed_o, every, q_o, k_o, v_o = rest[:5]
    scratch, sems = rest[5:8], rest[8]
    for index in range(3):
        pack.fetch(sources, index, scratch[index], sems.at[index])
    rows = own.shape[0]
    fill_every(every, own, others, pack.fsdp)
    q_o[...] = mm(own[...], pack.ready(scratch[0], sems.at[0])).astype(BF)
    k_o[...] = mm(every[...], pack.ready(scratch[1], sems.at[1])).astype(BF).reshape(k_o.shape)
    v_o[...] = mm(every[...], pack.ready(scratch[2], sems.at[2])).astype(BF).reshape(k_o.shape)

    def some_heads(step, carry):
        places, loaded = [], []
        for head in range(HEADS_AT_ONCE):
            cols = pl.ds(pl.multiple_of((step * HEADS_AT_ONCE + head) * HEAD, HEAD), HEAD)
            for start in range(0, rows, lat_rows):
                part = pl.ds(start, lat_rows)
                places.append((part, cols))
                loaded.append((q_o[part, cols], k_o[:, part, cols].reshape(-1, HEAD), v_o[:, part, cols].reshape(-1, HEAD)))
        scores = [mm_t(q, k) * HEAD**-0.5 for q, k, _ in loaded]
        probs = [softmax(score).astype(BF) for score in scores]
        mixed = [mm(prob, v).astype(BF) for prob, (_, _, v) in zip(probs, loaded)]
        for place, value in zip(places, mixed):
            mixed_o[place] = value
        return carry

    lax.fori_loop(0, HEADS // HEADS_AT_ONCE, some_heads, 0)


def attention_back_kernel(pack, n_source, lat_rows, *refs):
    q, k_ref, v_ref, grad, every = refs[:5]
    rest = refs[5:]
    sources, rest = rest[:n_source], rest[n_source:]
    outs = 2 + len(pack.grads(3))
    slots_o, slot_o, *grads_o = rest[:outs]
    scratch, (dq, dk, dv, sems) = rest[outs : outs + 3], rest[outs + 3 :]
    for index in range(3):
        pack.fetch(sources, index, scratch[index], sems.at[index])
    rows = q.shape[0]
    scale = HEAD**-0.5

    def some_heads(step, carry):
        places, loaded = [], []
        for head in range(HEADS_AT_ONCE):
            cols = pl.ds(pl.multiple_of((step * HEADS_AT_ONCE + head) * HEAD, HEAD), HEAD)
            for start in range(0, rows, lat_rows):
                part = pl.ds(start, lat_rows)
                places.append((part, cols))
                k, v = k_ref[:, part, cols].reshape(-1, HEAD), v_ref[:, part, cols].reshape(-1, HEAD)
                loaded.append((q[part, cols], k, v, grad[part, cols]))
        scores = [mm_t(query, k) * scale for query, k, _, _ in loaded]
        grad_probs = [mm_t(out_grad, v) for _, _, v, out_grad in loaded]
        results = []
        for score, grad_prob, (query, k, v, out_grad) in zip(scores, grad_probs, loaded):
            prob = softmax(score)
            inner = jnp.sum(prob * grad_prob, axis=-1, keepdims=True)
            grad_score = (prob * (grad_prob - inner) * scale).astype(BF)
            results.append((mm(grad_score, k), tm(grad_score, query), tm(prob.astype(BF), out_grad)))
        for (part, cols), (one, two, three) in zip(places, results):
            dq[part, cols] = one.astype(BF)
            dk[:, part, cols] = two.astype(BF).reshape(pack.fsdp, lat_rows, HEAD)
            dv[:, part, cols] = three.astype(BF).reshape(pack.fsdp, lat_rows, HEAD)
        return carry

    lax.fori_loop(0, HEADS // HEADS_AT_ONCE, some_heads, 0)
    d_q, d_k, d_v = dq[...], dk[...].reshape(-1, pack.width), dv[...].reshape(-1, pack.width)
    w_query = pack.ready(scratch[0], sems.at[0])
    w_key, w_value = pack.ready(scratch[1], sems.at[1]), pack.ready(scratch[2], sems.at[2])
    slot_o[...] = mm_t(d_q, w_query) + mm_t(d_k[:rows], w_key) + mm_t(d_v[:rows], w_value)
    others = mm_t(d_k[rows:], w_key) + mm_t(d_v[rows:], w_value)
    slots_o[...] = others.astype(BF).reshape(slots_o.shape)
    pack.put(grads_o, 0, [tm(left, d_q) for left in pack.columns(every.at[pl.ds(0, rows)])])
    columns = pack.columns(every)
    pack.put(grads_o, 1, [tm(left, d_k) for left in columns])
    pack.put(grads_o, 2, [tm(left, d_v) for left in columns])


def latent_kernel(pack, n_source, *refs):
    mixed, first_out, cotangent, small_ref = refs[:4]
    sources, rest = refs[4 : 4 + n_source], refs[4 + n_source :]
    outs = 4 + len(pack.grads(3))
    d_mixed_o, sums_o, result_o, grad_o, *grads_o = rest[:outs]
    scratch, (act_s, normed_s, sems) = rest[outs : outs + 3], rest[outs + 3 :]
    for index in range(3):
        pack.fetch(sources, index, scratch[index], sems.at[index])
    small = small_rows(small_ref)
    w_out = pack.ready(scratch[0], sems.at[0])
    resid = first_out[...] + mm(mixed[...], w_out)
    hat, inverse = norm_parts(resid)
    normed_s[...] = (hat * small(7) + small(9)).astype(BF)
    w_first = pack.ready(scratch[1], sems.at[1])
    pre = mm(normed_s[...], w_first) + small(10)
    act_s[...] = gelu(pre).astype(BF)
    w_second = pack.ready(scratch[2], sems.at[2])
    result_o[...] = (resid + mm(act_s[...], w_second) + small(11)).astype(BF)
    grad_low = cotangent[...]
    grad_out = grad_low.astype(F32)
    pack.put_product(grads_o, 1, act_s, grad_low)
    d_pre = mm_t(grad_low, w_second) * gelu_slope(pre)
    d_pre_low = d_pre.astype(BF)
    pack.put_product(grads_o, 0, normed_s, d_pre_low)
    d_normed = mm_t(d_pre_low, w_first)
    grad_mid = grad_out + norm_back(hat, inverse, small(7), d_normed)
    grad_o[...] = grad_mid
    grad_low = grad_mid.astype(BF)
    d_mixed_o[...] = mm_t(grad_low, w_out).astype(BF)
    pack.put_product(grads_o, 2, mixed, grad_low)
    sums_o[0:1] = column_sum(d_normed * hat)
    sums_o[1:2] = column_sum(d_normed)
    sums_o[2:3] = column_sum(d_pre)
    sums_o[3:4] = column_sum(grad_out)


def encoder_back_kernel(pack, n_source, n_other, *refs):
    slot, grad_mid, first_out, resid, pre_ref, act, small_ref = refs[:7]
    others, rest = refs[7 : 7 + n_other], refs[7 + n_other :]
    sources, rest = rest[:n_source], rest[n_source:]
    outs = 2 + len(pack.grads(2))
    grad_o, sums_o, *grads_o = rest[:outs]
    scratch, (normed_s, sems) = rest[outs : outs + 2], rest[outs + 2 :]
    for index in range(2):
        pack.fetch(sources, index, scratch[index], sems.at[index])
    small = small_rows(small_ref)
    d_normed = slot[...] + sum(ref[...].astype(F32) for ref in others)
    hat, inverse = norm_parts(first_out[...])
    sums_o[0:1] = column_sum(d_normed * hat)
    sums_o[1:2] = column_sum(d_normed)
    grad_out = grad_mid[...] + norm_back(hat, inverse, small(6), d_normed)
    grad_low = grad_out.astype(BF)
    w_second = pack.ready(scratch[1], sems.at[1])
    d_pre = mm_t(grad_low, w_second) * gelu_slope(pre_ref[...])
    d_pre_low = d_pre.astype(BF)
    d_normed = mm_t(d_pre_low, pack.ready(scratch[0], sems.at[0]))
    hat, inverse = norm_parts(resid[...])
    grad_o[...] = grad_out + norm_back(hat, inverse, small(1), d_normed)
    normed_s[...] = (hat * small(1) + small(3)).astype(BF)
    pack.put_product(grads_o, 0, normed_s, d_pre_low)
    pack.put_product(grads_o, 1, act, grad_low)
    sums_o[2:3] = column_sum(d_normed * hat)
    sums_o[3:4] = column_sum(d_normed)
    sums_o[4:5] = column_sum(d_pre)
    sums_o[5:6] = column_sum(grad_out)


def cross_back_kernel(pack, n_source, padded, share, *refs):
    grad_ref, latents, mixed, mixed_pix, probs_ref, pix, query_pix, enc_q, small_ref, lat_sums, enc_sums, pix_hat = refs[:12]
    sources, rest = refs[12 : 12 + n_source], refs[12 + n_source :]
    outs = 3 + len(pack.grads(3))
    d_pix_o, pix_sums_o, d_latents_o, *grads_o = rest[:outs]
    scratch, (d_mixed_s, in_low_s, high_s, low_s, sems) = rest[outs : outs + 3], rest[outs + 3 :]
    for slot, index in enumerate((3, 4, 2)):
        pack.fetch(sources, index, scratch[slot], sems.at[slot])
    small = small_rows(small_ref)
    half = pack.width // 2
    scale = pack.width**-0.5
    grad_enc = grad_ref[...]
    grad_low = grad_enc.astype(BF)
    d_mixed_s[...] = mm_t(grad_low, pack.ready(scratch[0], sems.at[0])).astype(BF)
    kv = pack.ready(scratch[1], sems.at[1])
    mixed_back = mm(d_mixed_s[...], kv[:, half : half + padded]).astype(BF)
    d_probs = mm_t(mixed_back, pix[...])
    probs = probs_ref[...]
    inner = jnp.sum(probs * d_probs, axis=-1, keepdims=True)
    d_scores = (probs * (d_probs - inner) * scale).astype(BF)
    d_pix = tm(query_pix[...], d_scores) + tm(mixed_back, probs.astype(BF))
    kept, used = pix_hat.shape
    d_pix = d_pix[:kept]
    gain_sum = jnp.sum(d_pix * pix_hat[...], axis=-1, keepdims=True)
    bias_sum = jnp.sum(d_pix, axis=-1, keepdims=True)
    lane = lax.broadcasted_iota(jnp.int32, pix_sums_o.shape, 1)
    pix_sums_o[...] = jnp.where(lane == 0, gain_sum, jnp.where(lane == 1, bias_sum, 0.0))
    shard = lax.axis_index("fsdp")
    for target in range(pack.fsdp):
        slot = lax.rem(shard + pack.fsdp - target, pack.fsdp)
        last = min(used, (target + 1) * share)
        piece = d_pix[:, target * share : last]
        if last < (target + 1) * share:
            piece = jnp.concatenate([piece, jnp.zeros((kept, (target + 1) * share - last), F32)], axis=1)
        d_pix_o[slot] = piece.astype(BF)
    d_query_pix = mm(d_scores, pix[...]).astype(BF)
    d_enc_q = mm_t(d_query_pix, kv[:, :padded]).astype(BF)
    hat, inverse = norm_parts(latents[...].astype(F32))
    in_low_s[...] = (hat * small(0) + small(2)).astype(BF)
    d_normed = mm_t(d_enc_q, pack.ready(scratch[2], sems.at[2]))
    d_latents_o[...] = grad_enc + norm_back(hat, inverse, small(0), d_normed)
    order = [column_sum(d_normed * hat), enc_sums[2:3], column_sum(d_normed), enc_sums[3:4], enc_sums[4:5], enc_sums[5:6]]
    order += [enc_sums[0:1], lat_sums[0:1], enc_sums[1:2], lat_sums[1:2], lat_sums[2:3], lat_sums[3:4]]
    sums = jnp.concatenate(order + [jnp.zeros((16 - len(order), pack.width), F32)], axis=0)
    high = sums.astype(BF)
    high_s[...] = high
    low_s[...] = (sums - high.astype(F32)).astype(BF)
    shape = (16, half - padded)
    eye = lax.broadcasted_iota(jnp.int32, shape, 0) == lax.broadcasted_iota(jnp.int32, shape, 1)
    eye = eye.astype(F32).astype(BF)
    blocks = []
    for left, high_c, right, low_c in zip(*(pack.columns(r) for r in (enc_q, high_s, d_mixed_s, low_s))):
        columns = [tm(left, d_query_pix), tm(high_c, eye), tm(right, mixed_pix[...]), tm(low_c, eye)]
        blocks.append(jnp.concatenate(columns, axis=1))
    pack.put(grads_o, 0, blocks)
    pack.put_product(grads_o, 1, in_low_s, d_enc_q)
    pack.put_product(grads_o, 2, mixed, grad_low)


def pack_kernel(own, padded, *refs):
    gains_biases, pix_kv, query, out, mlp, packed = refs[:4], *refs[4:]
    half = packed.shape[1] // 2

    def turned(values, columns, rowwise=False):
        rows = values.shape[1 if rowwise else 0]
        eye = lax.broadcasted_iota(jnp.int32, (rows, columns), 0) == lax.broadcasted_iota(jnp.int32, (rows, columns), 1)
        return (mm if rowwise else tm)(values, eye.astype(F32).astype(BF)).astype(BF)

    packed[0:own], packed[own : 2 * own] = mlp[0], mlp[1]
    packed[2 * own : 3 * own], packed[3 * own : 4 * own] = query[...], out[...]
    small = jnp.concatenate([ref[...].astype(F32) for ref in gains_biases], axis=0).astype(BF)
    last = packed.at[pl.ds(4 * own, own)]
    last[:, 0:padded] = turned(pix_kv[0], padded, True)
    last[:, padded:half] = turned(small, half - padded)
    last[:, half : half + padded] = turned(pix_kv[1], padded, True)
    last[:, half + padded :] = jnp.zeros((own, half - padded), BF)


def pad_lanes(values, width):
    return jnp.pad(values, [(0, 0)] * (values.ndim - 1) + [(0, width - values.shape[-1])])


def body(
    sizes,
    latents,
    pixels,
    lengths,
    pix_gain,
    pix_bias,
    pix_kv,
    enc_query,
    enc_out,
    enc_mlp,
    enc_gains,
    enc_biases,
    lat_qkv,
    lat_out,
    lat_mlp,
    lat_gains,
    lat_biases,
    cotangent,
):
    dp_size, fsdp_size = sizes
    devices = dp_size * fsdp_size
    my_fsdp = lax.axis_index("fsdp")
    me = lax.axis_index("dp") * fsdp_size + my_fsdp
    images, lat_rows, width = latents.shape
    rows = images * lat_rows
    pix_rows, features = pixels.shape
    padded = -(-features // LANES) * LANES
    own = width // devices

    _, _, far = bits_of(sizes)
    steps = range(1, len(far))
    half = width // 2

    wide, dma = jax.ShapeDtypeStruct, pltpu.SemaphoreType.DMA
    enc_pack = pl.pallas_call(
        partial(pack_kernel, own, padded), out_shape=wide((5 * own, width), BF), name="pack"
    )(enc_gains, enc_biases, lat_gains, lat_biases, jnp.transpose(pix_kv, (0, 2, 1)), enc_query, enc_out, enc_mlp)
    in_two = fsdp_size == 4
    enc_parts = exchange_one(enc_pack) if in_two else gather_slots(enc_pack, fsdp_size)
    gain_f = pix_gain.astype(F32)
    pix_hat, pix_inverse = norm_parts(pixels.astype(F32))
    pix_low = pad_lanes((pix_hat * gain_f + pix_bias.astype(F32)).astype(BF), padded)[:USED]
    pix_hat_t = jnp.pad(pix_hat[:USED].T, ((0, -features % 8), (0, 0)))
    if in_two:
        enc_parts, enc_pack = seal(enc_parts, enc_pack)
        enc_parts = [enc_pack] + slots_of(exchange_two(list(enc_parts), my_fsdp), my_fsdp)
    enc_parts, pix_low, pix_hat, pix_hat_t, pix_inverse, lat_qkv = seal(
        enc_parts, pix_low, pix_hat, pix_hat_t, pix_inverse, lat_qkv
    )

    enc_groups = far_step([v[None] for v in halves_of(order_slots(list(enc_parts), my_fsdp))], 0, sizes, me)
    lat_pack = jnp.concatenate([lat_qkv.reshape(3 * own, width), lat_out, lat_mlp[0], lat_mlp[1]], axis=0)
    lat_one = slot_shift(lat_pack, fsdp_size, 1)
    enc_groups, lat_pack, lat_one = seal(enc_groups, lat_pack, lat_one)

    for place in steps:
        enc_groups = far_step(enc_groups, place, sizes, me)
    lat_parts = [lat_pack, lat_one] + [slot_shift(lat_pack, fsdp_size, j) for j in range(2, fsdp_size)]
    enc_groups, lat_parts = seal(enc_groups, lat_parts)
    lat_whole = order_slots(list(lat_parts), my_fsdp)[None]
    qkv_groups = halves_of(lat_whole[:, :, : 3 * own])

    enc_whole = jnp.concatenate(enc_groups, axis=-1)
    enc_got = core_swap(enc_whole, sizes)
    qkv_groups = far_step(qkv_groups, 0, sizes, me)
    other_groups = halves_of(lat_whole[:, :, 3 * own :])
    enc_whole, enc_got, qkv_groups, other_groups = seal(enc_whole, enc_got, qkv_groups, other_groups)

    pack = Pack(sizes, own, width)
    for place in steps:
        qkv_groups = far_step(qkv_groups, place, sizes, me)
    enc_sources = sources_of(enc_whole, enc_got, 5, sizes, me)
    n_gain, n_bias = enc_gains.shape[0], enc_biases.shape[0]

    small_all, lat_low, enc_q, query_pix, probs, mixed_pix, enc_mixed, enc_resid, enc_pre, enc_act, first_out = kernel_call(
        partial(encoder_kernel, pack, len(enc_sources), padded, lat_rows),
        "encoder",
        [latents.reshape(rows, width), pix_low],
        enc_sources,
        [wide((16, width), F32), wide((rows, width), BF)]
        + [wide((rows, width), BF), wide((rows, padded), BF), wide((rows, USED), F32), wide((rows, padded), BF)]
        + [wide((rows, width), BF), wide((rows, width), F32), wide((rows, width), F32), wide((rows, width), BF)]
        + [wide((rows, width), F32)],
        [pack.scratch()] * 5,
        48,
        36,
        scalars=[lengths],
    )
    qkv_whole = jnp.concatenate(qkv_groups, axis=-1)
    lat_low, qkv_whole, other_groups = seal(lat_low, qkv_whole, other_groups)

    if in_two:
        shards = exchange_one(lat_low)
    else:
        shards = [slot_shift(lat_low, fsdp_size, j) for j in range(1, fsdp_size)]
    qkv_got = core_swap(qkv_whole, sizes)
    other_groups = far_step(other_groups, 0, sizes, me)
    lat_low, shards, qkv_got, other_groups = seal(lat_low, shards, qkv_got, other_groups)
    if in_two:
        shards = exchange_two(list(shards), my_fsdp)
    for place in steps:
        other_groups = far_step(other_groups, place, sizes, me)
    other_whole = jnp.concatenate(other_groups, axis=-1)
    shards, other_whole = seal(list(shards), other_whole)
    other_got = core_swap(other_whole, sizes)
    qkv_sources = sources_of(qkv_whole, qkv_got, 3, sizes, me)
    every = wide((fsdp_size, rows, width), BF)
    lat_mixed, lat_every, lat_q, lat_k, lat_v = kernel_call(
        partial(attention_kernel, pack, len(qkv_sources), len(shards), lat_rows),
        "attention",
        [lat_low] + shards,
        qkv_sources,
        [wide((rows, width), BF)]
        + [wide((fsdp_size * rows, width), BF), wide((rows, width), BF), every, every],
        [pack.scratch()] * 3 + [dma((3,))],
        40,
        40,
        held=False,
    )
    other_sources = sources_of(other_whole, other_got, 3, sizes, me)
    d_mixed, lat_sums, result, grad_mid, *grads_m = kernel_call(
        partial(latent_kernel, pack, len(other_sources)),
        "latent",
        [lat_mixed, first_out, cotangent.reshape(rows, width), small_all],
        other_sources,
        [wide((rows, width), BF), wide((8, width), F32)]
        + [wide((rows, width), BF), wide((rows, width), F32)] + pack.grads(3),
        [pack.scratch()] * 3 + [pltpu.VMEM((rows, width), BF)] * 2 + [dma((3,))],
        44,
        36,
        held=False,
    )

    grads_m = core_terms(grads_m, sizes, me)
    slots, slot, *grads_q = kernel_call(
        partial(attention_back_kernel, pack, len(qkv_sources), lat_rows),
        "attention_back",
        [lat_q, lat_k, lat_v, d_mixed, lat_every],
        qkv_sources,
        [wide((fsdp_size - 1, rows, width), BF)]
        + [wide((rows, width), F32)] + pack.grads(3),
        [pack.scratch()] * 3
        + [pltpu.VMEM((rows, width), BF)]
        + [pltpu.VMEM(every.shape, BF)] * 2
        + [dma((3,))],
        48,
        72,
        held=False,
    )
    slots, grads_q = seal(slots, grads_q)

    slots = [slots[j] for j in range(fsdp_size - 1)]
    if in_two:
        received = collect_one(slots, my_fsdp)
    else:
        received = [slot_shift(slots[j - 1], fsdp_size, fsdp_size - j) for j in range(1, fsdp_size)]
    grads_m = far_pair(grads_m, 0, sizes, me)
    slots, received, grads_m = seal(slots, received, grads_m)
    if in_two:
        received = collect_two(slots, received, my_fsdp)
    for place in steps:
        grads_m = far_pair(grads_m, place, sizes, me)
    grads_q = core_terms(grads_q, sizes, me)
    received, grads_m, grads_q = seal(received, grads_m, grads_q)
    received = list(received)
    grad_enc, enc_sums, *grads_e = kernel_call(
        partial(encoder_back_kernel, pack, len(enc_sources), len(received)),
        "encoder_back",
        [slot, grad_mid, first_out, enc_resid, enc_pre, enc_act, small_all] + received,
        enc_sources,
        [wide((rows, width), F32), wide((8, width), F32)] + pack.grads(2),
        [pack.scratch()] * 2 + [pltpu.VMEM((rows, width), BF), dma((2,))],
        40,
        36,
        held=False,
    )
    grad_enc, grads_m, grads_q = seal(grad_enc, grads_m, grads_q)
    l_other_own, l_other_got = fsdp_part(grads_m, my_fsdp, sizes), fsdp_swap(grads_m, sizes, my_fsdp)
    grads_q = far_pair(grads_q, 0, sizes, me)
    share = pix_rows // fsdp_size
    kept = pix_hat_t.shape[0]
    pieces, d_pix_sums, d_latents, *grads_f = kernel_call(
        partial(cross_back_kernel, pack, len(enc_sources), padded, share),
        "cross_back",
        [grad_enc, latents.reshape(rows, width), enc_mixed, mixed_pix, probs, pix_low, query_pix, enc_q, small_all]
        + [lat_sums, enc_sums, pix_hat_t],
        enc_sources,
        [wide((fsdp_size, kept, share), BF), wide((kept, LANES), F32)]
        + [wide((rows, width), F32)] + pack.grads(3),
        [pack.scratch()] * 3
        + [pltpu.VMEM((rows, width), BF)] * 2
        + [pltpu.VMEM((16, width), BF)] * 2
        + [dma((3,))],
        48,
        50,
        held=False,
    )
    pieces, grads_e, grads_f, d_pix_sums, grads_q, l_other_got = seal(
        pieces, grads_e, grads_f, d_pix_sums, grads_q, l_other_got
    )

    low_bits, core, _ = bits_of(sizes)
    grads_e, grads_f = core_terms(grads_e, sizes, me), core_terms(grads_f, sizes, me)
    for place in steps:
        grads_q = far_pair(grads_q, place, sizes, me)
    d_pix_sums = total_over(d_pix_sums[:features, :2].T, low_bits[::-1][:1], sizes)
    pieces, grads_e, grads_f, grads_q, d_pix_sums = seal(pieces, grads_e, grads_f, grads_q, d_pix_sums)

    grads_e = [[jnp.concatenate(both, axis=1) for both in zip(e, f)] for e, f in zip(grads_e, grads_f)]
    d_pix_own = pieces[0].astype(F32)
    for j in range(1, fsdp_size):
        d_pix_own = d_pix_own + slot_shift(pieces[j], fsdp_size, fsdp_size - j).astype(F32)
    grads_e = far_pair(grads_e, 0, sizes, me)
    d_pix_own, grads_e, grads_q, d_pix_sums = seal(d_pix_own, grads_e, grads_q, d_pix_sums)

    l_qkv_own, l_qkv_got = fsdp_part(grads_q, my_fsdp, sizes), fsdp_swap(grads_q, sizes, my_fsdp)
    for place in steps:
        grads_e = far_pair(grads_e, place, sizes, me)
    l_qkv_got, l_other_got, grads_e, d_pix_sums = seal(l_qkv_got, l_other_got, grads_e, d_pix_sums)
    d_pix_sums = total_over(d_pix_sums, low_bits[::-1][1:] + [core] + far, sizes)
    enc_got = fsdp_swap(grads_e, sizes, my_fsdp)
    l_other_grads = fsdp_sum(l_other_own, l_other_got)
    l_qkv_grads = fsdp_sum(l_qkv_own, l_qkv_got)
    enc_grads = fsdp_sum(fsdp_part(grads_e, my_fsdp, sizes), enc_got)
    hat_own = lax.dynamic_slice_in_dim(pix_hat, my_fsdp * share, share, 0)
    inverse_own = lax.dynamic_slice_in_dim(pix_inverse, my_fsdp * share, share, 0)
    d_pixels = norm_back(hat_own, inverse_own, gain_f, d_pix_own[:features].T)
    kv_own = enc_grads[2]
    d_pix_kv = jnp.stack([kv_own[:, :features].T, kv_own[:, width // 2 : width // 2 + features].T])
    start = width // 2 + padded
    n_small = 2 * (n_gain + n_bias)
    small_own = (kv_own[:, padded : padded + n_small] + kv_own[:, start : start + n_small]).T
    return (
        result.reshape(latents.shape),
        d_latents.reshape(latents.shape),
        d_pixels,
        d_pix_sums[0],
        d_pix_sums[1],
        d_pix_kv,
        enc_grads[3],
        enc_grads[4],
        enc_grads[:2],
        small_own[:n_gain],
        small_own[n_gain : n_gain + n_bias],
        l_qkv_grads,
        l_other_grads[2],
        l_other_grads[:2],
        small_own[n_gain + n_bias : 2 * n_gain + n_bias],
        small_own[2 * n_gain + n_bias :],
    )


def solution(mesh):
    split, rows, columns = P("dp", "fsdp", None), P(AXES, None), P(None, AXES)
    middle = P(None, AXES, None)
    weights = (P(None, None, AXES), rows, rows, middle, columns, columns, middle, rows, middle, columns, columns)
    return jax.shard_map(
        partial(body, (mesh.shape["dp"], mesh.shape["fsdp"])),
        mesh=mesh,
        in_specs=(split, P("dp", None), P("dp", None), P(), P()) + weights + (split,),
        out_specs=(split, split, rows, P(), P()) + weights,
        check_vma=False,
    )
```
